256 devices in a mesh: edge: 64 (over y, z, core), pix: 4 (over x).
Axes of the slice: x: 4, y: 4, z: 8, core: 2. Of those that a mesh axis runs over, the one named last changes fastest.
Arguments:
- features: bfloat16 [128, 48, 64, 128], P('edge', 'pix'), may hold values from -6 to 6
- poses: float32 [128, 6], replicated, may hold values from -1.5 to 1.5
- inv_depth: float32 [128, 3072], P('edge', 'pix'), may hold values from 0.25 to 2
- hidden: bfloat16 [256, 48, 64, 128], P('edge', 'pix'), may hold values from -1 to 1
- edges: int32 [256, 2], P('edge'), may hold values from 0 to 127, as said below
- counts: int32 [64], P('edge'), may hold values from 1 to 4, 128 in all
- w_gates: bfloat16 [9, 256, 256], replicated, may hold values from -0.125 to 0.125
- w_cand: bfloat16 [9, 256, 128], replicated, may hold values from -0.125 to 0.125
- w_head: bfloat16 [4, 128], replicated, may hold values from -0.5 to 0.5
Outputs:
- hidden_out: bfloat16 [256, 48, 64, 128], P('edge', 'pix')
- pose_update: float32 [128, 6], P('edge')
- depth_update: float32 [128, 3072], P('edge', 'pix')
The draws below stay inside these ranges and needn't reach their ends.
Inputs may be any that keep to these rules, and one draw needn't show every extreme that they name: `edges`: slot s lies on node n = s // 4; its source frame is 2n or 2n + 1 and its target is one of the frames 2n to 2n + 3 other than the source; on the last node the target is the other frame of its own pair. The first slot of node n goes from frame 2n to frame 2n + 2 (on the last node to 2n + 1). Dead slots hold such pairs too.
All inputs are finite; a program needn't handle non-finite values. No bound on the sum of `counts` on one device may be relied on, other than what follows from the above.
Results may differ from the reference program's by a relative error of at most 0.011.
Values may be sent and summed in bfloat16 or wider, within the bound.
No kernel may reach another device: no remote copies, remote signals or barrier semaphores. Data moves between devices by JAX's collectives and lax.ppermute only.
A program may use at most 192 MiB of HBM per device.

```python
import math
import jax
import jax.numpy as jnp
import numpy as np
from jax import lax

CH = 128
HID = 128
HT = 48
WD = 64
SLOTS = 4
FRAMES = 128
EDGES = 128
SLOT_ALL = 256
PIX = 3072
N_EDGE = 64


def draw_features(key, part):
    full_shape = (FRAMES, HT, WD, CH)
    return jnp.clip(jax.random.normal(jax.random.fold_in(key, 1), full_shape, jnp.float32), -6.0, 6.0).astype(jnp.bfloat16)


def draw_edges(key, part):
    slot_ids = jnp.arange(FRAMES // 2 * SLOTS, dtype=jnp.int32)
    owner_node = slot_ids // SLOTS
    first_slot = slot_ids - owner_node * SLOTS == 0
    src_local = jax.random.randint(jax.random.fold_in(key, 1), slot_ids.shape, 0, 2)
    src_local = jnp.where(first_slot, 0, src_local)
    target_draw = jax.random.randint(jax.random.fold_in(key, 2), slot_ids.shape, 0, 3)
    tgt_local = target_draw + (target_draw >= src_local).astype(jnp.int32)
    tgt_local = jnp.where(first_slot, 2, tgt_local)
    last_node = owner_node == FRAMES // 2 - 1
    tgt_local = jnp.where(last_node, 1 - src_local, tgt_local)
    return jnp.stack([2 * owner_node + src_local, 2 * owner_node + tgt_local], axis=1).astype(jnp.int32)


def block_levels(key, extent, shards, low, high):
    gain, own = 1.0, jax.random.fold_in(key, 6)
    for dim, parts in shards:
        heights = jnp.exp(jax.random.uniform(jax.random.fold_in(own, dim), (parts,), jnp.float32, low / len(shards), high / len(shards)))
        gain = gain * jnp.repeat(heights, extent[dim] // parts).reshape([-1 if axis == dim else 1 for axis in range(len(extent))])
    return gain


def profile(amount, total, bound, lean):
    weights = [(1 << 20) // math.isqrt(standing ** lean) + 1 for standing in range(2, amount + 1)]
    rest, given = total - bound - (amount - 1), [1] * (amount - 1)
    while rest > 0:
        candidates = [i for i in range(amount - 1) if given[i] < bound]
        mass, remaining = sum([weights[i] for i in candidates]), rest
        for i in candidates:
            addition = min(bound - given[i], max(1, remaining * weights[i] // mass), rest)
            given[i] = given[i] + addition
            rest = rest - addition
    return np.array([bound] + given)


def uneven_parts(key, count, total, most, skew):
    if count == 2:
        one = jax.random.randint(key, (), max(1, total - most), min(most, total - 1) + 1)
        return jnp.stack([one, total - one])
    sizes = jnp.asarray(profile(count, total, most, skew), jnp.int32)
    couples = (count - 1) // 2
    donor, sink = sizes[1:1 + 2 * couples:2], sizes[2:2 + 2 * couples:2]
    slack = jnp.minimum(donor - 1, most - sink)
    moved = jax.random.randint(jax.random.fold_in(key, 1), (couples,), 0, 1 << 20) % (slack + 1)
    sizes = sizes.at[1:1 + 2 * couples:2].set(donor - moved).at[2:2 + 2 * couples:2].set(sink + moved)
    return sizes[jax.random.permutation(jax.random.fold_in(key, 2), count)]


def noise(rng, dims, spread, reach, kind=jnp.bfloat16):
    return jnp.clip(spread * jax.random.normal(rng, dims, jnp.float32), -reach, reach).astype(kind)


def setup_inputs(seed: int = 0) -> dict:
    splits = jax.random.split(jax.random.key(seed), 10)
    return {
        "features": draw_features(jax.random.fold_in(splits[9], 71), 0),
        "poses": noise(splits[1], (FRAMES, 6), 0.3, 1.5, jnp.float32),
        "inv_depth": jnp.clip(jnp.exp(math.log(2.0) - 2.0794415 * jax.random.uniform(splits[2], (FRAMES, PIX), jnp.float32) ** block_levels(splits[2], (FRAMES, PIX), ((0, 64), (1, 4)), -0.2, 0.2)), 0.25, 2.0),
        "hidden": jnp.clip(jax.random.uniform(splits[3], (SLOT_ALL, HT, WD, HID), jnp.float32, -1.0, 1.0) * block_levels(splits[3], (SLOT_ALL, HT, WD, HID), ((0, 64), (1, 4)), -0.4, 0.0), -1.0, 1.0).astype(jnp.bfloat16),
        "edges": draw_edges(jax.random.fold_in(splits[9], 71), 0),
        "counts": uneven_parts(splits[5], N_EDGE, EDGES, SLOTS, 2).astype(jnp.int32),
        "w_gates": noise(splits[6], (9, HID + CH, 2 * HID), (9 * (HID + CH)) ** -0.5, 0.125),
        "w_cand": noise(splits[7], (9, HID + CH, HID), (9 * (HID + CH)) ** -0.5, 0.125),
        "w_head": noise(splits[8], (4, HID), HID ** -0.5, 0.5),
    }


PRECISE = lax.Precision.HIGHEST
POSE_DAMPING = 0.1
DEPTH_DAMPING = 0.1

def pixel_coords(row_start, row_count, total_rows, col_count):
    row_ids = (row_start + lax.broadcasted_iota(jnp.int32, (row_count, col_count), 0)).astype(jnp.float32)
    col_ids = lax.broadcasted_iota(jnp.int32, (row_count, col_count), 1).astype(jnp.float32)
    half_width = col_count / 2.0
    horizontal = (col_ids - (col_count - 1) / 2.0) / half_width
    vertical = (row_ids - (total_rows - 1) / 2.0) / half_width
    return (horizontal.reshape(-1), vertical.reshape(-1))

def match_rows(queries, targets, factor):
    scores = jnp.dot(queries.astype(jnp.float32), targets.T.astype(jnp.float32), preferred_element_type=jnp.float32) * factor
    row_max = lax.optimization_barrier(jnp.max(scores, axis=1, keepdims=True))
    weights = jnp.exp(scores - row_max)
    row_total = lax.optimization_barrier(jnp.sum(weights, axis=1, keepdims=True))
    weighted_sum = jnp.dot(weights.astype(jnp.bfloat16).astype(jnp.float32), targets.astype(jnp.float32), preferred_element_type=jnp.float32)
    return (weighted_sum / row_total).astype(jnp.bfloat16)

def conv_taps(framed, weight, row_count, col_count):
    padded = jnp.pad(framed, ((0, 0), (1, 1), (0, 0)))
    result = jnp.zeros((row_count, col_count, weight.shape[2]), jnp.float32)
    for tap_index in range(9):
        row_off = tap_index // 3
        col_off = tap_index % 3
        window = padded[row_off:row_off + row_count, col_off:col_off + col_count, :]
        result = result + jnp.einsum('rwc,cd->rwd', window.astype(jnp.float32), weight[tap_index].astype(jnp.float32))
    return result

def gru_reference(state_in, matched, w_gates, w_cand):
    hid_width = state_in.shape[-1]
    row_count, col_count = (state_in.shape[0], state_in.shape[1])
    joined = jnp.concatenate([state_in, matched], axis=-1)
    framed = jnp.pad(joined, ((1, 1), (0, 0), (0, 0)))
    gates = jax.nn.sigmoid(conv_taps(framed, w_gates, row_count, col_count))
    update = gates[..., :hid_width]
    reset_gate = gates[..., hid_width:]
    reset_state = (reset_gate * state_in.astype(jnp.float32)).astype(jnp.bfloat16)
    second = jnp.pad(jnp.concatenate([reset_state, matched], axis=-1), ((1, 1), (0, 0), (0, 0)))
    candidate = jnp.tanh(conv_taps(second, w_cand, row_count, col_count))
    return ((1.0 - update) * state_in.astype(jnp.float32) + update * candidate).astype(jnp.bfloat16)

def bundle_terms(head_out, live_mask, inv_rho, xi_rel, src_local, tgt_local, horizontal, vertical):
    flow_pred = head_out[:, 0:2]
    confidence = jax.nn.sigmoid(head_out[:, 2:4]) * live_mask[:, None, None]
    unit_row = jnp.ones_like(inv_rho)
    zero_row = jnp.zeros_like(inv_rho)
    horiz_row = horizontal[None, :] * unit_row
    vert_row = vertical[None, :] * unit_row
    jacobian_horiz = jnp.stack([inv_rho, zero_row, -horiz_row * inv_rho, -horiz_row * vert_row, 1.0 + horiz_row * horiz_row, -vert_row], axis=1)
    jacobian_vert = jnp.stack([zero_row, inv_rho, -vert_row * inv_rho, -(1.0 + vert_row * vert_row), horiz_row * vert_row, horiz_row], axis=1)
    jacobian = jnp.stack([jacobian_horiz, jacobian_vert], axis=1)
    predicted = jnp.einsum('skjp,sj->skp', jacobian, xi_rel, precision=PRECISE)
    residual = flow_pred - predicted
    forward_shift = xi_rel[:, 2:3]
    depth_jacobian = jnp.stack([xi_rel[:, 0:1] - horiz_row * forward_shift, xi_rel[:, 1:2] - vert_row * forward_shift], axis=1)
    frame_ids = jnp.arange(4, dtype=jnp.int32)
    select = (tgt_local[:, None] == frame_ids[None, :]).astype(jnp.float32) - (src_local[:, None] == frame_ids[None, :]).astype(jnp.float32)
    slot_count, pix_count = inv_rho.shape
    pose_jacobian = (select[:, None, :, None, None] * jacobian[:, :, None, :, :]).reshape(slot_count, 2, 24, pix_count)
    weighted = pose_jacobian * confidence[:, :, None, :]
    pose_pose = jnp.einsum('skip,skjp->ij', weighted, pose_jacobian, precision=PRECISE)
    pose_rhs = jnp.einsum('skip,skp->i', weighted, residual, precision=PRECISE)
    pose_depth_slot = jnp.einsum('skip,skp->sip', weighted, depth_jacobian, precision=PRECISE)
    depth_depth_slot = lax.optimization_barrier(jnp.sum(confidence * depth_jacobian * depth_jacobian, axis=1))
    depth_rhs_slot = lax.optimization_barrier(jnp.sum(confidence * depth_jacobian * residual, axis=1))
    source_pick = (src_local[:, None] == frame_ids[None, 0:2]).astype(jnp.float32)
    pose_depth = jnp.einsum('sf,sip->fip', source_pick, pose_depth_slot, precision=PRECISE)
    depth_depth = DEPTH_DAMPING + jnp.einsum('sf,sp->fp', source_pick, depth_depth_slot, precision=PRECISE)
    depth_rhs = jnp.einsum('sf,sp->fp', source_pick, depth_rhs_slot, precision=PRECISE)
    depth_ratio = pose_depth / depth_depth[:, None, :]
    reduced = pose_pose - jnp.einsum('fip,fjp->ij', depth_ratio, pose_depth, precision=PRECISE)
    reduced_rhs = pose_rhs - jnp.einsum('fip,fp->i', depth_ratio, depth_rhs, precision=PRECISE)
    return (reduced, reduced_rhs, pose_depth, depth_depth, depth_rhs)

def reference(features, poses, inv_depth, hidden, edges, counts, w_gates, w_cand, w_head):
    pixels = HT * WD
    factor = 2.0 / math.sqrt(CH)
    horizontal, vertical = pixel_coords(0, HT, HT, WD)
    slot_ids = jnp.arange(SLOTS * N_EDGE, dtype=jnp.int32)
    node_of = slot_ids // SLOTS
    live_mask = (slot_ids - node_of * SLOTS < counts[node_of]).astype(jnp.float32)
    flat_feats = features.reshape(FRAMES, pixels, CH)

    def one_slot(slot_args):
        state_in, src_frame, tgt_frame, alive_flag = slot_args

        def compute(unused):
            queries = lax.dynamic_index_in_dim(flat_feats, src_frame, 0, keepdims=False)
            targets = lax.dynamic_index_in_dim(flat_feats, tgt_frame, 0, keepdims=False)
            matched = match_rows(queries, targets, factor).reshape(HT, WD, CH)
            fresh = gru_reference(state_in, matched, w_gates, w_cand)
            head_out = jnp.dot(w_head.astype(jnp.float32), fresh.reshape(pixels, HID).T.astype(jnp.float32), preferred_element_type=jnp.float32)
            return (fresh, head_out)

        def keep_old(unused):
            return (state_in, jnp.zeros((4, pixels), jnp.float32))
        return lax.cond(alive_flag > 0.5, compute, keep_old, 0)
    hidden_out, head_rows = lax.map(one_slot, (hidden, edges[:, 0], edges[:, 1], live_mask))
    src_local = edges[:, 0] - 2 * node_of
    tgt_local = edges[:, 1] - 2 * node_of
    inv_rho = inv_depth[edges[:, 0]]
    xi_rel = poses[edges[:, 1]] - poses[edges[:, 0]]

    def node_terms(node_args):
        head_out, alive_row, rho_rows, xi_rows, src_row, tgt_row = node_args
        return bundle_terms(head_out, alive_row, rho_rows, xi_rows, src_row, tgt_row, horizontal, vertical)
    reduced, reduced_rhs, pose_depth, depth_depth, depth_rhs = lax.map(node_terms, (head_rows.reshape(N_EDGE, SLOTS, 4, pixels), live_mask.reshape(N_EDGE, SLOTS), inv_rho.reshape(N_EDGE, SLOTS, pixels), xi_rel.reshape(N_EDGE, SLOTS, 6), src_local.reshape(N_EDGE, SLOTS), tgt_local.reshape(N_EDGE, SLOTS)))
    system_size = 12 * N_EDGE
    system = jnp.zeros((system_size + 12, system_size + 12), jnp.float32)
    system_rhs = jnp.zeros((system_size + 12,), jnp.float32)
    for node_index in range(N_EDGE):
        low = 12 * node_index
        system = system.at[low:low + 24, low:low + 24].add(reduced[node_index])
        system_rhs = system_rhs.at[low:low + 24].add(reduced_rhs[node_index])
    system = system[:system_size, :system_size] + POSE_DAMPING * jnp.eye(system_size, dtype=jnp.float32)
    solution = jnp.linalg.solve(system, system_rhs[:system_size])
    padded = jnp.concatenate([solution, jnp.zeros((12,), jnp.float32)])
    pose_pairs = jnp.concatenate([padded[:system_size].reshape(N_EDGE, 12), padded[12:].reshape(N_EDGE, 12)], axis=1)
    depth_new = (depth_rhs - jnp.einsum('nfip,ni->nfp', pose_depth, pose_pairs, precision=PRECISE)) / depth_depth
    pose_update = solution.reshape(FRAMES, 6)
    depth_update = depth_new.reshape(FRAMES, pixels)
    return (hidden_out, pose_update, depth_update)
```

```python
import functools
import math

import jax
import jax.numpy as jnp
from jax import lax
from jax.experimental import pallas as pl
from jax.experimental.pallas import tpu as pltpu
from jax.sharding import Mesh
from jax.sharding import PartitionSpec as P

PRECISE = lax.Precision.HIGHEST
POSE_DAMPING = 0.1
DEPTH_DAMPING = 0.1

EDGE = ("y", "z", "core")


def swapped(value, axis, step):
    count = lax.axis_size(axis)
    return lax.ppermute(value, axis, [(i, i ^ step) for i in range(count)])


def gathered_blocks(block):
    pair = block + swapped(block, "x", 1)
    block = pair + (swapped(block, "x", 2) + swapped(block, "x", 3))
    parts = lax.all_gather(block, "core", axis=0)
    parts = jnp.stack([parts] + [swapped(parts, "z", s) for s in (1, 2, 3)])
    parts = jnp.stack([parts, swapped(parts, "z", 4)])
    parts = jnp.stack([parts] + [swapped(parts, "y", s) for s in (1, 2, 3)])
    return parts.reshape((-1,) + block.shape)


def rows_of(x):
    return lax.broadcasted_iota(jnp.int32, x, 0)


def bundle_body(slots, rows_all, cols, info, poses, rho_ref, head, out, h_ref, dd_ref, a_ref, w_ref):
    pix = rho_ref.shape[1]
    rows = pix // cols
    shift = cols.bit_length() - 1
    base = 2 * info[2 * slots + 1]
    live = info[2 * slots]
    lane = lax.broadcasted_iota(jnp.int32, (1, pix), 1)
    col = (lane & (cols - 1)).astype(jnp.float32)
    row = ((lane >> shift) + info[2 * slots + 2] * rows).astype(jnp.float32)
    half = cols / 2.0
    u = (col - (cols - 1) / 2.0) / half
    v = (row - (rows_all - 1) / 2.0) / half
    sub = lax.broadcasted_iota(jnp.int32, (8, pix), 0)
    zero = jnp.zeros((8, pix), jnp.float32)
    lead_h = jnp.where(sub == 0, 1.0, jnp.where(sub == 2, -u, zero))
    rest_h = jnp.where(sub == 3, -u * v, jnp.where(sub == 4, 1.0 + u * u, jnp.where(sub == 5, -v, zero)))
    lead_v = jnp.where(sub == 1, 1.0, jnp.where(sub == 2, -v, zero))
    rest_v = jnp.where(sub == 3, -(1.0 + v * v), jnp.where(sub == 4, u * v, jnp.where(sub == 5, u, zero)))
    sub1 = lax.broadcasted_iota(jnp.int32, (8, 1), 0)
    eye = lax.broadcasted_iota(jnp.int32, (8, 6), 0) == lax.broadcasted_iota(jnp.int32, (8, 6), 1)
    picks, sels = [], []
    for s in range(slots):
        src, tgt = info[2 * s], info[2 * s + 1]
        a_loc, b_loc = src - base, tgt - base
        alive = jnp.where(s < live, 1.0, 0.0)
        picks.append([jnp.where(a_loc == f, 1.0, 0.0) for f in range(2)])
        sels.append([jnp.where(b_loc == g, 1.0, 0.0) - jnp.where(a_loc == g, 1.0, 0.0) for g in range(4)])
        d_row = poses[pl.ds(tgt, 1), :] - poses[pl.ds(src, 1), :]
        d = jnp.sum(jnp.where(eye, jnp.broadcast_to(d_row, (8, 6)), 0.0), axis=1, keepdims=True)
        rho = rho_ref[pl.ds(a_loc, 1), :]
        conf_h = jax.nn.sigmoid(head[4 * s + 2 : 4 * s + 3, :]) * alive
        conf_v = jax.nn.sigmoid(head[4 * s + 3 : 4 * s + 4, :]) * alive
        a_h = rho * lead_h + rest_h
        a_v = rho * lead_v + rest_v
        e_h = head[4 * s : 4 * s + 1, :] - jnp.sum(a_h * d, axis=0, keepdims=True)
        e_v = head[4 * s + 1 : 4 * s + 2, :] - jnp.sum(a_v * d, axis=0, keepdims=True)
        k_h = jnp.sum(lead_h * d, axis=0, keepdims=True)
        k_v = jnp.sum(lead_v * d, axis=0, keepdims=True)
        a_h = jnp.where(sub == 6, e_h, a_h)
        a_v = jnp.where(sub == 6, e_v, a_v)
        w_h = conf_h * a_h
        w_v = conf_v * a_v
        at = slice(8 * s, 8 * s + 8)
        a_ref[at, :pix] = a_h
        a_ref[at, pix:] = a_v
        w_ref[at, :pix] = w_h
        w_ref[at, pix:] = w_v
        k_s = w_h * k_h + w_v * k_v
        dd = conf_h * k_h * k_h + conf_v * k_v * k_v
        for f in range(2):
            pick = picks[s][f]
            old = dd_ref[f : f + 1, :] if s else jnp.full((1, pix), DEPTH_DAMPING, jnp.float32)
            dd_ref[f : f + 1, :] = old + pick * dd
            for g in range(4):
                term = jnp.where(sub1 == 6, pick, pick * sels[s][g]) * k_s
                at = (slice(8 * g, 8 * g + 8), slice(f * pix, (f + 1) * pix))
                h_ref[at] = h_ref[at] + term if s else term
    nt = (((1,), (1,)), ((), ()))
    gram = lax.dot_general(w_ref[...], a_ref[...], nt, precision=PRECISE, preferred_element_type=jnp.float32)
    for f in range(2):
        at = slice(f * pix, (f + 1) * pix)
        w_ref[:, at] = h_ref[:, at] * (1.0 / dd_ref[f : f + 1, :])
    schur = lax.dot_general(w_ref[...], h_ref[...], nt, precision=PRECISE, preferred_element_type=jnp.float32)
    pad = jnp.zeros((32, 96), jnp.float32)
    gram = jnp.concatenate([gram, pad], axis=1)
    schur = jnp.concatenate([schur, pad], axis=1)
    lanes = lax.broadcasted_iota(jnp.int32, (8, 128), 1)
    group, inner = lanes >> 3, lanes & 7
    terms = []
    for s in range(slots):
        y = jnp.where(group == s, gram[8 * s : 8 * s + 8, :], 0.0)
        y = pltpu.roll(y, 128 - 8 * s, 1) if s else y
        y = y + pltpu.roll(y, 8, 1)
        y = y + pltpu.roll(y, 16, 1)
        coef = jnp.zeros((8, 128), jnp.float32)
        for g in range(4):
            coef = jnp.where(group == g, sels[s][g], coef)
        terms.append(y * jnp.where(inner == 6, 1.0, coef))
    total = None
    for g in range(4):
        part = -schur[8 * g : 8 * g + 8, :]
        for s in range(slots):
            part = part + sels[s][g] * terms[s]
        part = jnp.where(lanes < 32, part, 0.0)
        total = part if g == 0 else total + pltpu.roll(part, 32 * g, 1)
    out[...] = total


def bundle_call(info, poses, inv_depth, head, rows_all, cols):
    slots = head.shape[0] // 4
    pix = inv_depth.shape[1]
    vmem = pl.BlockSpec(memory_space=pltpu.VMEM)
    return pl.pallas_call(
        functools.partial(bundle_body, slots, rows_all, cols),
        out_shape=(
            jax.ShapeDtypeStruct((8, 128), jnp.float32),
            jax.ShapeDtypeStruct((32, 2 * pix), jnp.float32),
            jax.ShapeDtypeStruct((2, pix), jnp.float32),
        ),
        in_specs=[pl.BlockSpec(memory_space=pltpu.SMEM), vmem, vmem, vmem],
        out_specs=(vmem, vmem, vmem),
        scratch_shapes=[
            pltpu.VMEM((8 * slots, 2 * pix), jnp.float32),
            pltpu.VMEM((8 * slots, 2 * pix), jnp.float32),
        ],
        name="bundle",
    )(info, poses, inv_depth, head)


REAL = (0, 1, 2, 3, 4, 5, 8, 9, 10, 11, 12, 13)


def down(x, width=16):
    return jnp.broadcast_to(x, (width, 128))


def eliminate(diag, sides):
    diag, sides = list(diag), [list(side) for side in sides]
    count = len(REAL)
    for k in range(count):
        at = slice(REAL[k], REAL[k] + 1)
        scale = down(1.0 / diag[k][at, :])
        diag[k] = diag[k] * scale
        for side in sides:
            side[k] = side[k] * scale
        for i in range(count):
            if i != k:
                f = down(diag[i][at, :])
                diag[i] = diag[i] - f * diag[k]
                for side in sides:
                    side[i] = side[i] - f * side[k]
    return diag, sides


def solve_body(nodes, pix, info, g_ref, h_ref, dd_ref, pose_ref, depth_ref, t_ref, d_ref, l_ref, u_ref, near):
    count = len(REAL)
    lane = lax.broadcasted_iota(jnp.int32, (16, 128), 1)
    sub = lax.broadcasted_iota(jnp.int32, (16, 128), 0)
    me = info[0]
    flip = me - (me & 1)
    for n in range(nodes):
        t_ref[n] = g_ref[n ^ flip]
    rest = jnp.zeros((128 - nodes, 128), jnp.float32)
    for k in range(6):
        t = jnp.concatenate([t_ref[:, k, :], rest], axis=0).T
        for f in range(2):
            i = 6 * f + k
            far = jnp.where(lane < nodes, pltpu.roll(t[32 * f + 80 : 32 * f + 96], 1, 1), 0.0)
            d_ref[i] = t[32 * f : 32 * f + 16] + far + jnp.where(sub == REAL[i], POSE_DAMPING, 0.0)
            u_ref[i] = jnp.where(lane < nodes - 1, t[32 * f + 16 : 32 * f + 32], 0.0)
            l_ref[i] = jnp.where(lane < nodes, pltpu.roll(t[32 * f + 64 : 32 * f + 80], 1, 1), 0.0)

    def level(step, carry):
        s = jnp.left_shift(1, step)
        diag, (low, up) = eliminate(
            [d_ref[i] for i in range(count)], [[l_ref[i] for i in range(count)], [u_ref[i] for i in range(count)]]
        )
        for k in range(count):
            low_r = jnp.where(sub == 6, diag[k], low[k])
            up_r = jnp.where(sub == 6, diag[k], up[k])
            near[0, k] = pltpu.roll(up_r, s, 1)
            near[1, k] = pltpu.roll(low[k], s, 1)
            near[2, k] = pltpu.roll(low_r, 128 - s, 1)
            near[3, k] = pltpu.roll(up[k], 128 - s, 1)
        for i in range(count):
            d_new = d_ref[i]
            l_old, u_old = l_ref[i], u_ref[i]
            l_new = jnp.zeros((16, 128), jnp.float32)
            u_new = jnp.zeros((16, 128), jnp.float32)
            for k in range(count):
                at = slice(REAL[k], REAL[k] + 1)
                fl, fu = down(l_old[at, :]), down(u_old[at, :])
                d_new = d_new - fl * near[0, k] - fu * near[2, k]
                l_new = l_new - fl * near[1, k]
                u_new = u_new - fu * near[3, k]
            d_ref[i] = d_new
            l_ref[i] = l_new
            u_ref[i] = u_new
        return carry

    levels = max(1, (nodes - 1).bit_length())
    lax.fori_loop(0, levels, level, 0)
    diag, _ = eliminate([d_ref[i] for i in range(count)], [])
    x = jnp.zeros((16, 128), jnp.float32)
    for i in range(count):
        x = jnp.where(sub == REAL[i], down(diag[i][6:7, :]), x)
    own = jnp.sum(jnp.where(lane == me, x, 0.0), axis=1, keepdims=True)
    after = jnp.sum(jnp.where((lane == me + 1) & (lane < nodes), x, 0.0), axis=1, keepdims=True)
    spread = jnp.where((sub & 7) == lane, jnp.broadcast_to(own, (16, 128)), 0.0)
    for f in range(2):
        pose_ref[f : f + 1, :] = jnp.sum(spread[8 * f : 8 * f + 8], axis=0, keepdims=True)[:, :6]
    column = jnp.concatenate([own, after], axis=0)
    column = jnp.where(lax.broadcasted_iota(jnp.int32, (32, 1), 0) == 6, -1.0, column)
    for f in range(2):
        pull = jnp.sum(h_ref[:, f * pix : (f + 1) * pix] * column, axis=0, keepdims=True)
        depth_ref[f : f + 1, :] = -pull / dd_ref[f : f + 1, :]


def solve_call(me, gathered, h, dd):
    nodes = gathered.shape[0]
    pix = dd.shape[1]
    vmem = pl.BlockSpec(memory_space=pltpu.VMEM)
    return pl.pallas_call(
        functools.partial(solve_body, nodes, pix),
        out_shape=(
            jax.ShapeDtypeStruct((2, 6), jnp.float32),
            jax.ShapeDtypeStruct((2, pix), jnp.float32),
        ),
        in_specs=[pl.BlockSpec(memory_space=pltpu.SMEM), vmem, vmem, vmem],
        out_specs=(vmem, vmem),
        scratch_shapes=[
            pltpu.VMEM((nodes, 8, 128), jnp.float32),
            pltpu.VMEM((12, 16, 128), jnp.float32),
            pltpu.VMEM((12, 16, 128), jnp.float32),
            pltpu.VMEM((12, 16, 128), jnp.float32),
            pltpu.VMEM((4, 12, 16, 128), jnp.float32),
        ],
        name="pose_solve",
    )(me, gathered, h, dd)


def conv_taps(framed, weight, row_count, col_count):
    padded = jnp.pad(framed, ((0, 0), (0, 0), (1, 1), (0, 0)))
    result = None
    for tap_index in range(9):
        row_off = tap_index // 3
        col_off = tap_index % 3
        window = padded[:, row_off : row_off + row_count, col_off : col_off + col_count, :]
        tap_term = jnp.einsum(
            "srwc,cd->srwd", window, weight[tap_index], preferred_element_type=jnp.float32
        )
        result = tap_term if tap_index == 0 else result + tap_term
    return result


def match_rows(queries, targets, factor):
    scores = jnp.einsum("pc,qc->pq", queries, targets, preferred_element_type=jnp.float32) * factor
    row_max = jnp.max(scores, axis=1, keepdims=True)
    weights = jnp.exp(scores - row_max)
    row_total = jnp.sum(weights, axis=1, keepdims=True)
    weighted_sum = jnp.dot(
        weights.astype(jnp.bfloat16), targets, preferred_element_type=jnp.float32
    )
    return (weighted_sum / row_total).astype(jnp.bfloat16)


def padded_rows(cells, dim):
    count = lax.axis_size("x")
    head = lax.slice_in_dim(cells, 0, 1, axis=dim)
    tail = lax.slice_in_dim(cells, cells.shape[dim] - 1, cells.shape[dim], axis=dim)
    return jnp.concatenate(
        [
            lax.ppermute(tail, "x", [(i, i + 1) for i in range(count - 1)]),
            cells,
            lax.ppermute(head, "x", [(i + 1, i) for i in range(count - 1)]),
        ],
        axis=dim,
    )


def shards(features, poses, inv_depth, hidden, edges, counts, w_gates, w_cand, w_head):
    slot_count, row_count, col_count, hid_width = hidden.shape
    channels = features.shape[3]
    node_rank = lax.axis_index(EDGE)
    base_frame = 2 * node_rank
    pix_rank = lax.axis_index("x")
    total_rows = row_count * lax.axis_size("x")
    local_pixels = row_count * col_count
    nodes = lax.axis_size(EDGE)
    info = jnp.concatenate([edges.reshape(-1), counts, jnp.stack([node_rank, pix_rank])]).astype(jnp.int32)
    own_whole = lax.all_gather(features, "x", axis=1, tiled=True)
    next_whole = lax.ppermute(own_whole, EDGE, [(i + 1, i) for i in range(nodes - 1)])
    nearby = jnp.concatenate([own_whole, next_whole], axis=0)
    nearby = nearby.reshape(4, total_rows * col_count, channels)
    own_flat = features.reshape(2, local_pixels, channels)
    src_local = edges[:, 0] - base_frame
    tgt_local = edges[:, 1] - base_frame
    factor = 2.0 / math.sqrt(channels)
    matched_list = []
    for slot_index in range(slot_count):
        queries = lax.dynamic_index_in_dim(own_flat, src_local[slot_index], 0, keepdims=False)
        targets = lax.dynamic_index_in_dim(nearby, tgt_local[slot_index], 0, keepdims=False)
        matched_list.append(match_rows(queries, targets, factor))
    matched = jnp.stack(matched_list, axis=0).reshape(slot_count, row_count, col_count, channels)
    inputs = jnp.concatenate([hidden, matched], axis=3)
    state_wide = hidden.astype(jnp.float32)
    framed = padded_rows(inputs, 1)
    gates = jax.nn.sigmoid(conv_taps(framed, w_gates, row_count, col_count))
    update = gates[..., :hid_width]
    reset_state = (gates[..., hid_width:] * state_wide).astype(jnp.bfloat16)
    reset_framed = padded_rows(reset_state, 1)
    second = jnp.concatenate([reset_framed, framed[..., hid_width:]], axis=3)
    candidate = jnp.tanh(conv_taps(second, w_cand, row_count, col_count))
    fresh = ((1.0 - update) * state_wide + update * candidate).astype(jnp.bfloat16)
    live_mask = lax.broadcasted_iota(jnp.int32, (slot_count,), 0) < counts[0]
    hidden_out = jnp.where(live_mask[:, None, None, None], fresh, hidden)
    head_out = jnp.einsum(
        "kc,spc->skp",
        w_head,
        fresh.reshape(slot_count, local_pixels, hid_width),
        preferred_element_type=jnp.float32,
    )
    block, pull, scale = bundle_call(
        info, poses, inv_depth, head_out.reshape(4 * slot_count, local_pixels), total_rows, col_count
    )
    gathered = gathered_blocks(block)
    pose_update, depth_update = solve_call(info[2 * slot_count + 1 :], gathered, pull, scale)
    return (hidden_out, pose_update, depth_update)


def solution(mesh):
    nodes, pix = mesh.devices.shape
    fine = Mesh(mesh.devices.reshape(nodes // 16, 8, 2, pix), EDGE + ("x",))
    placed = (
        P(EDGE, "x", None, None),
        P(),
        P(EDGE, "x"),
        P(EDGE, "x", None, None),
        P(EDGE, None),
        P(EDGE),
        P(),
        P(),
        P(),
    )
    return jax.shard_map(
        shards,
        mesh=fine,
        in_specs=placed,
        out_specs=(P(EDGE, "x", None, None), P(EDGE, None), P(EDGE, "x")),
        check_vma=False,
    )
```

```python
import functools
import math

import jax
import jax.numpy as jnp
from jax import lax
from jax.experimental import pallas as pl
from jax.experimental.pallas import tpu as pltpu
from jax.sharding import Mesh
from jax.sharding import PartitionSpec as P

PRECISE = lax.Precision.HIGHEST
POSE_DAMPING = 0.1
DEPTH_DAMPING = 0.1

EDGE = ("y", "z", "core")


def swapped(value, axis, step):
    count = lax.axis_size(axis)
    return lax.ppermute(value, axis, [(i, i ^ step) for i in range(count)])


def gathered_blocks(block):
    pair = block + swapped(block, "x", 1)
    block = pair + (swapped(block, "x", 2) + swapped(block, "x", 3))
    parts = lax.all_gather(block, "core", axis=0)
    parts = jnp.stack([parts] + [swapped(parts, "z", s) for s in (1, 2, 3)])
    parts = jnp.stack([parts, swapped(parts, "z", 4)])
    parts = jnp.stack([parts] + [swapped(parts, "y", s) for s in (1, 2, 3)])
    return parts.reshape((-1,) + block.shape)


def bundle_body(slots, rows_all, cols, info, poses, rho_ref, head, out, h_ref, dd_ref, a_ref, w_ref):
    pix = rho_ref.shape[1]
    rows = pix // cols
    shift = cols.bit_length() - 1
    base = 2 * info[2 * slots + 1]
    live = info[2 * slots]
    lane = lax.broadcasted_iota(jnp.int32, (1, pix), 1)
    col = (lane & (cols - 1)).astype(jnp.float32)
    row = ((lane >> shift) + info[2 * slots + 2] * rows).astype(jnp.float32)
    half = cols / 2.0
    u = (col - (cols - 1) / 2.0) / half
    v = (row - (rows_all - 1) / 2.0) / half
    sub = lax.broadcasted_iota(jnp.int32, (8, pix), 0)
    zero = jnp.zeros((8, pix), jnp.float32)
    lead_h = jnp.where(sub == 0, 1.0, jnp.where(sub == 2, -u, zero))
    rest_h = jnp.where(sub == 3, -u * v, jnp.where(sub == 4, 1.0 + u * u, jnp.where(sub == 5, -v, zero)))
    lead_v = jnp.where(sub == 1, 1.0, jnp.where(sub == 2, -v, zero))
    rest_v = jnp.where(sub == 3, -(1.0 + v * v), jnp.where(sub == 4, u * v, jnp.where(sub == 5, u, zero)))
    sub1 = lax.broadcasted_iota(jnp.int32, (8, 1), 0)
    eye = lax.broadcasted_iota(jnp.int32, (8, 6), 0) == lax.broadcasted_iota(jnp.int32, (8, 6), 1)
    picks, sels = [], []
    for s in range(slots):
        src, tgt = info[2 * s], info[2 * s + 1]
        a_loc, b_loc = src - base, tgt - base
        alive = jnp.where(s < live, 1.0, 0.0)
        picks.append([jnp.where(a_loc == f, 1.0, 0.0) for f in range(2)])
        sels.append([jnp.where(b_loc == g, 1.0, 0.0) - jnp.where(a_loc == g, 1.0, 0.0) for g in range(4)])
        d_row = poses[pl.ds(tgt, 1), :] - poses[pl.ds(src, 1), :]
        d = jnp.sum(jnp.where(eye, jnp.broadcast_to(d_row, (8, 6)), 0.0), axis=1, keepdims=True)
        rho = rho_ref[pl.ds(a_loc, 1), :]
        conf_h = jax.nn.sigmoid(head[8 * s + 2 : 8 * s + 3, :]) * alive
        conf_v = jax.nn.sigmoid(head[8 * s + 3 : 8 * s + 4, :]) * alive
        a_h = rho * lead_h + rest_h
        a_v = rho * lead_v + rest_v
        e_h = head[8 * s : 8 * s + 1, :] - jnp.sum(a_h * d, axis=0, keepdims=True)
        e_v = head[8 * s + 1 : 8 * s + 2, :] - jnp.sum(a_v * d, axis=0, keepdims=True)
        k_h = jnp.sum(lead_h * d, axis=0, keepdims=True)
        k_v = jnp.sum(lead_v * d, axis=0, keepdims=True)
        a_h = jnp.where(sub == 6, e_h, a_h)
        a_v = jnp.where(sub == 6, e_v, a_v)
        w_h = conf_h * a_h
        w_v = conf_v * a_v
        at = slice(8 * s, 8 * s + 8)
        a_ref[at, :pix] = a_h
        a_ref[at, pix:] = a_v
        w_ref[at, :pix] = w_h
        w_ref[at, pix:] = w_v
        k_s = w_h * k_h + w_v * k_v
        dd = conf_h * k_h * k_h + conf_v * k_v * k_v
        for f in range(2):
            pick = picks[s][f]
            old = dd_ref[f : f + 1, :] if s else jnp.full((1, pix), DEPTH_DAMPING, jnp.float32)
            dd_ref[f : f + 1, :] = old + pick * dd
            for g in range(4):
                term = jnp.where(sub1 == 6, pick, pick * sels[s][g]) * k_s
                at = (slice(8 * g, 8 * g + 8), slice(f * pix, (f + 1) * pix))
                h_ref[at] = h_ref[at] + term if s else term
    nt = (((1,), (1,)), ((), ()))
    gram = lax.dot_general(w_ref[...], a_ref[...], nt, precision=PRECISE, preferred_element_type=jnp.float32)
    for f in range(2):
        at = slice(f * pix, (f + 1) * pix)
        w_ref[:, at] = h_ref[:, at] * (1.0 / dd_ref[f : f + 1, :])
    schur = lax.dot_general(w_ref[...], h_ref[...], nt, precision=PRECISE, preferred_element_type=jnp.float32)
    pad = jnp.zeros((32, 96), jnp.float32)
    gram = jnp.concatenate([gram, pad], axis=1)
    schur = jnp.concatenate([schur, pad], axis=1)
    lanes = lax.broadcasted_iota(jnp.int32, (8, 128), 1)
    group, inner = lanes >> 3, lanes & 7
    terms = []
    for s in range(slots):
        y = jnp.where(group == s, gram[8 * s : 8 * s + 8, :], 0.0)
        y = pltpu.roll(y, 128 - 8 * s, 1) if s else y
        y = y + pltpu.roll(y, 8, 1)
        y = y + pltpu.roll(y, 16, 1)
        coef = jnp.zeros((8, 128), jnp.float32)
        for g in range(4):
            coef = jnp.where(group == g, sels[s][g], coef)
        terms.append(y * jnp.where(inner == 6, 1.0, coef))
    total = None
    for g in range(4):
        part = -schur[8 * g : 8 * g + 8, :]
        for s in range(slots):
            part = part + sels[s][g] * terms[s]
        part = jnp.where(lanes < 32, part, 0.0)
        total = part if g == 0 else total + pltpu.roll(part, 32 * g, 1)
    out[...] = total


REAL = (0, 1, 2, 3, 4, 5, 8, 9, 10, 11, 12, 13)


def down(x, width=16):
    return jnp.broadcast_to(x, (width, 128))


def eliminate(diag, sides):
    diag, sides = list(diag), [list(side) for side in sides]
    count = len(REAL)
    for k in range(count):
        at = slice(REAL[k], REAL[k] + 1)
        scale = down(1.0 / diag[k][at, :])
        diag[k] = diag[k] * scale
        for side in sides:
            side[k] = side[k] * scale
        for i in range(count):
            if i != k:
                f = down(diag[i][at, :])
                diag[i] = diag[i] - f * diag[k]
                for side in sides:
                    side[i] = side[i] - f * side[k]
    return diag, sides


def solve_body(nodes, pix, info, g_ref, h_ref, dd_ref, pose_ref, depth_ref, t_ref, d_ref, l_ref, u_ref, near):
    count = len(REAL)
    lane = lax.broadcasted_iota(jnp.int32, (16, 128), 1)
    sub = lax.broadcasted_iota(jnp.int32, (16, 128), 0)
    me = info[0]
    flip = me - (me & 1)
    for n in range(nodes):
        t_ref[n] = g_ref[n ^ flip]
    rest = jnp.zeros((128 - nodes, 128), jnp.float32)
    for k in range(6):
        t = jnp.concatenate([t_ref[:, k, :], rest], axis=0).T
        for f in range(2):
            i = 6 * f + k
            far = jnp.where(lane < nodes, pltpu.roll(t[32 * f + 80 : 32 * f + 96], 1, 1), 0.0)
            d_ref[i] = t[32 * f : 32 * f + 16] + far + jnp.where(sub == REAL[i], POSE_DAMPING, 0.0)
            u_ref[i] = jnp.where(lane < nodes - 1, t[32 * f + 16 : 32 * f + 32], 0.0)
            l_ref[i] = jnp.where(lane < nodes, pltpu.roll(t[32 * f + 64 : 32 * f + 80], 1, 1), 0.0)

    def level(step, carry):
        s = jnp.left_shift(1, step)
        diag, (low, up) = eliminate(
            [d_ref[i] for i in range(count)], [[l_ref[i] for i in range(count)], [u_ref[i] for i in range(count)]]
        )
        for k in range(count):
            low_r = jnp.where(sub == 6, diag[k], low[k])
            up_r = jnp.where(sub == 6, diag[k], up[k])
            near[0, k] = pltpu.roll(up_r, s, 1)
            near[1, k] = pltpu.roll(low[k], s, 1)
            near[2, k] = pltpu.roll(low_r, 128 - s, 1)
            near[3, k] = pltpu.roll(up[k], 128 - s, 1)
        for i in range(count):
            d_new = d_ref[i]
            l_old, u_old = l_ref[i], u_ref[i]
            l_new = jnp.zeros((16, 128), jnp.float32)
            u_new = jnp.zeros((16, 128), jnp.float32)
            for k in range(count):
                at = slice(REAL[k], REAL[k] + 1)
                fl, fu = down(l_old[at, :]), down(u_old[at, :])
                d_new = d_new - fl * near[0, k] - fu * near[2, k]
                l_new = l_new - fl * near[1, k]
                u_new = u_new - fu * near[3, k]
            d_ref[i] = d_new
            l_ref[i] = l_new
            u_ref[i] = u_new
        return carry

    levels = max(1, (nodes - 1).bit_length())
    lax.fori_loop(0, levels, level, 0)
    diag, _ = eliminate([d_ref[i] for i in range(count)], [])
    x = jnp.zeros((16, 128), jnp.float32)
    for i in range(count):
        x = jnp.where(sub == REAL[i], down(diag[i][6:7, :]), x)
    own = jnp.sum(jnp.where(lane == me, x, 0.0), axis=1, keepdims=True)
    after = jnp.sum(jnp.where((lane == me + 1) & (lane < nodes), x, 0.0), axis=1, keepdims=True)
    spread = jnp.where((sub & 7) == lane, jnp.broadcast_to(own, (16, 128)), 0.0)
    for f in range(2):
        pose_ref[f : f + 1, :] = jnp.sum(spread[8 * f : 8 * f + 8], axis=0, keepdims=True)[:, :6]
    column = jnp.concatenate([own, after], axis=0)
    column = jnp.where(lax.broadcasted_iota(jnp.int32, (32, 1), 0) == 6, -1.0, column)
    for f in range(2):
        pull = jnp.sum(h_ref[:, f * pix : (f + 1) * pix] * column, axis=0, keepdims=True)
        depth_ref[f : f + 1, :] = -pull / dd_ref[f : f + 1, :]


def solve_call(me, gathered, h, dd):
    nodes = gathered.shape[0]
    pix = dd.shape[1]
    vmem = pl.BlockSpec(memory_space=pltpu.VMEM)
    return pl.pallas_call(
        functools.partial(solve_body, nodes, pix),
        out_shape=(
            jax.ShapeDtypeStruct((2, 6), jnp.float32),
            jax.ShapeDtypeStruct((2, pix), jnp.float32),
        ),
        in_specs=[pl.BlockSpec(memory_space=pltpu.SMEM), vmem, vmem, vmem],
        out_specs=(vmem, vmem),
        scratch_shapes=[
            pltpu.VMEM((nodes, 8, 128), jnp.float32),
            pltpu.VMEM((12, 16, 128), jnp.float32),
            pltpu.VMEM((12, 16, 128), jnp.float32),
            pltpu.VMEM((12, 16, 128), jnp.float32),
            pltpu.VMEM((4, 12, 16, 128), jnp.float32),
        ],
        name="pose_solve",
    )(me, gathered, h, dd)


NT = (((1,), (1,)), ((), ()))
TILE = 256
CHUNK = 768


def gate(value):
    return 0.5 * jnp.tanh(0.5 * value) + 0.5


def spots(info, slots, pix, halo):
    odd = (info[2 * slots + 2] & 1) == 1
    at1 = pl.multiple_of(jnp.where(odd, 0, halo + pix), halo)
    at3 = pl.multiple_of(jnp.where(odd, halo + pix, 0), halo)
    return at1, at3


def load_keys(near, owns, nexts, k_ref, vt_ref):
    channels = k_ref.shape[1]

    @pl.when(near)
    def _():
        base = 0
        for part in owns:
            k_ref[base : base + part.shape[1], :] = part[0]
            base += part.shape[1]

    @pl.when(jnp.logical_not(near))
    def _():
        base = 0
        for part in nexts:
            k_ref[base : base + part.shape[1], :] = part[0]
            base += part.shape[1]

    vt_ref[:channels, :] = k_ref[...].T
    vt_ref[channels:, :] = jnp.ones((vt_ref.shape[0] - channels, vt_ref.shape[1]), jnp.bfloat16)


def add_keys(k_ref, vt_ref, qt_ref, acc_ref, old, factor):
    keys, ext = k_ref.shape[0], qt_ref.shape[1]
    for t in range(ext // TILE):
        at = slice(t * TILE, (t + 1) * TILE)
        acc = None if old is None else old[0, :, at]
        for j in range(keys // CHUNK):
            span = slice(j * CHUNK, (j + 1) * CHUNK)
            s = jnp.dot(k_ref[span, :], qt_ref[:, at], preferred_element_type=jnp.float32)
            p = jnp.exp2(s * factor).astype(jnp.bfloat16)
            part = jnp.dot(vt_ref[:, span], p, preferred_element_type=jnp.float32)
            acc = part if acc is None else acc + part
        acc_ref[0, :, at] = acc


def load_queries(info, slots, own_q, side1, side3, q_ref, qt_ref):
    pix, halo = own_q.shape[1], side1.shape[1]
    at1, at3 = spots(info, slots, pix, halo)
    q_ref[halo : halo + pix, :] = own_q[0]
    q_ref[pl.ds(at1, halo), :] = side1[0]
    q_ref[pl.ds(at3, halo), :] = side3[0]
    qt_ref[...] = q_ref[...].T


def match_factor(channels):
    return 2.0 / math.sqrt(channels) * math.log2(math.e)


def match_body(dims, info, own_q, side1, side3, *refs):
    slots, parts, chained = dims
    owns, refs = refs[:parts], refs[parts:]
    nexts, refs = refs[:parts], refs[parts:]
    old = refs[0] if chained else None
    acc_ref, q_ref, qt_ref, k_ref, vt_ref = refs[chained:]
    slot = pl.program_id(0)

    @pl.when(slot < info[2 * slots])
    def _():
        near = info[2 * slot + 1] - 2 * info[2 * slots + 1] < 2
        load_queries(info, slots, own_q, side1, side3, q_ref, qt_ref)
        load_keys(near, owns, nexts, k_ref, vt_ref)
        add_keys(k_ref, vt_ref, qt_ref, acc_ref, old, match_factor(q_ref.shape[1]))


def fused_body(dims, info, *refs):
    slots, total_rows, rows, cols, last, parts = dims
    (own_q, side1, side3, old), refs = refs[:4], refs[4:]
    (state, hide1, hide3), refs = refs[:3], refs[3:]
    owns, refs = refs[:parts], refs[parts:]
    nexts, refs = refs[:parts], refs[parts:]
    (wg, wc01, wc2, wh, poses, rho_ref), refs = refs[:6], refs[6:]
    (fresh_ref, block_ref, pull_ref, scale_ref), refs = refs[:4], refs[4:]
    q_ref, qt_ref, k_ref, vt_ref, acc_ref, kall_ref, vtall_ref, x_ref, h_ref, head_ref, a_ref, w_ref = refs
    slot = pl.program_id(0)
    live = slot < info[2 * slots]
    pix_rank = info[2 * slots + 2]
    pix = rows * cols
    halo = 2 * cols
    ext = pix + 2 * halo
    channels = own_q.shape[-1]
    factor = match_factor(channels)
    at1, at3 = spots(info, slots, pix, halo)
    px = lax.broadcasted_iota(jnp.int32, (ext, 1), 0)

    def inside(px):
        grow = (px >> (cols.bit_length() - 1)) - 2 + rows * pix_rank
        return jnp.where((grow >= 0) & (grow < total_rows), 1.0, 0.0)

    valid = inside(px)

    @pl.when(jnp.logical_not(live))
    def _():
        fresh_ref[...] = state[...]
        head_ref[pl.ds(pl.multiple_of(8 * slot, 8), 8), :] = jnp.zeros((8, pix), jnp.float32)

    @pl.when(live)
    def _():
        near = info[2 * slot + 1] - 2 * info[2 * slots + 1] < 2
        load_queries(info, slots, own_q, side1, side3, q_ref, qt_ref)
        load_keys(near, owns[parts - last :], nexts[parts - last :], k_ref, vt_ref)
        add_keys(k_ref, vt_ref, qt_ref, acc_ref, old, factor)
        sums = acc_ref[0, channels : channels + 1, :]
        fits = (jnp.min(sums) > 1e-20) & (jnp.max(sums) < 1e25)

        @pl.when(jnp.logical_not(fits))
        def _():
            load_keys(near, owns, nexts, kall_ref, vtall_ref)
            chunks = kall_ref.shape[0] // CHUNK

            def exact(t, carry):
                at = pl.ds(pl.multiple_of(t * TILE, TILE), TILE)
                q = qt_ref[:, at]

                def scores(j):
                    span = pl.ds(pl.multiple_of(j * CHUNK, CHUNK), CHUNK)
                    return jnp.dot(kall_ref[span, :], q, preferred_element_type=jnp.float32)

                top = lax.fori_loop(
                    0,
                    chunks,
                    lambda j, top: jnp.maximum(top, jnp.max(scores(j), axis=0, keepdims=True)),
                    jnp.full((1, TILE), -3e38, jnp.float32),
                )

                def add(j, acc):
                    span = pl.ds(pl.multiple_of(j * CHUNK, CHUNK), CHUNK)
                    p = jnp.exp2((scores(j) - top) * factor).astype(jnp.bfloat16)
                    return acc + jnp.dot(vtall_ref[:, span], p, preferred_element_type=jnp.float32)

                acc_ref[0, :, at] = lax.fori_loop(
                    0, chunks, add, jnp.zeros((acc_ref.shape[1], TILE), jnp.float32)
                )
                return carry

            lax.fori_loop(0, ext // TILE, exact, 0)

        h_ref[halo : halo + pix, :] = state[0]
        h_ref[pl.ds(at1, halo), :] = hide1[0]
        h_ref[pl.ds(at3, halo), :] = hide3[0]
        col = px & (cols - 1)
        first, final = col == 0, col == cols - 1

        def spread(value, at, lane):
            size = value.shape[0]
            span = slice(lane, lane + channels)
            x_ref[at, span] = jnp.where(first[at], 0.0, pltpu.roll(value, 1, 0)).astype(jnp.bfloat16)
            span = slice(lane + 2 * channels, lane + 3 * channels)
            x_ref[at, span] = value.astype(jnp.bfloat16)
            span = slice(lane + 4 * channels, lane + 5 * channels)
            x_ref[at, span] = jnp.where(final[at], 0.0, pltpu.roll(value, size - 1, 0)).astype(jnp.bfloat16)

        wide = h_ref[...].astype(jnp.float32) * valid
        spread(wide, slice(0, ext), 0)
        weight = inside(lax.broadcasted_iota(jnp.int32, (1, ext), 1)) / acc_ref[0, channels : channels + 1, :]
        spread((acc_ref[0, :channels, :] * weight).T, slice(0, ext), channels)
        mid = ext - 2 * cols
        gates = None
        for r in range(3):
            part = jnp.dot(x_ref[r * cols : r * cols + mid, :], wg[r], preferred_element_type=jnp.float32)
            gates = part if r == 0 else gates + part
        inner = slice(cols, cols + mid)
        spread(gate(gates[:, channels:]) * wide[inner], inner, 0)
        pair = jnp.dot(x_ref[cols : 2 * cols + pix, :], wc01[...], preferred_element_type=jnp.float32)
        cand = jnp.dot(x_ref[3 * cols : 3 * cols + pix, :], wc2[...], preferred_element_type=jnp.float32)
        cand = cand + pair[:pix, :channels] + pair[cols : cols + pix, channels:]
        update = gate(gates[cols : cols + pix, :channels])
        kept = wide[halo : halo + pix]
        fresh = ((1.0 - update) * kept + update * jnp.tanh(cand)).astype(jnp.bfloat16)
        fresh_ref[0] = fresh
        head = lax.dot_general(wh[...], fresh, NT, preferred_element_type=jnp.float32)
        head_ref[pl.ds(pl.multiple_of(8 * slot, 8), 8), :] = head

    @pl.when(slot == slots - 1)
    def _():
        bundle_body(
            slots, total_rows, cols, info, poses, rho_ref, head_ref, block_ref, pull_ref, scale_ref, a_ref, w_ref
        )


class Specs:
    def __init__(self, slots, pix, channels, halo):
        self.slots, self.pix, self.channels, self.halo = slots, pix, channels, halo
        self.at = 2 * slots + 1

    def source(self, s, info):
        return jnp.clip(info[2 * s] - 2 * info[self.at], 0, 1)

    def target(self, s, info):
        return info[2 * s + 1] - 2 * info[self.at]

    def side(self, flip):
        far = self.pix // self.halo - 1

        def index(s, info):
            low = (info[self.at + 1] & 1) == flip
            return (self.source(s, info), jnp.where(low, far, 0), 0)

        return pl.BlockSpec((1, self.halo, self.channels), index)

    def queries(self):
        main = pl.BlockSpec((1, self.pix, self.channels), lambda s, info: (self.source(s, info), 0, 0))
        return [main, self.side(1), self.side(0)]

    def parts(self, parts, base):
        return [
            pl.BlockSpec(
                (1, part.shape[1], self.channels),
                lambda s, info: (jnp.clip(self.target(s, info) - base, 0, 1), 0, 0),
            )
            for part in parts
        ]

    def slot(self, rows, lanes):
        return pl.BlockSpec((1, rows, lanes), lambda s, info: (s, 0, 0))

    def whole(self, shape):
        return pl.BlockSpec(shape, lambda s, info: (0,) * len(shape))


def match_call(info, slots, cols, queries, owns, nexts, old):
    pix, channels = queries[0].shape[1:]
    halo = 2 * cols
    ext = pix + 2 * halo
    keys = sum(part.shape[1] for part in owns)
    specs = Specs(slots, pix, channels, halo)
    chained = () if old is None else (old,)
    return pl.pallas_call(
        functools.partial(match_body, (slots, len(owns), len(chained))),
        grid_spec=pltpu.PrefetchScalarGridSpec(
            num_scalar_prefetch=1,
            grid=(slots,),
            in_specs=specs.queries()
            + specs.parts(owns, 0)
            + specs.parts(nexts, 2)
            + [specs.slot(channels + 8, ext) for _ in chained],
            out_specs=specs.slot(channels + 8, ext),
            scratch_shapes=[
                pltpu.VMEM((ext, channels), jnp.bfloat16),
                pltpu.VMEM((channels, ext), jnp.bfloat16),
                pltpu.VMEM((keys, channels), jnp.bfloat16),
                pltpu.VMEM((channels + 8, keys), jnp.bfloat16),
            ],
        ),
        out_shape=jax.ShapeDtypeStruct((slots, channels + 8, ext), jnp.float32),
        cost_estimate=pl.CostEstimate(
            flops=4 * slots * ext * keys * 2 * channels,
            bytes_accessed=slots * ext * (channels + 8) * 8,
            transcendentals=slots * ext * keys,
        ),
        compiler_params=pltpu.CompilerParams(vmem_limit_bytes=32 << 20),
        name="match_part",
    )(info, *queries, *owns, *nexts, *chained)


def fused_call(info, queries, old, state, hide1, hide3, owns, nexts, last, weights, poses, inv_depth, total_rows, cols):
    slots, pix, channels = state.shape
    halo = 2 * cols
    ext = pix + 2 * halo
    keys = sum(part.shape[1] for part in owns)
    part_keys = sum(part.shape[1] for part in owns[len(owns) - last :])
    specs = Specs(slots, pix, channels, halo)
    dims = (slots, total_rows, pix // cols, cols, last, len(owns))
    wide = channels + 8
    return pl.pallas_call(
        functools.partial(fused_body, dims),
        grid_spec=pltpu.PrefetchScalarGridSpec(
            num_scalar_prefetch=1,
            grid=(slots,),
            in_specs=specs.queries()
            + [specs.slot(wide, ext), specs.slot(pix, channels), specs.slot(halo, channels), specs.slot(halo, channels)]
            + specs.parts(owns, 0)
            + specs.parts(nexts, 2)
            + [specs.whole(value.shape) for value in (*weights, poses, inv_depth)],
            out_specs=(
                specs.slot(pix, channels),
                specs.whole((8, 128)),
                specs.whole((32, 2 * pix)),
                specs.whole((2, pix)),
            ),
            scratch_shapes=[
                pltpu.VMEM((ext, channels), jnp.bfloat16),
                pltpu.VMEM((channels, ext), jnp.bfloat16),
                pltpu.VMEM((part_keys, channels), jnp.bfloat16),
                pltpu.VMEM((wide, part_keys), jnp.bfloat16),
                pltpu.VMEM((1, wide, ext), jnp.float32),
                pltpu.VMEM((keys, channels), jnp.bfloat16),
                pltpu.VMEM((wide, keys), jnp.bfloat16),
                pltpu.VMEM((ext, 6 * channels), jnp.bfloat16),
                pltpu.VMEM((ext, channels), jnp.bfloat16),
                pltpu.VMEM((8 * slots, pix), jnp.float32),
                pltpu.VMEM((8 * slots, 2 * pix), jnp.float32),
                pltpu.VMEM((8 * slots, 2 * pix), jnp.float32),
            ],
        ),
        out_shape=(
            jax.ShapeDtypeStruct((slots, pix, channels), jnp.bfloat16),
            jax.ShapeDtypeStruct((8, 128), jnp.float32),
            jax.ShapeDtypeStruct((32, 2 * pix), jnp.float32),
            jax.ShapeDtypeStruct((2, pix), jnp.float32),
        ),
        compiler_params=pltpu.CompilerParams(vmem_limit_bytes=40 << 20),
        name="match_update",
    )(info, *queries, old, state, hide1, hide3, *owns, *nexts, *weights, poses, inv_depth)


def shards(features, poses, inv_depth, hidden, edges, counts, w_gates, w_cand, w_head):
    slot_count, row_count, col_count, hid_width = hidden.shape
    channels = features.shape[3]
    node_rank = lax.axis_index(EDGE)
    pix_rank = lax.axis_index("x")
    total_rows = row_count * lax.axis_size("x")
    pix = row_count * col_count
    nodes = lax.axis_size(EDGE)
    halo = 2 * col_count
    info = jnp.concatenate([edges.reshape(-1), counts, jnp.stack([node_rank, pix_rank])]).astype(jnp.int32)

    def following(value):
        return lax.ppermute(value, EDGE, [(i + 1, i) for i in range(nodes - 1)])

    own = features.reshape(2, pix, channels)
    state = hidden.reshape(slot_count, pix, hid_width)
    own1, own3 = swapped(own, "x", 1), swapped(own, "x", 3)
    next0 = following(own)
    odd = pix_rank & 1
    send1 = lax.dynamic_slice_in_dim(state, (1 - odd) * (pix - halo), halo, axis=1)
    send3 = lax.dynamic_slice_in_dim(state, odd * (pix - halo), halo, axis=1)
    hide1, hide3 = swapped(send1, "x", 1), swapped(send3, "x", 3)
    half = pix // 2
    own2a = swapped(own1[:, :half], "x", 3)
    own2b = swapped(own3[:, half:], "x", 1)
    next1, next3 = following(own1), following(own3)
    next2a, next2b = following(own2a), following(own2b)
    queries = (own, own1, own3)
    first = match_call(info, slot_count, col_count, queries, (own,), (next0,), None)
    second = match_call(info, slot_count, col_count, queries, (own1, own3), (next1, next3), first)
    wg = w_gates.reshape(3, -1, w_gates.shape[2])
    wc = w_cand.reshape(3, -1, w_cand.shape[2])
    wc01 = jnp.concatenate([wc[0], wc[1]], axis=1)
    wh = jnp.concatenate([w_head, jnp.zeros_like(w_head)], axis=0)
    fresh, block, pull, scale = fused_call(
        info,
        queries,
        second,
        state,
        hide1,
        hide3,
        (own, own1, own3, own2a, own2b),
        (next0, next1, next3, next2a, next2b),
        2,
        (wg, wc01, wc[2], wh),
        poses,
        inv_depth,
        total_rows,
        col_count,
    )
    gathered = gathered_blocks(block)
    pose_update, depth_update = solve_call(info[2 * slot_count + 1 :], gathered, pull, scale)
    return (fresh.reshape(hidden.shape), pose_update, depth_update)


def solution(mesh):
    nodes, pix = mesh.devices.shape
    fine = Mesh(mesh.devices.reshape(nodes // 16, 8, 2, pix), EDGE + ("x",))
    placed = (
        P(EDGE, "x", None, None),
        P(),
        P(EDGE, "x"),
        P(EDGE, "x", None, None),
        P(EDGE, None),
        P(EDGE),
        P(),
        P(),
        P(),
    )
    return jax.shard_map(
        shards,
        mesh=fine,
        in_specs=placed,
        out_specs=(P(EDGE, "x", None, None), P(EDGE, None), P(EDGE, "x")),
        check_vma=False,
    )
```

```python
import functools
import math

import jax
import jax.numpy as jnp
from jax import lax
from jax.experimental import pallas as pl
from jax.experimental.pallas import tpu as pltpu
from jax.sharding import Mesh
from jax.sharding import PartitionSpec as P

PRECISE = lax.Precision.HIGHEST
POSE_DAMPING = 0.1
DEPTH_DAMPING = 0.1

EDGE = ("y", "z", "core")


def swapped(value, axis, step):
    count = lax.axis_size(axis)
    return lax.ppermute(value, axis, [(i, i ^ step) for i in range(count)])


def gathered_blocks(block):
    pair = block + swapped(block, "x", 1)
    block = pair + (swapped(block, "x", 2) + swapped(block, "x", 3))
    parts = lax.all_gather(block, "core", axis=0)
    parts = jnp.stack([parts] + [swapped(parts, "z", s) for s in (1, 2, 3)])
    parts = jnp.stack([parts, swapped(parts, "z", 4)])
    parts = jnp.stack([parts] + [swapped(parts, "y", s) for s in (1, 2, 3)])
    return parts.reshape((-1,) + block.shape)


def bundle_body(slots, rows_all, cols, info, poses, rho_ref, head, out, h_ref, h_out, a_ref, w_ref, sem):
    pix = rho_ref.shape[1]
    rows = pix // cols
    shift = cols.bit_length() - 1
    base = 2 * info[2 * slots + 1]
    live = info[2 * slots]
    lane = lax.broadcasted_iota(jnp.int32, (1, pix), 1)
    col = (lane & (cols - 1)).astype(jnp.float32)
    row = ((lane >> shift) + info[2 * slots + 2] * rows).astype(jnp.float32)
    half = cols / 2.0
    u = (col - (cols - 1) / 2.0) / half
    v = (row - (rows_all - 1) / 2.0) / half
    sub = lax.broadcasted_iota(jnp.int32, (8, pix), 0)
    zero = jnp.zeros((8, pix), jnp.float32)
    lead_h = jnp.where(sub == 0, 1.0, jnp.where(sub == 2, -u, zero))
    rest_h = jnp.where(sub == 3, -u * v, jnp.where(sub == 4, 1.0 + u * u, jnp.where(sub == 5, -v, zero)))
    lead_v = jnp.where(sub == 1, 1.0, jnp.where(sub == 2, -v, zero))
    rest_v = jnp.where(sub == 3, -(1.0 + v * v), jnp.where(sub == 4, u * v, jnp.where(sub == 5, u, zero)))
    sub1 = lax.broadcasted_iota(jnp.int32, (8, 1), 0)
    eye = lax.broadcasted_iota(jnp.int32, (8, 6), 0) == lax.broadcasted_iota(jnp.int32, (8, 6), 1)
    picks, sels = [], []
    for s in range(slots):
        src, tgt = info[2 * s], info[2 * s + 1]
        a_loc, b_loc = src - base, tgt - base
        alive = jnp.where(s < live, 1.0, 0.0)
        picks.append([jnp.where(a_loc == f, 1.0, 0.0) for f in range(2)])
        sels.append([jnp.where(b_loc == g, 1.0, 0.0) - jnp.where(a_loc == g, 1.0, 0.0) for g in range(4)])
        d_row = poses[pl.ds(tgt, 1), :] - poses[pl.ds(src, 1), :]
        d = jnp.sum(jnp.where(eye, jnp.broadcast_to(d_row, (8, 6)), 0.0), axis=1, keepdims=True)
        rho = rho_ref[pl.ds(a_loc, 1), :]
        conf_h = jax.nn.sigmoid(head[8 * s + 2 : 8 * s + 3, :]) * alive
        conf_v = jax.nn.sigmoid(head[8 * s + 3 : 8 * s + 4, :]) * alive
        a_h = rho * lead_h + rest_h
        a_v = rho * lead_v + rest_v
        e_h = head[8 * s : 8 * s + 1, :] - jnp.sum(a_h * d, axis=0, keepdims=True)
        e_v = head[8 * s + 1 : 8 * s + 2, :] - jnp.sum(a_v * d, axis=0, keepdims=True)
        k_h = jnp.sum(lead_h * d, axis=0, keepdims=True)
        k_v = jnp.sum(lead_v * d, axis=0, keepdims=True)
        a_h = jnp.where(sub == 6, e_h, a_h)
        a_v = jnp.where(sub == 6, e_v, a_v)
        w_h = conf_h * a_h
        w_v = conf_v * a_v
        at = slice(8 * s, 8 * s + 8)
        a_ref[at, :pix] = a_h
        a_ref[at, pix:] = a_v
        w_ref[at, :pix] = w_h
        w_ref[at, pix:] = w_v
        k_s = w_h * k_h + w_v * k_v
        dd = conf_h * k_h * k_h + conf_v * k_v * k_v
        for f in range(2):
            pick = picks[s][f]
            at = slice(f * pix, (f + 1) * pix)
            old = h_ref[32:33, at] if s else jnp.full((1, pix), DEPTH_DAMPING, jnp.float32)
            h_ref[32:33, at] = old + pick * dd
            for g in range(4):
                term = jnp.where(sub1 == 6, pick, pick * sels[s][g]) * k_s
                at = (slice(8 * g, 8 * g + 8), slice(f * pix, (f + 1) * pix))
                h_ref[at] = h_ref[at] + term if s else term
    copy = pltpu.make_async_copy(h_ref, h_out, sem)
    copy.start()
    nt = (((1,), (1,)), ((), ()))
    gram = lax.dot_general(w_ref[...], a_ref[...], nt, precision=PRECISE, preferred_element_type=jnp.float32)
    for f in range(2):
        at = slice(f * pix, (f + 1) * pix)
        w_ref[:, at] = h_ref[:32, at] * (1.0 / h_ref[32:33, at])
    schur = lax.dot_general(w_ref[...], h_ref[:32, :], nt, precision=PRECISE, preferred_element_type=jnp.float32)
    pad = jnp.zeros((32, 96), jnp.float32)
    gram = jnp.concatenate([gram, pad], axis=1)
    schur = jnp.concatenate([schur, pad], axis=1)
    lanes = lax.broadcasted_iota(jnp.int32, (8, 128), 1)
    group, inner = lanes >> 3, lanes & 7
    terms = []
    for s in range(slots):
        y = jnp.where(group == s, gram[8 * s : 8 * s + 8, :], 0.0)
        y = pltpu.roll(y, 128 - 8 * s, 1) if s else y
        y = y + pltpu.roll(y, 8, 1)
        y = y + pltpu.roll(y, 16, 1)
        coef = jnp.zeros((8, 128), jnp.float32)
        for g in range(4):
            coef = jnp.where(group == g, sels[s][g], coef)
        terms.append(y * jnp.where(inner == 6, 1.0, coef))
    total = None
    for g in range(4):
        part = -schur[8 * g : 8 * g + 8, :]
        for s in range(slots):
            part = part + sels[s][g] * terms[s]
        part = jnp.where(lanes < 32, part, 0.0)
        total = part if g == 0 else total + pltpu.roll(part, 32 * g, 1)
    out[...] = total
    copy.wait()


REAL = (0, 1, 2, 3, 4, 5, 8, 9, 10, 11, 12, 13)


def down(x, width=16):
    return jnp.broadcast_to(x, (width, 128))


def eliminate(diag, sides):
    diag, sides = list(diag), [list(side) for side in sides]
    count = len(REAL)
    for k in range(count):
        at = slice(REAL[k], REAL[k] + 1)
        scale = down(1.0 / diag[k][at, :])
        diag[k] = diag[k] * scale
        for side in sides:
            side[k] = side[k] * scale
        for i in range(count):
            if i != k:
                f = down(diag[i][at, :])
                diag[i] = diag[i] - f * diag[k]
                for side in sides:
                    side[i] = side[i] - f * side[k]
    return diag, sides


def solve_body(nodes, pix, info, g_ref, h_ref, pose_ref, depth_ref, t_ref, d_ref, l_ref, u_ref, near):
    count = len(REAL)
    lane = lax.broadcasted_iota(jnp.int32, (16, 128), 1)
    sub = lax.broadcasted_iota(jnp.int32, (16, 128), 0)
    me = info[0]
    flip = me - (me & 1)
    for n in range(nodes):
        t_ref[n] = g_ref[n ^ flip]
    rest = jnp.zeros((128 - nodes, 128), jnp.float32)
    for k in range(6):
        t = jnp.concatenate([t_ref[:, k, :], rest], axis=0).T
        for f in range(2):
            i = 6 * f + k
            far = jnp.where(lane < nodes, pltpu.roll(t[32 * f + 80 : 32 * f + 96], 1, 1), 0.0)
            d_ref[i] = t[32 * f : 32 * f + 16] + far + jnp.where(sub == REAL[i], POSE_DAMPING, 0.0)
            u_ref[i] = jnp.where(lane < nodes - 1, t[32 * f + 16 : 32 * f + 32], 0.0)
            l_ref[i] = jnp.where(lane < nodes, pltpu.roll(t[32 * f + 64 : 32 * f + 80], 1, 1), 0.0)

    def level(step, carry):
        s = jnp.left_shift(1, step)
        diag, (low, up) = eliminate(
            [d_ref[i] for i in range(count)], [[l_ref[i] for i in range(count)], [u_ref[i] for i in range(count)]]
        )
        for k in range(count):
            low_r = jnp.where(sub == 6, diag[k], low[k])
            up_r = jnp.where(sub == 6, diag[k], up[k])
            near[0, k] = pltpu.roll(up_r, s, 1)
            near[1, k] = pltpu.roll(low[k], s, 1)
            near[2, k] = pltpu.roll(low_r, 128 - s, 1)
            near[3, k] = pltpu.roll(up[k], 128 - s, 1)
        for i in range(count):
            d_new = d_ref[i]
            l_old, u_old = l_ref[i], u_ref[i]
            l_new = jnp.zeros((16, 128), jnp.float32)
            u_new = jnp.zeros((16, 128), jnp.float32)
            for k in range(count):
                at = slice(REAL[k], REAL[k] + 1)
                fl, fu = down(l_old[at, :]), down(u_old[at, :])
                d_new = d_new - fl * near[0, k] - fu * near[2, k]
                l_new = l_new - fl * near[1, k]
                u_new = u_new - fu * near[3, k]
            d_ref[i] = d_new
            l_ref[i] = l_new
            u_ref[i] = u_new
        return carry

    levels = max(1, (nodes - 1).bit_length())
    lax.fori_loop(0, levels, level, 0)
    diag, _ = eliminate([d_ref[i] for i in range(count)], [])
    x = jnp.zeros((16, 128), jnp.float32)
    for i in range(count):
        x = jnp.where(sub == REAL[i], down(diag[i][6:7, :]), x)
    own = jnp.sum(jnp.where(lane == me, x, 0.0), axis=1, keepdims=True)
    after = jnp.sum(jnp.where((lane == me + 1) & (lane < nodes), x, 0.0), axis=1, keepdims=True)
    spread = jnp.where((sub & 7) == lane, jnp.broadcast_to(own, (16, 128)), 0.0)
    for f in range(2):
        pose_ref[f : f + 1, :] = jnp.sum(spread[8 * f : 8 * f + 8], axis=0, keepdims=True)[:, :6]
    column = jnp.concatenate([own, after], axis=0)
    column = jnp.where(lax.broadcasted_iota(jnp.int32, (32, 1), 0) == 6, -1.0, column)
    for f in range(2):
        at = slice(f * pix, (f + 1) * pix)
        depth_ref[f : f + 1, :] = -jnp.sum(h_ref[:32, at] * column, axis=0, keepdims=True) / h_ref[32:33, at]


def solve_call(me, gathered, h):
    nodes = gathered.shape[0]
    pix = h.shape[1] // 2
    vmem = pl.BlockSpec(memory_space=pltpu.VMEM)
    return pl.pallas_call(
        functools.partial(solve_body, nodes, pix),
        out_shape=(
            jax.ShapeDtypeStruct((2, 6), jnp.float32),
            jax.ShapeDtypeStruct((2, pix), jnp.float32),
        ),
        in_specs=[pl.BlockSpec(memory_space=pltpu.SMEM), vmem, vmem],
        out_specs=(vmem, vmem),
        scratch_shapes=[
            pltpu.VMEM((nodes, 8, 128), jnp.float32),
            pltpu.VMEM((12, 16, 128), jnp.float32),
            pltpu.VMEM((12, 16, 128), jnp.float32),
            pltpu.VMEM((12, 16, 128), jnp.float32),
            pltpu.VMEM((4, 12, 16, 128), jnp.float32),
        ],
        name="pose_solve",
    )(me, gathered, h)


NT = (((1,), (1,)), ((), ()))
TILE = 256
CHUNK = 768


def spots(info, slots, pix, halo):
    odd = (info[2 * slots + 2] & 1) == 1
    at1 = pl.multiple_of(jnp.where(odd, 0, halo + pix), halo)
    at3 = pl.multiple_of(jnp.where(odd, halo + pix, 0), halo)
    return at1, at3


def turned(value):
    return value.astype(jnp.float32).T.astype(jnp.bfloat16)


def load_keys(target, owns, nexts, k_ref, vt_ref):
    channels = k_ref.shape[1]

    @pl.when(target < 2)
    def _():
        base = 0
        for part in owns:
            k_ref[base : base + part.shape[1], :] = part[target]
            base += part.shape[1]

    @pl.when(target >= 2)
    def _():
        base = 0
        for part in nexts:
            k_ref[base : base + part.shape[1], :] = part[target - 2]
            base += part.shape[1]

    vt_ref[:channels, :] = turned(k_ref[...])
    vt_ref[channels:, :] = jnp.ones((vt_ref.shape[0] - channels, vt_ref.shape[1]), jnp.bfloat16)


def add_keys(slot, k_ref, vt_ref, qt_ref, old, factor, put):
    chunks = k_ref.shape[0] // CHUNK
    spots_t = [slice(t * TILE, (t + 1) * TILE) for t in range(qt_ref.shape[2] // TILE)]

    def scores(j):
        keys = k_ref[j * CHUNK : (j + 1) * CHUNK, :]
        return [jnp.dot(keys, qt_ref[slot, :, at], preferred_element_type=jnp.float32) for at in spots_t]

    held = scores(0)
    sums = [None if old is None else old[slot, :, at] for at in spots_t]
    for j in range(chunks):
        later = scores(j + 1) if j + 1 < chunks else None
        for t in range(len(spots_t)):
            p = jnp.exp2(held[t] * factor).astype(jnp.bfloat16)
            part = jnp.dot(vt_ref[:, j * CHUNK : (j + 1) * CHUNK], p, preferred_element_type=jnp.float32)
            sums[t] = part if sums[t] is None else sums[t] + part
        held = later
    for at, value in zip(spots_t, sums):
        put(at, value)


def load_queries(info, slots, slot, own_q, side1, side3, qt_ref):
    pix, halo = own_q.shape[1], qt_ref.shape[2] - own_q.shape[1]
    halo = halo // 2
    at1, at3 = spots(info, slots, pix, halo)
    odd = (info[2 * slots + 2] & 1) == 1
    from1 = pl.multiple_of(jnp.where(odd, pix - halo, 0), halo)
    from3 = pl.multiple_of(jnp.where(odd, 0, pix - halo), halo)
    src = info[2 * slot] - 2 * info[2 * slots + 1]
    qt_ref[slot, :, halo : halo + pix] = turned(own_q[src])
    qt_ref[slot, :, pl.ds(at1, halo)] = turned(side1[src, pl.ds(from1, halo), :])
    qt_ref[slot, :, pl.ds(at3, halo)] = turned(side3[src, pl.ds(from3, halo), :])


def match_factor(channels):
    return 2.0 / math.sqrt(channels) * math.log2(math.e)


def first_body(slots, info, own_q, side1, side3, own, after, acc_ref, qt_ref, k_ref, vt_ref):
    def one(slot, carry):
        target = info[2 * slot + 1] - 2 * info[2 * slots + 1]
        load_queries(info, slots, slot, own_q, side1, side3, qt_ref)
        load_keys(target, (own,), (after,), k_ref, vt_ref)


        def put(at, value):
            acc_ref[slot, :, at] = value

        add_keys(slot, k_ref, vt_ref, qt_ref, None, match_factor(k_ref.shape[1]), put)
        return carry

    lax.fori_loop(0, info[2 * slots], one, 0)


def second_body(slots, parts, info, qt_ref, old, *refs):
    owns, nexts = refs[:parts], refs[parts : 2 * parts]
    acc_ref, k_ref, vt_ref = refs[2 * parts :]

    def one(slot, carry):
        target = info[2 * slot + 1] - 2 * info[2 * slots + 1]
        load_keys(target, owns, nexts, k_ref, vt_ref)


        def put(at, value):
            acc_ref[slot, :, at] = value

        add_keys(slot, k_ref, vt_ref, qt_ref, old, match_factor(k_ref.shape[1]), put)
        return carry

    lax.fori_loop(0, info[2 * slots], one, 0)


def fused_body(dims, info, *refs):
    slots, total_rows, rows, cols, last, parts = dims
    (qt_ref, old), refs = refs[:2], refs[2:]
    (state, hide1, hide3), refs = refs[:3], refs[3:]
    owns, refs = refs[:parts], refs[parts:]
    nexts, refs = refs[:parts], refs[parts:]
    (wg, wc01, wc2, wh, poses, rho_ref), refs = refs[:6], refs[6:]
    (fresh_out, block_ref, pull_out), refs = refs[:3], refs[3:]
    fresh_ref, pull_ref, k_ref, vt_ref, acc_ref, kall_ref, vtall_ref, x_ref, h_ref = refs[:9]
    head_ref, a_ref, w_ref, sems = refs[9:]
    pix_rank = info[2 * slots + 2]
    pix = rows * cols
    halo = 2 * cols
    ext = pix + 2 * halo
    channels = state.shape[-1]
    factor = match_factor(channels)
    at1, at3 = spots(info, slots, pix, halo)
    px = lax.broadcasted_iota(jnp.int32, (ext, 1), 0)

    def inside(px):
        grow = (px >> (cols.bit_length() - 1)) - 2 + rows * pix_rank
        return jnp.where((grow >= 0) & (grow < total_rows), 1.0, 0.0)

    valid = inside(px)

    def send(slot):
        return pltpu.make_async_copy(fresh_ref.at[slot], fresh_out.at[slot], sems.at[slot])

    def keep(slot, carry):
        fresh_ref[slot] = state[slot]
        head_ref[pl.ds(pl.multiple_of(8 * slot, 8), 8), :] = jnp.zeros((8, pix), jnp.float32)
        send(slot).start()
        return carry

    lax.fori_loop(info[2 * slots], slots, keep, 0)

    def one(slot, carry):
        target = info[2 * slot + 1] - 2 * info[2 * slots + 1]
        load_keys(target, owns[parts - last :], nexts[parts - last :], k_ref, vt_ref)

        def put(at, value):
            acc_ref[0, :, at] = value

        add_keys(slot, k_ref, vt_ref, qt_ref, old, factor, put)
        sums = acc_ref[0, channels : channels + 1, :]
        fits = (jnp.min(sums) > 1e-20) & (jnp.max(sums) < 1e25)

        @pl.when(jnp.logical_not(fits))
        def _():
            load_keys(target, owns, nexts, kall_ref, vtall_ref)
            chunks = kall_ref.shape[0] // CHUNK

            def exact(t, carry):
                at = pl.ds(pl.multiple_of(t * TILE, TILE), TILE)
                q = qt_ref[slot, :, at]

                def scores(j):
                    span = pl.ds(pl.multiple_of(j * CHUNK, CHUNK), CHUNK)
                    return jnp.dot(kall_ref[span, :], q, preferred_element_type=jnp.float32)

                top = lax.fori_loop(
                    0,
                    chunks,
                    lambda j, top: jnp.maximum(top, jnp.max(scores(j), axis=0, keepdims=True)),
                    jnp.full((1, TILE), -3e38, jnp.float32),
                )

                def add(j, acc):
                    span = pl.ds(pl.multiple_of(j * CHUNK, CHUNK), CHUNK)
                    p = jnp.exp2((scores(j) - top) * factor).astype(jnp.bfloat16)
                    return acc + jnp.dot(vtall_ref[:, span], p, preferred_element_type=jnp.float32)

                acc_ref[0, :, at] = lax.fori_loop(
                    0, chunks, add, jnp.zeros((acc_ref.shape[1], TILE), jnp.float32)
                )
                return carry

            lax.fori_loop(0, ext // TILE, exact, 0)

        h_ref[halo : halo + pix, :] = state[slot]
        h_ref[pl.ds(at1, halo), :] = hide1[slot]
        h_ref[pl.ds(at3, halo), :] = hide3[slot]
        col = px & (cols - 1)
        first, final = col == 0, col == cols - 1

        def spread(value, at, lane):
            size = value.shape[0]
            span = slice(lane, lane + channels)
            x_ref[at, span] = jnp.where(first[at], 0.0, pltpu.roll(value, 1, 0)).astype(jnp.bfloat16)
            span = slice(lane + 2 * channels, lane + 3 * channels)
            x_ref[at, span] = value.astype(jnp.bfloat16)
            span = slice(lane + 4 * channels, lane + 5 * channels)
            x_ref[at, span] = jnp.where(final[at], 0.0, pltpu.roll(value, size - 1, 0)).astype(jnp.bfloat16)

        wide = h_ref[...].astype(jnp.float32) * valid
        spread(wide, slice(0, ext), 0)
        weight = inside(lax.broadcasted_iota(jnp.int32, (1, ext), 1)) / acc_ref[0, channels : channels + 1, :]
        spread((acc_ref[0, :channels, :] * weight).T, slice(0, ext), channels)
        mid = ext - 2 * cols
        gates = None
        for r in range(3):
            part = jnp.dot(x_ref[r * cols : r * cols + mid, :], wg[r], preferred_element_type=jnp.float32)
            gates = part if r == 0 else gates + part
        inner = slice(cols, cols + mid)
        spread(jax.nn.sigmoid(gates[:, channels:]) * wide[inner], inner, 0)
        pair = jnp.dot(x_ref[cols : 2 * cols + pix, :], wc01[...], preferred_element_type=jnp.float32)
        cand = jnp.dot(x_ref[3 * cols : 3 * cols + pix, :], wc2[...], preferred_element_type=jnp.float32)
        cand = cand + pair[:pix, :channels] + pair[cols : cols + pix, channels:]
        update = jax.nn.sigmoid(gates[cols : cols + pix, :channels])
        kept = wide[halo : halo + pix]
        fresh = ((1.0 - update) * kept + update * jnp.tanh(cand)).astype(jnp.bfloat16)
        fresh_ref[slot] = fresh
        head = lax.dot_general(wh[...], fresh, NT, preferred_element_type=jnp.float32)
        head_ref[pl.ds(pl.multiple_of(8 * slot, 8), 8), :] = head
        send(slot).start()
        return carry

    lax.fori_loop(0, info[2 * slots], one, 0)
    bundle_body(
        slots, total_rows, cols, info, poses, rho_ref, head_ref, block_ref, pull_ref, pull_out, a_ref, w_ref, sems.at[slots]
    )
    for slot in range(slots):
        send(slot).wait()


VMEM = pl.BlockSpec(memory_space=pltpu.VMEM)
SMEM = pl.BlockSpec(memory_space=pltpu.SMEM)


def work(slots, ext, keys, channels):
    return pl.CostEstimate(
        flops=4 * slots * ext * keys * 2 * channels,
        bytes_accessed=slots * ext * (channels + 8) * 8,
        transcendentals=slots * ext * keys,
    )


def first_call(info, slots, cols, queries, own, after):
    pix, channels = own.shape[1:]
    ext = pix + 4 * cols
    return pl.pallas_call(
        functools.partial(first_body, slots),
        in_specs=[SMEM] + [VMEM] * 5,
        out_specs=(VMEM, VMEM),
        scratch_shapes=[pltpu.VMEM((pix, channels), jnp.bfloat16), pltpu.VMEM((channels + 8, pix), jnp.bfloat16)],
        out_shape=(
            jax.ShapeDtypeStruct((slots, channels + 8, ext), jnp.float32),
            jax.ShapeDtypeStruct((slots, channels, ext), jnp.bfloat16),
        ),
        cost_estimate=work(slots, ext, pix, channels),
        compiler_params=pltpu.CompilerParams(vmem_limit_bytes=14 << 20),
        name="match_first",
    )(info, *queries, own, after)


def second_call(info, qt, old, owns, nexts):
    slots, channels, ext = qt.shape
    keys = sum(part.shape[1] for part in owns)
    return pl.pallas_call(
        functools.partial(second_body, slots, len(owns)),
        in_specs=[SMEM] + [VMEM] * (2 + 2 * len(owns)),
        out_specs=VMEM,
        scratch_shapes=[pltpu.VMEM((keys, channels), jnp.bfloat16), pltpu.VMEM((channels + 8, keys), jnp.bfloat16)],
        out_shape=jax.ShapeDtypeStruct(old.shape, jnp.float32),
        cost_estimate=work(slots, ext, keys, channels),
        compiler_params=pltpu.CompilerParams(vmem_limit_bytes=14 << 20),
        name="match_second",
    )(info, qt, old, *owns, *nexts)


def fused_call(info, qt, old, state, hide1, hide3, owns, nexts, last, weights, poses, inv_depth, total_rows, cols):
    slots, pix, channels = state.shape
    ext = qt.shape[2]
    keys = sum(part.shape[1] for part in owns)
    part_keys = sum(part.shape[1] for part in owns[len(owns) - last :])
    dims = (slots, total_rows, pix // cols, cols, last, len(owns))
    wide = channels + 8
    return pl.pallas_call(
        functools.partial(fused_body, dims),
        in_specs=[SMEM] + [VMEM] * (5 + 2 * len(owns) + len(weights) + 2),
        out_specs=(pl.BlockSpec(memory_space=pltpu.HBM), VMEM, pl.BlockSpec(memory_space=pltpu.HBM)),
        scratch_shapes=[
            pltpu.VMEM((slots, pix, channels), jnp.bfloat16),
            pltpu.VMEM((40, 2 * pix), jnp.float32),
            pltpu.VMEM((part_keys, channels), jnp.bfloat16),
            pltpu.VMEM((wide, part_keys), jnp.bfloat16),
            pltpu.VMEM((1, wide, ext), jnp.float32),
            pltpu.VMEM((keys, channels), jnp.bfloat16),
            pltpu.VMEM((wide, keys), jnp.bfloat16),
            pltpu.VMEM((ext, 6 * channels), jnp.bfloat16),
            pltpu.VMEM((ext, channels), jnp.bfloat16),
            pltpu.VMEM((8 * slots, pix), jnp.float32),
            pltpu.VMEM((8 * slots, 2 * pix), jnp.float32),
            pltpu.VMEM((8 * slots, 2 * pix), jnp.float32),
            pltpu.SemaphoreType.DMA((slots + 1,)),
        ],
        out_shape=(
            jax.ShapeDtypeStruct((slots, pix, channels), jnp.bfloat16),
            jax.ShapeDtypeStruct((8, 128), jnp.float32),
            jax.ShapeDtypeStruct((40, 2 * pix), jnp.float32),
        ),
        compiler_params=pltpu.CompilerParams(vmem_limit_bytes=26 << 20),
        name="match_update",
    )(info, qt, old, state, hide1, hide3, *owns, *nexts, *weights, poses, inv_depth)


def shards(features, poses, inv_depth, hidden, edges, counts, w_gates, w_cand, w_head):
    slot_count, row_count, col_count, hid_width = hidden.shape
    channels = features.shape[3]
    node_rank = lax.axis_index(EDGE)
    pix_rank = lax.axis_index("x")
    total_rows = row_count * lax.axis_size("x")
    pix = row_count * col_count
    nodes = lax.axis_size(EDGE)
    halo = 2 * col_count
    info = jnp.concatenate([edges.reshape(-1), counts, jnp.stack([node_rank, pix_rank])]).astype(jnp.int32)

    def following(value):
        return lax.ppermute(value, EDGE, [(i + 1, i) for i in range(nodes - 1)])

    own = features.reshape(2, pix, channels)
    state = hidden.reshape(slot_count, pix, hid_width)
    own1, own3 = swapped(own, "x", 1), swapped(own, "x", 3)
    next0 = following(own)
    odd = pix_rank & 1
    send1 = lax.dynamic_slice_in_dim(state, (1 - odd) * (pix - halo), halo, axis=1)
    send3 = lax.dynamic_slice_in_dim(state, odd * (pix - halo), halo, axis=1)
    hide1, hide3 = swapped(send1, "x", 1), swapped(send3, "x", 3)
    half = pix // 2
    own2a = swapped(own1[:, :half], "x", 3)
    own2b = swapped(own3[:, half:], "x", 1)
    next1, next3 = following(own1), following(own3)
    next2a, next2b = following(own2a), following(own2b)
    queries = (own, own1, own3)
    acc, turned = first_call(info, slot_count, col_count, queries, own, next0)
    acc = second_call(info, turned, acc, (own1, own3), (next1, next3))
    wg = w_gates.reshape(3, -1, w_gates.shape[2])
    wc = w_cand.reshape(3, -1, w_cand.shape[2])
    wc01 = jnp.concatenate([wc[0], wc[1]], axis=1)
    wh = jnp.concatenate([w_head, jnp.zeros_like(w_head)], axis=0)
    fresh, block, pull = fused_call(
        info,
        turned,
        acc,
        state,
        hide1,
        hide3,
        (own, own1, own3, own2a, own2b),
        (next0, next1, next3, next2a, next2b),
        2,
        (wg, wc01, wc[2], wh),
        poses,
        inv_depth,
        total_rows,
        col_count,
    )
    gathered = gathered_blocks(block)
    pose_update, depth_update = solve_call(info[2 * slot_count + 1 :], gathered, pull)
    return (fresh.reshape(hidden.shape), pose_update, depth_update)


def solution(mesh):
    nodes, pix = mesh.devices.shape
    fine = Mesh(mesh.devices.reshape(nodes // 16, 8, 2, pix), EDGE + ("x",))
    placed = (
        P(EDGE, "x", None, None),
        P(),
        P(EDGE, "x"),
        P(EDGE, "x", None, None),
        P(EDGE, None),
        P(EDGE),
        P(),
        P(),
        P(),
    )
    return jax.shard_map(
        shards,
        mesh=fine,
        in_specs=placed,
        out_specs=(P(EDGE, "x", None, None), P(EDGE, None), P(EDGE, "x")),
        check_vma=False,
    )
```

```python
import functools
import math

import jax
import jax.numpy as jnp
from jax import lax
from jax.experimental import pallas as pl
from jax.experimental.pallas import tpu as pltpu
from jax.sharding import Mesh
from jax.sharding import PartitionSpec as P

PRECISE = lax.Precision.HIGHEST
POSE_DAMPING = 0.1
DEPTH_DAMPING = 0.1

EDGE = ("y", "z", "core")


def swapped(value, axis, step):
    count = lax.axis_size(axis)
    return lax.ppermute(value, axis, [(i, i ^ step) for i in range(count)])


def gathered_blocks(block):
    pair = block + swapped(block, "x", 1)
    block = pair + (swapped(block, "x", 2) + swapped(block, "x", 3))
    parts = jnp.stack([block, swapped(block, "core", 1)])
    parts = jnp.stack([parts] + [swapped(parts, "z", s) for s in (1, 2, 3)])
    parts = jnp.stack([parts, swapped(parts, "z", 4)])
    parts = jnp.stack([parts] + [swapped(parts, "y", s) for s in (1, 2, 3)])
    return parts.reshape((-1,) + block.shape)


class Facts:
    def __init__(self, edges, counts, ranks):
        self.edges, self.counts, self.ranks = edges, counts, ranks

    def source(self, slot):
        return self.edges[0, slot]

    def target(self, slot):
        return self.edges[1, slot]

    def live(self):
        return self.counts[0]

    def node(self):
        return self.ranks[0]

    def pix(self):
        return self.ranks[1]


def bundle_body(slots, rows_all, cols, info, poses, rho_ref, head, out, h_ref, h_out, a_ref, w_ref, sem):
    pix = rho_ref.shape[1]
    rows = pix // cols
    shift = cols.bit_length() - 1
    base = 2 * info.node()
    live = info.live()
    lane = lax.broadcasted_iota(jnp.int32, (1, pix), 1)
    col = (lane & (cols - 1)).astype(jnp.float32)
    row = ((lane >> shift) + info.pix() * rows).astype(jnp.float32)
    half = cols / 2.0
    u = (col - (cols - 1) / 2.0) / half
    v = (row - (rows_all - 1) / 2.0) / half
    sub = lax.broadcasted_iota(jnp.int32, (8, pix), 0)
    zero = jnp.zeros((8, pix), jnp.float32)
    lead_h = jnp.where(sub == 0, 1.0, jnp.where(sub == 2, -u, zero))
    rest_h = jnp.where(sub == 3, -u * v, jnp.where(sub == 4, 1.0 + u * u, jnp.where(sub == 5, -v, zero)))
    lead_v = jnp.where(sub == 1, 1.0, jnp.where(sub == 2, -v, zero))
    rest_v = jnp.where(sub == 3, -(1.0 + v * v), jnp.where(sub == 4, u * v, jnp.where(sub == 5, u, zero)))
    sub1 = lax.broadcasted_iota(jnp.int32, (8, 1), 0)
    frame = lax.broadcasted_iota(jnp.int32, (1, poses.shape[1]), 1)
    picks, sels = [], []
    for s in range(slots):
        src, tgt = info.source(s), info.target(s)
        a_loc, b_loc = src - base, tgt - base
        alive = jnp.where(s < live, 1.0, 0.0)
        picks.append([jnp.where(a_loc == f, 1.0, 0.0) for f in range(2)])
        sels.append([jnp.where(b_loc == g, 1.0, 0.0) - jnp.where(a_loc == g, 1.0, 0.0) for g in range(4)])
        pick_d = jnp.where(frame == tgt, 1.0, 0.0) - jnp.where(frame == src, 1.0, 0.0)
        d = jnp.sum(poses[...] * pick_d, axis=1, keepdims=True)
        d = jnp.concatenate([d, jnp.zeros((2, 1), jnp.float32)], axis=0)
        rho = rho_ref[pl.ds(a_loc, 1), :]
        conf_h = jax.nn.sigmoid(head[8 * s + 2 : 8 * s + 3, :]) * alive
        conf_v = jax.nn.sigmoid(head[8 * s + 3 : 8 * s + 4, :]) * alive
        a_h = rho * lead_h + rest_h
        a_v = rho * lead_v + rest_v
        e_h = head[8 * s : 8 * s + 1, :] - jnp.sum(a_h * d, axis=0, keepdims=True)
        e_v = head[8 * s + 1 : 8 * s + 2, :] - jnp.sum(a_v * d, axis=0, keepdims=True)
        k_h = jnp.sum(lead_h * d, axis=0, keepdims=True)
        k_v = jnp.sum(lead_v * d, axis=0, keepdims=True)
        a_h = jnp.where(sub == 6, e_h, a_h)
        a_v = jnp.where(sub == 6, e_v, a_v)
        w_h = conf_h * a_h
        w_v = conf_v * a_v
        at = slice(8 * s, 8 * s + 8)
        a_ref[at, :pix] = a_h
        a_ref[at, pix:] = a_v
        w_ref[at, :pix] = w_h
        w_ref[at, pix:] = w_v
        k_s = w_h * k_h + w_v * k_v
        dd = conf_h * k_h * k_h + conf_v * k_v * k_v
        for f in range(2):
            pick = picks[s][f]
            at = slice(f * pix, (f + 1) * pix)
            old = h_ref[32:33, at] if s else jnp.full((1, pix), DEPTH_DAMPING, jnp.float32)
            h_ref[32:33, at] = old + pick * dd
            for g in range(4):
                term = jnp.where(sub1 == 6, pick, pick * sels[s][g]) * k_s
                at = (slice(8 * g, 8 * g + 8), slice(f * pix, (f + 1) * pix))
                h_ref[at] = h_ref[at] + term if s else term
    copy = pltpu.make_async_copy(h_ref, h_out, sem)
    copy.start()
    nt = (((1,), (1,)), ((), ()))
    gram = lax.dot_general(w_ref[...], a_ref[...], nt, precision=PRECISE, preferred_element_type=jnp.float32)
    for f in range(2):
        at = slice(f * pix, (f + 1) * pix)
        w_ref[:, at] = h_ref[:32, at] * (1.0 / h_ref[32:33, at])
    schur = lax.dot_general(w_ref[...], h_ref[:32, :], nt, precision=PRECISE, preferred_element_type=jnp.float32)
    pad = jnp.zeros((32, 96), jnp.float32)
    gram = jnp.concatenate([gram, pad], axis=1)
    schur = jnp.concatenate([schur, pad], axis=1)
    lanes = lax.broadcasted_iota(jnp.int32, (8, 128), 1)
    group, inner = lanes >> 3, lanes & 7
    terms = []
    for s in range(slots):
        y = jnp.where(group == s, gram[8 * s : 8 * s + 8, :], 0.0)
        y = pltpu.roll(y, 128 - 8 * s, 1) if s else y
        y = y + pltpu.roll(y, 8, 1)
        y = y + pltpu.roll(y, 16, 1)
        coef = jnp.zeros((8, 128), jnp.float32)
        for g in range(4):
            coef = jnp.where(group == g, sels[s][g], coef)
        terms.append(y * jnp.where(inner == 6, 1.0, coef))
    total = None
    for g in range(4):
        part = -schur[8 * g : 8 * g + 8, :]
        for s in range(slots):
            part = part + sels[s][g] * terms[s]
        part = jnp.where(lanes < 32, part, 0.0)
        total = part if g == 0 else total + pltpu.roll(part, 32 * g, 1)
    out[...] = total
    copy.wait()


REAL = (0, 1, 2, 3, 4, 5, 8, 9, 10, 11, 12, 13)


def down(x, width=16):
    return jnp.broadcast_to(x, (width, 128))


def eliminate(diag, sides):
    diag, sides = list(diag), [list(side) for side in sides]
    count = len(REAL)
    for k in range(count):
        at = slice(REAL[k], REAL[k] + 1)
        scale = down(1.0 / diag[k][at, :])
        diag[k] = diag[k] * scale
        for side in sides:
            side[k] = side[k] * scale
        for i in range(count):
            if i != k:
                f = down(diag[i][at, :])
                diag[i] = diag[i] - f * diag[k]
                for side in sides:
                    side[i] = side[i] - f * side[k]
    return diag, sides


def solve_body(nodes, pix, info, g_ref, h_ref, pose_ref, depth_ref, t_ref, d_ref, l_ref, u_ref, near):
    count = len(REAL)
    lane = lax.broadcasted_iota(jnp.int32, (16, 128), 1)
    sub = lax.broadcasted_iota(jnp.int32, (16, 128), 0)
    me = info[0]
    for n in range(nodes):
        t_ref[n] = g_ref[n ^ me]
    rest = jnp.zeros((128 - nodes, 128), jnp.float32)
    for k in range(6):
        t = jnp.concatenate([t_ref[:, k, :], rest], axis=0).T
        for f in range(2):
            i = 6 * f + k
            far = jnp.where(lane < nodes, pltpu.roll(t[32 * f + 80 : 32 * f + 96], 1, 1), 0.0)
            d_ref[i] = t[32 * f : 32 * f + 16] + far + jnp.where(sub == REAL[i], POSE_DAMPING, 0.0)
            u_ref[i] = jnp.where(lane < nodes - 1, t[32 * f + 16 : 32 * f + 32], 0.0)
            l_ref[i] = jnp.where(lane < nodes, pltpu.roll(t[32 * f + 64 : 32 * f + 80], 1, 1), 0.0)

    def level(step, carry):
        s = jnp.left_shift(1, step)
        diag, (low, up) = eliminate(
            [d_ref[i] for i in range(count)], [[l_ref[i] for i in range(count)], [u_ref[i] for i in range(count)]]
        )
        for k in range(count):
            low_r = jnp.where(sub == 6, diag[k], low[k])
            up_r = jnp.where(sub == 6, diag[k], up[k])
            near[0, k] = pltpu.roll(up_r, s, 1)
            near[1, k] = pltpu.roll(low[k], s, 1)
            near[2, k] = pltpu.roll(low_r, 128 - s, 1)
            near[3, k] = pltpu.roll(up[k], 128 - s, 1)
        for i in range(count):
            d_new = d_ref[i]
            l_old, u_old = l_ref[i], u_ref[i]
            l_new = jnp.zeros((16, 128), jnp.float32)
            u_new = jnp.zeros((16, 128), jnp.float32)
            for k in range(count):
                at = slice(REAL[k], REAL[k] + 1)
                fl, fu = down(l_old[at, :]), down(u_old[at, :])
                d_new = d_new - fl * near[0, k] - fu * near[2, k]
                l_new = l_new - fl * near[1, k]
                u_new = u_new - fu * near[3, k]
            d_ref[i] = d_new
            l_ref[i] = l_new
            u_ref[i] = u_new
        return carry

    levels = max(1, (nodes - 1).bit_length())
    lax.fori_loop(0, levels, level, 0)
    diag, _ = eliminate([d_ref[i] for i in range(count)], [])
    x = jnp.zeros((16, 128), jnp.float32)
    for i in range(count):
        x = jnp.where(sub == REAL[i], down(diag[i][6:7, :]), x)
    own = jnp.sum(jnp.where(lane == me, x, 0.0), axis=1, keepdims=True)
    after = jnp.sum(jnp.where((lane == me + 1) & (lane < nodes), x, 0.0), axis=1, keepdims=True)
    spread = jnp.where((sub & 7) == lane, jnp.broadcast_to(own, (16, 128)), 0.0)
    for f in range(2):
        pose_ref[f : f + 1, :] = jnp.sum(spread[8 * f : 8 * f + 8], axis=0, keepdims=True)[:, :6]
    column = jnp.concatenate([own, after], axis=0)
    column = jnp.where(lax.broadcasted_iota(jnp.int32, (32, 1), 0) == 6, -1.0, column)
    for f in range(2):
        at = slice(f * pix, (f + 1) * pix)
        depth_ref[f : f + 1, :] = -jnp.sum(h_ref[:32, at] * column, axis=0, keepdims=True) / h_ref[32:33, at]


def solve_call(me, gathered, h):
    nodes = gathered.shape[0]
    pix = h.shape[1] // 2
    vmem = pl.BlockSpec(memory_space=pltpu.VMEM)
    return pl.pallas_call(
        functools.partial(solve_body, nodes, pix),
        out_shape=(
            jax.ShapeDtypeStruct((2, 6), jnp.float32),
            jax.ShapeDtypeStruct((2, pix), jnp.float32),
        ),
        in_specs=[pl.BlockSpec(memory_space=pltpu.SMEM), vmem, vmem],
        out_specs=(vmem, vmem),
        scratch_shapes=[
            pltpu.VMEM((nodes, 8, 128), jnp.float32),
            pltpu.VMEM((12, 16, 128), jnp.float32),
            pltpu.VMEM((12, 16, 128), jnp.float32),
            pltpu.VMEM((12, 16, 128), jnp.float32),
            pltpu.VMEM((4, 12, 16, 128), jnp.float32),
        ],
        compiler_params=pltpu.CompilerParams(vmem_limit_bytes=12 << 20),
        name="pose_solve",
    )(me, gathered, h)


NT = (((1,), (1,)), ((), ()))
TILE = 256
CHUNK = 768


def spots(info, slots, pix, halo):
    odd = (info.pix() & 1) == 1
    at1 = pl.multiple_of(jnp.where(odd, 0, halo + pix), halo)
    at3 = pl.multiple_of(jnp.where(odd, halo + pix, 0), halo)
    return at1, at3


def turned(value):
    return value.astype(jnp.float32).T.astype(jnp.bfloat16)


def load_keys(target, owns, nexts, k_ref, vt_ref):
    channels = k_ref.shape[1]

    @pl.when(target < 2)
    def _():
        base = 0
        for part in owns:
            k_ref[base : base + part.shape[1], :] = part[target]
            base += part.shape[1]

    @pl.when(target >= 2)
    def _():
        base = 0
        for part in nexts:
            k_ref[base : base + part.shape[1], :] = part[target - 2]
            base += part.shape[1]

    vt_ref[:channels, :] = turned(k_ref[...])
    vt_ref[channels:, :] = jnp.ones((vt_ref.shape[0] - channels, vt_ref.shape[1]), jnp.bfloat16)


def add_keys(slot, k_ref, vt_ref, qt_ref, old, factor, put):
    chunks = k_ref.shape[0] // CHUNK
    spots_t = [slice(t * TILE, (t + 1) * TILE) for t in range(qt_ref.shape[2] // TILE)]

    def scores(j):
        keys = k_ref[j * CHUNK : (j + 1) * CHUNK, :]
        return [jnp.dot(keys, qt_ref[slot, :, at], preferred_element_type=jnp.float32) for at in spots_t]

    held = scores(0)
    sums = [None if old is None else old[slot, :, at] for at in spots_t]
    for j in range(chunks):
        later = scores(j + 1) if j + 1 < chunks else None
        for t in range(len(spots_t)):
            p = jnp.exp2(held[t] * factor).astype(jnp.bfloat16)
            part = jnp.dot(vt_ref[:, j * CHUNK : (j + 1) * CHUNK], p, preferred_element_type=jnp.float32)
            sums[t] = part if sums[t] is None else sums[t] + part
        held = later
    for at, value in zip(spots_t, sums):
        put(at, value)


def load_queries(info, slots, slot, own_q, side1, side3, qt_ref):
    pix, halo = own_q.shape[1], qt_ref.shape[2] - own_q.shape[1]
    halo = halo // 2
    at1, at3 = spots(info, slots, pix, halo)
    odd = (info.pix() & 1) == 1
    from1 = pl.multiple_of(jnp.where(odd, pix - halo, 0), halo)
    from3 = pl.multiple_of(jnp.where(odd, 0, pix - halo), halo)
    src = info.source(slot) - 2 * info.node()
    qt_ref[slot, :, halo : halo + pix] = turned(own_q[src])
    qt_ref[slot, :, pl.ds(at1, halo)] = turned(side1[src, pl.ds(from1, halo), :])
    qt_ref[slot, :, pl.ds(at3, halo)] = turned(side3[src, pl.ds(from3, halo), :])


def match_factor(channels):
    return 2.0 / math.sqrt(channels) * math.log2(math.e)


def first_body(slots, edges, counts, ranks, own_q, side1, side3, own, after, acc_ref, qt_ref, k_ref, vt_ref):
    info = Facts(edges, counts, ranks)

    def one(slot, carry):
        target = info.target(slot) - 2 * info.node()
        load_queries(info, slots, slot, own_q, side1, side3, qt_ref)
        load_keys(target, (own,), (after,), k_ref, vt_ref)


        def put(at, value):
            acc_ref[slot, :, at] = value

        add_keys(slot, k_ref, vt_ref, qt_ref, None, match_factor(k_ref.shape[1]), put)
        return carry

    lax.fori_loop(0, info.live(), one, 0)


def second_body(slots, parts, edges, counts, ranks, qt_ref, old, *refs):
    info = Facts(edges, counts, ranks)
    owns, nexts = refs[:parts], refs[parts : 2 * parts]
    acc_ref, k_ref, vt_ref = refs[2 * parts :]

    def one(slot, carry):
        target = info.target(slot) - 2 * info.node()
        load_keys(target, owns, nexts, k_ref, vt_ref)


        def put(at, value):
            acc_ref[slot, :, at] = value

        add_keys(slot, k_ref, vt_ref, qt_ref, old, match_factor(k_ref.shape[1]), put)
        return carry

    lax.fori_loop(0, info.live(), one, 0)


def fused_body(dims, edges, counts, ranks, *refs):
    info = Facts(edges, counts, ranks)
    slots, total_rows, rows, cols, last, parts = dims
    (qt_ref, old), refs = refs[:2], refs[2:]
    (state, hide_up, hide_down), refs = refs[:3], refs[3:]
    owns, refs = refs[:parts], refs[parts:]
    nexts, refs = refs[:parts], refs[parts:]
    (wg, wc, wh, poses, rho_ref), refs = refs[:5], refs[5:]
    (fresh_out, block_ref, pull_out), refs = refs[:3], refs[3:]
    fresh_ref, pull_ref, k_ref, vt_ref, acc_ref, kall_ref, vtall_ref, x_ref, h_ref = refs[:9]
    head_ref, a_ref, w_ref, wc01, sems = refs[9:]
    pix_rank = info.pix()
    pix = rows * cols
    halo = 2 * cols
    ext = pix + 2 * halo
    channels = state.shape[-1]
    factor = match_factor(channels)
    px = lax.broadcasted_iota(jnp.int32, (ext, 1), 0)

    def inside(px):
        grow = (px >> (cols.bit_length() - 1)) - 2 + rows * pix_rank
        return jnp.where((grow >= 0) & (grow < total_rows), 1.0, 0.0)

    valid = inside(px)
    wc01[:, :channels] = wc[0]
    wc01[:, channels:] = wc[1]

    def send(slot):
        return pltpu.make_async_copy(fresh_ref.at[slot], fresh_out.at[slot], sems.at[slot])

    def keep(slot, carry):
        fresh_ref[slot] = state[slot]
        head_ref[pl.ds(pl.multiple_of(8 * slot, 8), 8), :] = jnp.zeros((8, pix), jnp.float32)
        send(slot).start()
        return carry

    lax.fori_loop(info.live(), slots, keep, 0)

    def one(slot, carry):
        target = info.target(slot) - 2 * info.node()
        load_keys(target, owns[parts - last :], nexts[parts - last :], k_ref, vt_ref)

        def put(at, value):
            acc_ref[0, :, at] = value

        add_keys(slot, k_ref, vt_ref, qt_ref, old, factor, put)
        sums = acc_ref[0, channels : channels + 1, :]
        fits = (jnp.min(sums) > 1e-20) & (jnp.max(sums) < 1e25)

        @pl.when(jnp.logical_not(fits))
        def _():
            load_keys(target, owns, nexts, kall_ref, vtall_ref)
            chunks = kall_ref.shape[0] // CHUNK

            def exact(t, carry):
                at = pl.ds(pl.multiple_of(t * TILE, TILE), TILE)
                q = qt_ref[slot, :, at]

                def scores(j):
                    span = pl.ds(pl.multiple_of(j * CHUNK, CHUNK), CHUNK)
                    return jnp.dot(kall_ref[span, :], q, preferred_element_type=jnp.float32)

                top = lax.fori_loop(
                    0,
                    chunks,
                    lambda j, top: jnp.maximum(top, jnp.max(scores(j), axis=0, keepdims=True)),
                    jnp.full((1, TILE), -3e38, jnp.float32),
                )

                def add(j, acc):
                    span = pl.ds(pl.multiple_of(j * CHUNK, CHUNK), CHUNK)
                    p = jnp.exp2((scores(j) - top) * factor).astype(jnp.bfloat16)
                    return acc + jnp.dot(vtall_ref[:, span], p, preferred_element_type=jnp.float32)

                acc_ref[0, :, at] = lax.fori_loop(
                    0, chunks, add, jnp.zeros((acc_ref.shape[1], TILE), jnp.float32)
                )
                return carry

            lax.fori_loop(0, ext // TILE, exact, 0)

        h_ref[halo : halo + pix, :] = state[slot]
        h_ref[:halo, :] = hide_up[slot]
        h_ref[halo + pix :, :] = hide_down[slot]
        col = px & (cols - 1)
        first, final = col == 0, col == cols - 1

        def spread(value, at, lane):
            size = value.shape[0]
            span = slice(lane, lane + channels)
            x_ref[at, span] = jnp.where(first[at], 0.0, pltpu.roll(value, 1, 0)).astype(jnp.bfloat16)
            span = slice(lane + 2 * channels, lane + 3 * channels)
            x_ref[at, span] = value.astype(jnp.bfloat16)
            span = slice(lane + 4 * channels, lane + 5 * channels)
            x_ref[at, span] = jnp.where(final[at], 0.0, pltpu.roll(value, size - 1, 0)).astype(jnp.bfloat16)

        wide = h_ref[...].astype(jnp.float32) * valid
        spread(wide, slice(0, ext), 0)
        weight = inside(lax.broadcasted_iota(jnp.int32, (1, ext), 1)) / acc_ref[0, channels : channels + 1, :]
        spread((acc_ref[0, :channels, :] * weight).T, slice(0, ext), channels)
        mid = ext - 2 * cols
        gates = None
        for r in range(3):
            part = jnp.dot(x_ref[r * cols : r * cols + mid, :], wg[r], preferred_element_type=jnp.float32)
            gates = part if r == 0 else gates + part
        inner = slice(cols, cols + mid)
        spread(jax.nn.sigmoid(gates[:, channels:]) * wide[inner], inner, 0)
        pair = jnp.dot(x_ref[cols : 2 * cols + pix, :], wc01[...], preferred_element_type=jnp.float32)
        cand = jnp.dot(x_ref[3 * cols : 3 * cols + pix, :], wc[2], preferred_element_type=jnp.float32)
        cand = cand + pair[:pix, :channels] + pair[cols : cols + pix, channels:]
        update = jax.nn.sigmoid(gates[cols : cols + pix, :channels])
        kept = wide[halo : halo + pix]
        fresh = ((1.0 - update) * kept + update * jnp.tanh(cand)).astype(jnp.bfloat16)
        fresh_ref[slot] = fresh
        head = lax.dot_general(wh[...], fresh, NT, preferred_element_type=jnp.float32)
        head_ref[pl.ds(pl.multiple_of(8 * slot, 8), 4), :] = head
        send(slot).start()
        return carry

    lax.fori_loop(0, info.live(), one, 0)
    bundle_body(
        slots, total_rows, cols, info, poses, rho_ref, head_ref, block_ref, pull_ref, pull_out, a_ref, w_ref, sems.at[slots]
    )
    for slot in range(slots):
        send(slot).wait()


VMEM = pl.BlockSpec(memory_space=pltpu.VMEM)
SMEM = pl.BlockSpec(memory_space=pltpu.SMEM)


def work(slots, ext, keys, channels):
    return pl.CostEstimate(
        flops=4 * slots * ext * keys * 2 * channels,
        bytes_accessed=slots * ext * (channels + 8) * 8,
        transcendentals=slots * ext * keys,
    )


def first_call(facts, slots, cols, queries, own, after):
    pix, channels = own.shape[1:]
    ext = pix + 4 * cols
    return pl.pallas_call(
        functools.partial(first_body, slots),
        in_specs=[SMEM] * 3 + [VMEM] * 5,
        out_specs=(VMEM, VMEM),
        scratch_shapes=[pltpu.VMEM((pix, channels), jnp.bfloat16), pltpu.VMEM((channels + 8, pix), jnp.bfloat16)],
        out_shape=(
            jax.ShapeDtypeStruct((slots, channels + 8, ext), jnp.float32),
            jax.ShapeDtypeStruct((slots, channels, ext), jnp.bfloat16),
        ),
        cost_estimate=work(slots, ext, pix, channels),
        compiler_params=pltpu.CompilerParams(vmem_limit_bytes=14 << 20),
        name="match_first",
    )(*facts, *queries, own, after)


def second_call(facts, qt, old, owns, nexts):
    slots, channels, ext = qt.shape
    keys = sum(part.shape[1] for part in owns)
    return pl.pallas_call(
        functools.partial(second_body, slots, len(owns)),
        in_specs=[SMEM] * 3 + [VMEM] * (2 + 2 * len(owns)),
        out_specs=VMEM,
        scratch_shapes=[pltpu.VMEM((keys, channels), jnp.bfloat16), pltpu.VMEM((channels + 8, keys), jnp.bfloat16)],
        out_shape=jax.ShapeDtypeStruct(old.shape, jnp.float32),
        cost_estimate=work(slots, ext, keys, channels),
        compiler_params=pltpu.CompilerParams(vmem_limit_bytes=14 << 20),
        name="match_second",
    )(*facts, qt, old, *owns, *nexts)


def fused_call(facts, qt, old, state, hide_up, hide_down, owns, nexts, last, weights, poses, inv_depth, total_rows, cols):
    slots, pix, channels = state.shape
    ext = qt.shape[2]
    keys = sum(part.shape[1] for part in owns)
    part_keys = sum(part.shape[1] for part in owns[len(owns) - last :])
    dims = (slots, total_rows, pix // cols, cols, last, len(owns))
    wide = channels + 8
    return pl.pallas_call(
        functools.partial(fused_body, dims),
        in_specs=[SMEM] * 3 + [VMEM] * (5 + 2 * len(owns) + len(weights) + 2),
        out_specs=(pl.BlockSpec(memory_space=pltpu.HBM), VMEM, pl.BlockSpec(memory_space=pltpu.HBM)),
        scratch_shapes=[
            pltpu.VMEM((slots, pix, channels), jnp.bfloat16),
            pltpu.VMEM((40, 2 * pix), jnp.float32),
            pltpu.VMEM((part_keys, channels), jnp.bfloat16),
            pltpu.VMEM((wide, part_keys), jnp.bfloat16),
            pltpu.VMEM((1, wide, ext), jnp.float32),
            pltpu.VMEM((keys, channels), jnp.bfloat16),
            pltpu.VMEM((wide, keys), jnp.bfloat16),
            pltpu.VMEM((ext, 6 * channels), jnp.bfloat16),
            pltpu.VMEM((ext, channels), jnp.bfloat16),
            pltpu.VMEM((8 * slots, pix), jnp.float32),
            pltpu.VMEM((8 * slots, 2 * pix), jnp.float32),
            pltpu.VMEM((8 * slots, 2 * pix), jnp.float32),
            pltpu.VMEM((weights[1].shape[1], 2 * channels), jnp.bfloat16),
            pltpu.SemaphoreType.DMA((slots + 1,)),
        ],
        out_shape=(
            jax.ShapeDtypeStruct((slots, pix, channels), jnp.bfloat16),
            jax.ShapeDtypeStruct((8, 128), jnp.float32),
            jax.ShapeDtypeStruct((40, 2 * pix), jnp.float32),
        ),
        compiler_params=pltpu.CompilerParams(vmem_limit_bytes=26 << 20),
        name="match_update",
    )(*facts, qt, old, state, hide_up, hide_down, *owns, *nexts, *weights, poses, inv_depth)


def shards(features, poses, inv_depth, hidden, edges, counts, w_gates, w_cand, w_head):
    slot_count, row_count, col_count, hid_width = hidden.shape
    channels = features.shape[3]
    node_rank = lax.axis_index(EDGE)
    pix_rank = lax.axis_index("x")
    total_rows = row_count * lax.axis_size("x")
    pix = row_count * col_count
    nodes = lax.axis_size(EDGE)
    halo = 2 * col_count
    facts = (edges.T, counts, jnp.stack([node_rank, pix_rank]).astype(jnp.int32))

    def following(value):
        return lax.ppermute(value, EDGE, [(i + 1, i) for i in range(nodes - 1)])

    own = features.reshape(2, pix, channels)
    state = hidden.reshape(slot_count, pix, hid_width)
    own1, own3, own2 = [swapped(own, "x", step) for step in (1, 3, 2)]
    next0 = following(own)
    next1, next3, next2 = following(own1), following(own3), following(own2)
    acc, turned_q = first_call(facts, slot_count, col_count, (own, own1, own3), own, next0)
    acc, late = lax.optimization_barrier((acc, state))
    rows_x = lax.axis_size("x")
    hide_up = lax.ppermute(late[:, pix - halo :], "x", [(i, i + 1) for i in range(rows_x - 1)])
    hide_down = lax.ppermute(late[:, :halo], "x", [(i + 1, i) for i in range(rows_x - 1)])
    acc = second_call(facts, turned_q, acc, (own1, own3), (next1, next3))
    wg = w_gates.reshape(3, -1, w_gates.shape[2])
    wc = w_cand.reshape(3, -1, w_cand.shape[2])
    fresh, block, pull = fused_call(
        facts,
        turned_q,
        acc,
        state,
        hide_up,
        hide_down,
        (own, own1, own3, own2),
        (next0, next1, next3, next2),
        1,
        (wg, wc, w_head),
        poses.T,
        inv_depth,
        total_rows,
        col_count,
    )
    gathered = gathered_blocks(block)
    pose_update, depth_update = solve_call(facts[2], gathered, pull)
    return (fresh.reshape(hidden.shape), pose_update, depth_update)


def solution(mesh):
    nodes, pix = mesh.devices.shape
    fine = Mesh(mesh.devices.reshape(nodes // 16, 8, 2, pix), EDGE + ("x",))
    placed = (
        P(EDGE, "x", None, None),
        P(),
        P(EDGE, "x"),
        P(EDGE, "x", None, None),
        P(EDGE, None),
        P(EDGE),
        P(),
        P(),
        P(),
    )
    return jax.shard_map(
        shards,
        mesh=fine,
        in_specs=placed,
        out_specs=(P(EDGE, "x", None, None), P(EDGE, None), P(EDGE, "x")),
        check_vma=False,
    )
```

```python
import functools
import math

import jax
import jax.numpy as jnp
from jax import lax
from jax.experimental import pallas as pl
from jax.experimental.pallas import tpu as pltpu
from jax.sharding import Mesh
from jax.sharding import PartitionSpec as P

PRECISE = lax.Precision.HIGHEST
POSE_DAMPING = 0.1
DEPTH_DAMPING = 0.1

EDGE = ("y", "z", "core")


def swapped(value, axis, step):
    count = lax.axis_size(axis)
    return lax.ppermute(value, axis, [(i, i ^ step) for i in range(count)])


def gathered_blocks(block):
    pair = block + swapped(block, "x", 1)
    block = pair + (swapped(block, "x", 2) + swapped(block, "x", 3))
    parts = jnp.stack([block, swapped(block, "core", 1)])
    parts = jnp.stack([parts] + [swapped(parts, "z", s) for s in (1, 2, 3)])
    parts = jnp.stack([parts, swapped(parts, "z", 4)])
    parts = jnp.stack([parts] + [swapped(parts, "y", s) for s in (1, 2, 3)])
    return parts.reshape((-1,) + block.shape)


class Facts:
    def __init__(self, edges, counts, ranks):
        self.edges, self.counts, self.ranks = edges, counts, ranks

    def source(self, slot):
        return self.edges[0, slot]

    def target(self, slot):
        return self.edges[1, slot]

    def live(self):
        return self.counts[0]

    def node(self):
        return self.ranks[0]

    def pix(self):
        return self.ranks[1]


def bundle_body(slots, rows_all, cols, info, poses, rho_ref, head, out, h_ref, h_out, a_ref, w_ref, sem):
    pix = rho_ref.shape[1]
    rows = pix // cols
    shift = cols.bit_length() - 1
    base = 2 * info.node()
    live = info.live()
    lane = lax.broadcasted_iota(jnp.int32, (1, pix), 1)
    col = (lane & (cols - 1)).astype(jnp.float32)
    row = ((lane >> shift) + info.pix() * rows).astype(jnp.float32)
    half = cols / 2.0
    u = (col - (cols - 1) / 2.0) / half
    v = (row - (rows_all - 1) / 2.0) / half
    sub = lax.broadcasted_iota(jnp.int32, (8, pix), 0)
    zero = jnp.zeros((8, pix), jnp.float32)
    lead_h = jnp.where(sub == 0, 1.0, jnp.where(sub == 2, -u, zero))
    rest_h = jnp.where(sub == 3, -u * v, jnp.where(sub == 4, 1.0 + u * u, jnp.where(sub == 5, -v, zero)))
    lead_v = jnp.where(sub == 1, 1.0, jnp.where(sub == 2, -v, zero))
    rest_v = jnp.where(sub == 3, -(1.0 + v * v), jnp.where(sub == 4, u * v, jnp.where(sub == 5, u, zero)))
    sub1 = lax.broadcasted_iota(jnp.int32, (8, 1), 0)
    frame = lax.broadcasted_iota(jnp.int32, (1, poses.shape[1]), 1)
    picks, sels = [], []
    for s in range(slots):
        src, tgt = info.source(s), info.target(s)
        a_loc, b_loc = src - base, tgt - base
        alive = jnp.where(s < live, 1.0, 0.0)
        picks.append([jnp.where(a_loc == f, 1.0, 0.0) for f in range(2)])
        sels.append([jnp.where(b_loc == g, 1.0, 0.0) - jnp.where(a_loc == g, 1.0, 0.0) for g in range(4)])
        pick_d = jnp.where(frame == tgt, 1.0, 0.0) - jnp.where(frame == src, 1.0, 0.0)
        d = jnp.sum(poses[...] * pick_d, axis=1, keepdims=True)
        d = jnp.concatenate([d, jnp.zeros((2, 1), jnp.float32)], axis=0)
        rho = rho_ref[pl.ds(a_loc, 1), :]
        conf_h = jax.nn.sigmoid(head[8 * s + 2 : 8 * s + 3, :]) * alive
        conf_v = jax.nn.sigmoid(head[8 * s + 3 : 8 * s + 4, :]) * alive
        a_h = rho * lead_h + rest_h
        a_v = rho * lead_v + rest_v
        e_h = head[8 * s : 8 * s + 1, :] - jnp.sum(a_h * d, axis=0, keepdims=True)
        e_v = head[8 * s + 1 : 8 * s + 2, :] - jnp.sum(a_v * d, axis=0, keepdims=True)
        k_h = jnp.sum(lead_h * d, axis=0, keepdims=True)
        k_v = jnp.sum(lead_v * d, axis=0, keepdims=True)
        a_h = jnp.where(sub == 6, e_h, a_h)
        a_v = jnp.where(sub == 6, e_v, a_v)
        w_h = conf_h * a_h
        w_v = conf_v * a_v
        at = slice(8 * s, 8 * s + 8)
        a_ref[at, :pix] = a_h
        a_ref[at, pix:] = a_v
        w_ref[at, :pix] = w_h
        w_ref[at, pix:] = w_v
        k_s = w_h * k_h + w_v * k_v
        dd = conf_h * k_h * k_h + conf_v * k_v * k_v
        for f in range(2):
            pick = picks[s][f]
            at = slice(f * pix, (f + 1) * pix)
            old = h_ref[32:33, at] if s else jnp.full((1, pix), DEPTH_DAMPING, jnp.float32)
            h_ref[32:33, at] = old + pick * dd
            for g in range(4):
                term = jnp.where(sub1 == 6, pick, pick * sels[s][g]) * k_s
                at = (slice(8 * g, 8 * g + 8), slice(f * pix, (f + 1) * pix))
                h_ref[at] = h_ref[at] + term if s else term
    copy = pltpu.make_async_copy(h_ref, h_out, sem)
    copy.start()
    nt = (((1,), (1,)), ((), ()))
    gram = lax.dot_general(w_ref[...], a_ref[...], nt, precision=PRECISE, preferred_element_type=jnp.float32)
    for f in range(2):
        at = slice(f * pix, (f + 1) * pix)
        w_ref[:, at] = h_ref[:32, at] * (1.0 / h_ref[32:33, at])
    schur = lax.dot_general(w_ref[...], h_ref[:32, :], nt, precision=PRECISE, preferred_element_type=jnp.float32)
    pad = jnp.zeros((32, 96), jnp.float32)
    gram = jnp.concatenate([gram, pad], axis=1)
    schur = jnp.concatenate([schur, pad], axis=1)
    lanes = lax.broadcasted_iota(jnp.int32, (8, 128), 1)
    group, inner = lanes >> 3, lanes & 7
    terms = []
    for s in range(slots):
        y = jnp.where(group == s, gram[8 * s : 8 * s + 8, :], 0.0)
        y = pltpu.roll(y, 128 - 8 * s, 1) if s else y
        y = y + pltpu.roll(y, 8, 1)
        y = y + pltpu.roll(y, 16, 1)
        coef = jnp.zeros((8, 128), jnp.float32)
        for g in range(4):
            coef = jnp.where(group == g, sels[s][g], coef)
        terms.append(y * jnp.where(inner == 6, 1.0, coef))
    total = None
    for g in range(4):
        part = -schur[8 * g : 8 * g + 8, :]
        for s in range(slots):
            part = part + sels[s][g] * terms[s]
        part = jnp.where(lanes < 32, part, 0.0)
        total = part if g == 0 else total + pltpu.roll(part, 32 * g, 1)
    out[...] = total
    copy.wait()


REAL = (0, 1, 2, 3, 4, 5, 8, 9, 10, 11, 12, 13)


def down(x, width=16):
    return jnp.broadcast_to(x, (width, 128))


def eliminate(diag, sides):
    diag, sides = list(diag), [list(side) for side in sides]
    count = len(REAL)
    for k in range(count):
        at = slice(REAL[k], REAL[k] + 1)
        scale = down(1.0 / diag[k][at, :])
        diag[k] = diag[k] * scale
        for side in sides:
            side[k] = side[k] * scale
        for i in range(count):
            if i != k:
                f = down(diag[i][at, :])
                diag[i] = diag[i] - f * diag[k]
                for side in sides:
                    side[i] = side[i] - f * side[k]
    return diag, sides


def solve_body(nodes, pix, info, g_ref, h_ref, pose_ref, depth_ref, t_ref, d_ref, l_ref, u_ref, near):
    count = len(REAL)
    lane = lax.broadcasted_iota(jnp.int32, (16, 128), 1)
    sub = lax.broadcasted_iota(jnp.int32, (16, 128), 0)
    me = info[0]
    for n in range(nodes):
        t_ref[n] = g_ref[n ^ me]
    rest = jnp.zeros((128 - nodes, 128), jnp.float32)
    for k in range(6):
        t = jnp.concatenate([t_ref[:, k, :], rest], axis=0).T
        for f in range(2):
            i = 6 * f + k
            far = jnp.where(lane < nodes, pltpu.roll(t[32 * f + 80 : 32 * f + 96], 1, 1), 0.0)
            d_ref[i] = t[32 * f : 32 * f + 16] + far + jnp.where(sub == REAL[i], POSE_DAMPING, 0.0)
            u_ref[i] = jnp.where(lane < nodes - 1, t[32 * f + 16 : 32 * f + 32], 0.0)
            l_ref[i] = jnp.where(lane < nodes, pltpu.roll(t[32 * f + 64 : 32 * f + 80], 1, 1), 0.0)

    def level(step, carry):
        s = jnp.left_shift(1, step)
        diag, (low, up) = eliminate(
            [d_ref[i] for i in range(count)], [[l_ref[i] for i in range(count)], [u_ref[i] for i in range(count)]]
        )
        for k in range(count):
            low_r = jnp.where(sub == 6, diag[k], low[k])
            up_r = jnp.where(sub == 6, diag[k], up[k])
            near[0, k] = pltpu.roll(up_r, s, 1)
            near[1, k] = pltpu.roll(low[k], s, 1)
            near[2, k] = pltpu.roll(low_r, 128 - s, 1)
            near[3, k] = pltpu.roll(up[k], 128 - s, 1)
        for i in range(count):
            d_new = d_ref[i]
            l_old, u_old = l_ref[i], u_ref[i]
            l_new = jnp.zeros((16, 128), jnp.float32)
            u_new = jnp.zeros((16, 128), jnp.float32)
            for k in range(count):
                at = slice(REAL[k], REAL[k] + 1)
                fl, fu = down(l_old[at, :]), down(u_old[at, :])
                d_new = d_new - fl * near[0, k] - fu * near[2, k]
                l_new = l_new - fl * near[1, k]
                u_new = u_new - fu * near[3, k]
            d_ref[i] = d_new
            l_ref[i] = l_new
            u_ref[i] = u_new
        return carry

    levels = max(1, (nodes - 1).bit_length())
    lax.fori_loop(0, levels, level, 0)
    diag, _ = eliminate([d_ref[i] for i in range(count)], [])
    x = jnp.zeros((16, 128), jnp.float32)
    for i in range(count):
        x = jnp.where(sub == REAL[i], down(diag[i][6:7, :]), x)
    own = jnp.sum(jnp.where(lane == me, x, 0.0), axis=1, keepdims=True)
    after = jnp.sum(jnp.where((lane == me + 1) & (lane < nodes), x, 0.0), axis=1, keepdims=True)
    spread = jnp.where((sub & 7) == lane, jnp.broadcast_to(own, (16, 128)), 0.0)
    for f in range(2):
        pose_ref[f : f + 1, :] = jnp.sum(spread[8 * f : 8 * f + 8], axis=0, keepdims=True)[:, :6]
    column = jnp.concatenate([own, after], axis=0)
    column = jnp.where(lax.broadcasted_iota(jnp.int32, (32, 1), 0) == 6, -1.0, column)
    for f in range(2):
        at = slice(f * pix, (f + 1) * pix)
        depth_ref[f : f + 1, :] = -jnp.sum(h_ref[:32, at] * column, axis=0, keepdims=True) / h_ref[32:33, at]


def solve_call(me, gathered, h):
    nodes = gathered.shape[0]
    pix = h.shape[1] // 2
    vmem = pl.BlockSpec(memory_space=pltpu.VMEM)
    return pl.pallas_call(
        functools.partial(solve_body, nodes, pix),
        out_shape=(
            jax.ShapeDtypeStruct((2, 6), jnp.float32),
            jax.ShapeDtypeStruct((2, pix), jnp.float32),
        ),
        in_specs=[pl.BlockSpec(memory_space=pltpu.SMEM), vmem, vmem],
        out_specs=(vmem, vmem),
        scratch_shapes=[
            pltpu.VMEM((nodes, 8, 128), jnp.float32),
            pltpu.VMEM((12, 16, 128), jnp.float32),
            pltpu.VMEM((12, 16, 128), jnp.float32),
            pltpu.VMEM((12, 16, 128), jnp.float32),
            pltpu.VMEM((4, 12, 16, 128), jnp.float32),
        ],
        compiler_params=pltpu.CompilerParams(vmem_limit_bytes=12 << 20),
        name="pose_solve",
    )(me, gathered, h)


NT = (((1,), (1,)), ((), ()))
TILE = 256
CHUNK = 768


def spots(info, slots, pix, halo):
    odd = (info.pix() & 1) == 1
    at1 = pl.multiple_of(jnp.where(odd, 0, halo + pix), halo)
    at3 = pl.multiple_of(jnp.where(odd, halo + pix, 0), halo)
    return at1, at3


def turned(value):
    return value.astype(jnp.float32).T.astype(jnp.bfloat16)


def load_keys(target, owns, nexts, k_ref, vt_ref):
    channels = k_ref.shape[1]

    @pl.when(target < 2)
    def _():
        base = 0
        for part in owns:
            k_ref[base : base + part.shape[1], :] = part[target]
            base += part.shape[1]

    @pl.when(target >= 2)
    def _():
        base = 0
        for part in nexts:
            k_ref[base : base + part.shape[1], :] = part[target - 2]
            base += part.shape[1]

    vt_ref[:channels, :] = turned(k_ref[...])
    vt_ref[channels:, :] = jnp.ones((vt_ref.shape[0] - channels, vt_ref.shape[1]), jnp.bfloat16)


def add_keys(slot, k_ref, vt_ref, qt_ref, old, factor, put):
    chunks = k_ref.shape[0] // CHUNK
    spots_t = [slice(t * TILE, (t + 1) * TILE) for t in range(qt_ref.shape[2] // TILE)]

    def scores(j):
        keys = k_ref[j * CHUNK : (j + 1) * CHUNK, :]
        return [jnp.dot(keys, qt_ref[slot, :, at], preferred_element_type=jnp.float32) for at in spots_t]

    held = scores(0)
    sums = [None if old is None else old[slot, :, at] for at in spots_t]
    for j in range(chunks):
        later = scores(j + 1) if j + 1 < chunks else None
        for t in range(len(spots_t)):
            p = jnp.exp2(held[t] * factor).astype(jnp.bfloat16)
            part = jnp.dot(vt_ref[:, j * CHUNK : (j + 1) * CHUNK], p, preferred_element_type=jnp.float32)
            sums[t] = part if sums[t] is None else sums[t] + part
        held = later
    for at, value in zip(spots_t, sums):
        put(at, value)


def load_queries(info, slots, slot, own_q, side1, side3, qt_ref):
    pix, halo = own_q.shape[1], qt_ref.shape[2] - own_q.shape[1]
    halo = halo // 2
    at1, at3 = spots(info, slots, pix, halo)
    odd = (info.pix() & 1) == 1
    from1 = pl.multiple_of(jnp.where(odd, pix - halo, 0), halo)
    from3 = pl.multiple_of(jnp.where(odd, 0, pix - halo), halo)
    src = info.source(slot) - 2 * info.node()
    qt_ref[slot, :, halo : halo + pix] = turned(own_q[src])
    qt_ref[slot, :, pl.ds(at1, halo)] = turned(side1[src, pl.ds(from1, halo), :])
    qt_ref[slot, :, pl.ds(at3, halo)] = turned(side3[src, pl.ds(from3, halo), :])


def match_factor(channels):
    return 2.0 / math.sqrt(channels) * math.log2(math.e)


def first_body(slots, edges, counts, ranks, own_q, side1, side3, own, after, acc_ref, qt_ref, k_ref, vt_ref):
    info = Facts(edges, counts, ranks)

    def one(slot, carry):
        target = info.target(slot) - 2 * info.node()
        load_queries(info, slots, slot, own_q, side1, side3, qt_ref)
        load_keys(target, (own,), (after,), k_ref, vt_ref)


        def put(at, value):
            acc_ref[slot, :, at] = value

        add_keys(slot, k_ref, vt_ref, qt_ref, None, match_factor(k_ref.shape[1]), put)
        return carry

    lax.fori_loop(0, info.live(), one, 0)


def second_body(slots, parts, edges, counts, ranks, qt_ref, old, *refs):
    info = Facts(edges, counts, ranks)
    owns, nexts = refs[:parts], refs[parts : 2 * parts]
    acc_ref, k_ref, vt_ref = refs[2 * parts :]

    def one(slot, carry):
        target = info.target(slot) - 2 * info.node()
        load_keys(target, owns, nexts, k_ref, vt_ref)


        def put(at, value):
            acc_ref[slot, :, at] = value

        add_keys(slot, k_ref, vt_ref, qt_ref, old, match_factor(k_ref.shape[1]), put)
        return carry

    lax.fori_loop(0, info.live(), one, 0)


def fused_body(dims, edges, counts, ranks, *refs):
    info = Facts(edges, counts, ranks)
    slots, total_rows, rows, cols, last, parts = dims
    (qt_ref, old), refs = refs[:2], refs[2:]
    (state, hide_up, hide_down), refs = refs[:3], refs[3:]
    owns, refs = refs[:parts], refs[parts:]
    nexts, refs = refs[:parts], refs[parts:]
    (wg, wc, wh, poses, rho_ref), refs = refs[:5], refs[5:]
    (fresh_out, block_ref, pull_out), refs = refs[:3], refs[3:]
    fresh_ref, pull_ref, k_ref, vt_ref, acc_ref, kall_ref, vtall_ref, x_ref, h_ref = refs[:9]
    head_ref, a_ref, w_ref, wc01, sems = refs[9:]
    pix_rank = info.pix()
    pix = rows * cols
    halo = 2 * cols
    ext = pix + 2 * halo
    channels = state.shape[-1]
    factor = match_factor(channels)
    px = lax.broadcasted_iota(jnp.int32, (ext, 1), 0)

    def inside(px):
        grow = (px >> (cols.bit_length() - 1)) - 2 + rows * pix_rank
        return jnp.where((grow >= 0) & (grow < total_rows), 1.0, 0.0)

    valid = inside(px)
    wc01[:, :channels] = wc[0]
    wc01[:, channels:] = wc[1]

    def send(slot):
        return pltpu.make_async_copy(fresh_ref.at[slot], fresh_out.at[slot], sems.at[slot])

    def keep(slot, carry):
        fresh_ref[slot] = state[slot]
        head_ref[pl.ds(pl.multiple_of(8 * slot, 8), 8), :] = jnp.zeros((8, pix), jnp.float32)
        send(slot).start()
        return carry

    lax.fori_loop(info.live(), slots, keep, 0)

    def one(slot, carry):
        target = info.target(slot) - 2 * info.node()
        load_keys(target, owns[parts - last :], nexts[parts - last :], k_ref, vt_ref)

        def put(at, value):
            acc_ref[0, :, at] = value

        add_keys(slot, k_ref, vt_ref, qt_ref, old, factor, put)
        sums = acc_ref[0, channels : channels + 1, :]
        fits = (jnp.min(sums) > 1e-20) & (jnp.max(sums) < 1e25)

        @pl.when(jnp.logical_not(fits))
        def _():
            load_keys(target, owns, nexts, kall_ref, vtall_ref)
            chunks = kall_ref.shape[0] // CHUNK

            def exact(t, carry):
                at = pl.ds(pl.multiple_of(t * TILE, TILE), TILE)
                q = qt_ref[slot, :, at]

                def scores(j):
                    span = pl.ds(pl.multiple_of(j * CHUNK, CHUNK), CHUNK)
                    return jnp.dot(kall_ref[span, :], q, preferred_element_type=jnp.float32)

                top = lax.fori_loop(
                    0,
                    chunks,
                    lambda j, top: jnp.maximum(top, jnp.max(scores(j), axis=0, keepdims=True)),
                    jnp.full((1, TILE), -3e38, jnp.float32),
                )

                def add(j, acc):
                    span = pl.ds(pl.multiple_of(j * CHUNK, CHUNK), CHUNK)
                    p = jnp.exp2((scores(j) - top) * factor).astype(jnp.bfloat16)
                    return acc + jnp.dot(vtall_ref[:, span], p, preferred_element_type=jnp.float32)

                acc_ref[0, :, at] = lax.fori_loop(
                    0, chunks, add, jnp.zeros((acc_ref.shape[1], TILE), jnp.float32)
                )
                return carry

            lax.fori_loop(0, ext // TILE, exact, 0)

        h_ref[halo : halo + pix, :] = state[slot]
        h_ref[:halo, :] = hide_up[slot]
        h_ref[halo + pix :, :] = hide_down[slot]
        col = px & (cols - 1)
        first, final = col == 0, col == cols - 1

        def spread(value, at, lane):
            size = value.shape[0]
            span = slice(lane, lane + channels)
            x_ref[at, span] = jnp.where(first[at], 0.0, pltpu.roll(value, 1, 0)).astype(jnp.bfloat16)
            span = slice(lane + 2 * channels, lane + 3 * channels)
            x_ref[at, span] = value.astype(jnp.bfloat16)
            span = slice(lane + 4 * channels, lane + 5 * channels)
            x_ref[at, span] = jnp.where(final[at], 0.0, pltpu.roll(value, size - 1, 0)).astype(jnp.bfloat16)

        wide = h_ref[...].astype(jnp.float32) * valid
        spread(wide, slice(0, ext), 0)
        weight = inside(lax.broadcasted_iota(jnp.int32, (1, ext), 1)) / acc_ref[0, channels : channels + 1, :]
        spread((acc_ref[0, :channels, :] * weight).T, slice(0, ext), channels)
        mid = ext - 2 * cols
        gates = None
        for r in range(3):
            part = jnp.dot(x_ref[r * cols : r * cols + mid, :], wg[r], preferred_element_type=jnp.float32)
            gates = part if r == 0 else gates + part
        inner = slice(cols, cols + mid)
        spread(jax.nn.sigmoid(gates[:, channels:]) * wide[inner], inner, 0)
        pair = jnp.dot(x_ref[cols : 2 * cols + pix, :], wc01[...], preferred_element_type=jnp.float32)
        cand = jnp.dot(x_ref[3 * cols : 3 * cols + pix, :], wc[2], preferred_element_type=jnp.float32)
        cand = cand + pair[:pix, :channels] + pair[cols : cols + pix, channels:]
        update = jax.nn.sigmoid(gates[cols : cols + pix, :channels])
        kept = wide[halo : halo + pix]
        fresh = ((1.0 - update) * kept + update * jnp.tanh(cand)).astype(jnp.bfloat16)
        fresh_ref[slot] = fresh
        head = lax.dot_general(wh[...], fresh, NT, preferred_element_type=jnp.float32)
        head_ref[pl.ds(pl.multiple_of(8 * slot, 8), 4), :] = head
        send(slot).start()
        return carry

    lax.fori_loop(0, info.live(), one, 0)
    bundle_body(
        slots, total_rows, cols, info, poses, rho_ref, head_ref, block_ref, pull_ref, pull_out, a_ref, w_ref, sems.at[slots]
    )
    for slot in range(slots):
        send(slot).wait()


VMEM = pl.BlockSpec(memory_space=pltpu.VMEM)
SMEM = pl.BlockSpec(memory_space=pltpu.SMEM)


def work(slots, ext, keys, channels):
    return pl.CostEstimate(
        flops=4 * slots * ext * keys * 2 * channels,
        bytes_accessed=slots * ext * (channels + 8) * 8,
        transcendentals=slots * ext * keys,
    )


def first_call(facts, slots, cols, queries, own, after):
    pix, channels = own.shape[1:]
    ext = pix + 4 * cols
    return pl.pallas_call(
        functools.partial(first_body, slots),
        in_specs=[SMEM] * 3 + [VMEM] * 5,
        out_specs=(VMEM, VMEM),
        scratch_shapes=[pltpu.VMEM((pix, channels), jnp.bfloat16), pltpu.VMEM((channels + 8, pix), jnp.bfloat16)],
        out_shape=(
            jax.ShapeDtypeStruct((slots, channels + 8, ext), jnp.float32),
            jax.ShapeDtypeStruct((slots, channels, ext), jnp.bfloat16),
        ),
        cost_estimate=work(slots, ext, pix, channels),
        compiler_params=pltpu.CompilerParams(vmem_limit_bytes=14 << 20),
        name="match_first",
    )(*facts, *queries, own, after)


def second_call(facts, qt, old, owns, nexts):
    slots, channels, ext = qt.shape
    keys = sum(part.shape[1] for part in owns)
    return pl.pallas_call(
        functools.partial(second_body, slots, len(owns)),
        in_specs=[SMEM] * 3 + [VMEM] * (2 + 2 * len(owns)),
        out_specs=VMEM,
        scratch_shapes=[pltpu.VMEM((keys, channels), jnp.bfloat16), pltpu.VMEM((channels + 8, keys), jnp.bfloat16)],
        out_shape=jax.ShapeDtypeStruct(old.shape, jnp.float32),
        cost_estimate=work(slots, ext, keys, channels),
        compiler_params=pltpu.CompilerParams(vmem_limit_bytes=14 << 20),
        name="match_second",
    )(*facts, qt, old, *owns, *nexts)


def fused_call(facts, qt, old, state, hide_up, hide_down, owns, nexts, last, weights, poses, inv_depth, total_rows, cols):
    slots, pix, channels = state.shape
    ext = qt.shape[2]
    keys = sum(part.shape[1] for part in owns)
    part_keys = sum(part.shape[1] for part in owns[len(owns) - last :])
    dims = (slots, total_rows, pix // cols, cols, last, len(owns))
    wide = channels + 8
    return pl.pallas_call(
        functools.partial(fused_body, dims),
        in_specs=[SMEM] * 3 + [VMEM] * (5 + 2 * len(owns) + len(weights) + 2),
        out_specs=(pl.BlockSpec(memory_space=pltpu.HBM), VMEM, pl.BlockSpec(memory_space=pltpu.HBM)),
        scratch_shapes=[
            pltpu.VMEM((slots, pix, channels), jnp.bfloat16),
            pltpu.VMEM((40, 2 * pix), jnp.float32),
            pltpu.VMEM((part_keys, channels), jnp.bfloat16),
            pltpu.VMEM((wide, part_keys), jnp.bfloat16),
            pltpu.VMEM((1, wide, ext), jnp.float32),
            pltpu.VMEM((keys, channels), jnp.bfloat16),
            pltpu.VMEM((wide, keys), jnp.bfloat16),
            pltpu.VMEM((ext, 6 * channels), jnp.bfloat16),
            pltpu.VMEM((ext, channels), jnp.bfloat16),
            pltpu.VMEM((8 * slots, pix), jnp.float32),
            pltpu.VMEM((8 * slots, 2 * pix), jnp.float32),
            pltpu.VMEM((8 * slots, 2 * pix), jnp.float32),
            pltpu.VMEM((weights[1].shape[1], 2 * channels), jnp.bfloat16),
            pltpu.SemaphoreType.DMA((slots + 1,)),
        ],
        out_shape=(
            jax.ShapeDtypeStruct((slots, pix, channels), jnp.bfloat16),
            jax.ShapeDtypeStruct((8, 128), jnp.float32),
            jax.ShapeDtypeStruct((40, 2 * pix), jnp.float32),
        ),
        compiler_params=pltpu.CompilerParams(vmem_limit_bytes=26 << 20),
        name="match_update",
    )(*facts, qt, old, state, hide_up, hide_down, *owns, *nexts, *weights, poses, inv_depth)


def shards(features, poses, inv_depth, hidden, edges, counts, w_gates, w_cand, w_head):
    slot_count, row_count, col_count, hid_width = hidden.shape
    channels = features.shape[3]
    node_rank = lax.axis_index(EDGE)
    pix_rank = lax.axis_index("x")
    total_rows = row_count * lax.axis_size("x")
    pix = row_count * col_count
    nodes = lax.axis_size(EDGE)
    halo = 2 * col_count
    facts = (edges.T, counts, jnp.stack([node_rank, pix_rank]).astype(jnp.int32))

    def following(value):
        return lax.ppermute(value, EDGE, [(i + 1, i) for i in range(nodes - 1)])

    own = features.reshape(2, pix, channels)
    state = hidden.reshape(slot_count, pix, hid_width)
    own1, own3 = swapped(own, "x", 1), swapped(own, "x", 3)
    next0 = following(own)
    next1, next3 = following(own1), following(own3)
    half = pix // 2
    own2a, own2b = swapped(own1[:, :half], "x", 3), swapped(own3[:, half:], "x", 1)
    next2a, next2b = following(own2a), following(own2b)
    acc, turned_q = first_call(facts, slot_count, col_count, (own, own1, own3), own, next0)
    acc, late = lax.optimization_barrier((acc, state))
    rows_x = lax.axis_size("x")
    hide_up = lax.ppermute(late[:, pix - halo :], "x", [(i, i + 1) for i in range(rows_x - 1)])
    hide_down = lax.ppermute(late[:, :halo], "x", [(i + 1, i) for i in range(rows_x - 1)])
    acc = second_call(facts, turned_q, acc, (own1, own3), (next1, next3))
    wg = w_gates.reshape(3, -1, w_gates.shape[2])
    wc = w_cand.reshape(3, -1, w_cand.shape[2])
    fresh, block, pull = fused_call(
        facts,
        turned_q,
        acc,
        state,
        hide_up,
        hide_down,
        (own, own1, own3, own2a, own2b),
        (next0, next1, next3, next2a, next2b),
        2,
        (wg, wc, w_head),
        poses.T,
        inv_depth,
        total_rows,
        col_count,
    )
    gathered = gathered_blocks(block)
    pose_update, depth_update = solve_call(facts[2], gathered, pull)
    return (fresh.reshape(hidden.shape), pose_update, depth_update)


def solution(mesh):
    nodes, pix = mesh.devices.shape
    fine = Mesh(mesh.devices.reshape(nodes // 16, 8, 2, pix), EDGE + ("x",))
    placed = (
        P(EDGE, "x", None, None),
        P(),
        P(EDGE, "x"),
        P(EDGE, "x", None, None),
        P(EDGE, None),
        P(EDGE),
        P(),
        P(),
        P(),
    )
    return jax.shard_map(
        shards,
        mesh=fine,
        in_specs=placed,
        out_specs=(P(EDGE, "x", None, None), P(EDGE, None), P(EDGE, "x")),
        check_vma=False,
    )
```

```python
import functools
import math

import jax
import jax.numpy as jnp
from jax import lax
from jax.experimental import pallas as pl
from jax.experimental.pallas import tpu as pltpu
from jax.sharding import Mesh
from jax.sharding import PartitionSpec as P

PRECISE = lax.Precision.HIGHEST
POSE_DAMPING = 0.1
DEPTH_DAMPING = 0.1

EDGE = ("y", "z", "core")


def swapped(value, axis, step):
    count = lax.axis_size(axis)
    return lax.ppermute(value, axis, [(i, i ^ step) for i in range(count)])


def gathered_blocks(block):
    pair = block + swapped(block, "x", 1)
    block = pair + (swapped(block, "x", 2) + swapped(block, "x", 3))
    parts = jnp.stack([block, swapped(block, "core", 1)])
    parts = jnp.stack([parts] + [swapped(parts, "z", s) for s in (1, 2, 3)])
    parts = jnp.stack([parts, swapped(parts, "z", 4)])
    parts = jnp.stack([parts] + [swapped(parts, "y", s) for s in (1, 2, 3)])
    return parts.reshape((-1,) + block.shape)


class Facts:
    def __init__(self, edges, counts, ranks):
        self.edges, self.counts, self.ranks = edges, counts, ranks

    def source(self, slot):
        return self.edges[0, slot]

    def target(self, slot):
        return self.edges[1, slot]

    def live(self):
        return self.counts[0]

    def node(self):
        return self.ranks[0]

    def pix(self):
        return self.ranks[1]


def bundle_body(slots, rows_all, cols, info, poses, rho_ref, head, out, h_ref, h_out, a_ref, w_ref, sem):
    pix = rho_ref.shape[1]
    rows = pix // cols
    shift = cols.bit_length() - 1
    base = 2 * info.node()
    live = info.live()
    lane = lax.broadcasted_iota(jnp.int32, (1, pix), 1)
    col = (lane & (cols - 1)).astype(jnp.float32)
    row = ((lane >> shift) + info.pix() * rows).astype(jnp.float32)
    half = cols / 2.0
    u = (col - (cols - 1) / 2.0) / half
    v = (row - (rows_all - 1) / 2.0) / half
    sub = lax.broadcasted_iota(jnp.int32, (8, pix), 0)
    zero = jnp.zeros((8, pix), jnp.float32)
    lead_h = jnp.where(sub == 0, 1.0, jnp.where(sub == 2, -u, zero))
    rest_h = jnp.where(sub == 3, -u * v, jnp.where(sub == 4, 1.0 + u * u, jnp.where(sub == 5, -v, zero)))
    lead_v = jnp.where(sub == 1, 1.0, jnp.where(sub == 2, -v, zero))
    rest_v = jnp.where(sub == 3, -(1.0 + v * v), jnp.where(sub == 4, u * v, jnp.where(sub == 5, u, zero)))
    sub1 = lax.broadcasted_iota(jnp.int32, (8, 1), 0)
    frame = lax.broadcasted_iota(jnp.int32, (1, poses.shape[1]), 1)
    picks, sels = [], []
    for s in range(slots):
        src, tgt = info.source(s), info.target(s)
        a_loc, b_loc = src - base, tgt - base
        alive = jnp.where(s < live, 1.0, 0.0)
        picks.append([jnp.where(a_loc == f, 1.0, 0.0) for f in range(2)])
        sels.append([jnp.where(b_loc == g, 1.0, 0.0) - jnp.where(a_loc == g, 1.0, 0.0) for g in range(4)])
        pick_d = jnp.where(frame == tgt, 1.0, 0.0) - jnp.where(frame == src, 1.0, 0.0)
        d = jnp.sum(poses[...] * pick_d, axis=1, keepdims=True)
        d = jnp.concatenate([d, jnp.zeros((2, 1), jnp.float32)], axis=0)
        rho = rho_ref[pl.ds(a_loc, 1), :]
        conf_h = jax.nn.sigmoid(head[8 * s + 2 : 8 * s + 3, :]) * alive
        conf_v = jax.nn.sigmoid(head[8 * s + 3 : 8 * s + 4, :]) * alive
        a_h = rho * lead_h + rest_h
        a_v = rho * lead_v + rest_v
        e_h = head[8 * s : 8 * s + 1, :] - jnp.sum(a_h * d, axis=0, keepdims=True)
        e_v = head[8 * s + 1 : 8 * s + 2, :] - jnp.sum(a_v * d, axis=0, keepdims=True)
        k_h = jnp.sum(lead_h * d, axis=0, keepdims=True)
        k_v = jnp.sum(lead_v * d, axis=0, keepdims=True)
        a_h = jnp.where(sub == 6, e_h, a_h)
        a_v = jnp.where(sub == 6, e_v, a_v)
        w_h = conf_h * a_h
        w_v = conf_v * a_v
        at = slice(8 * s, 8 * s + 8)
        a_ref[at, :pix] = a_h
        a_ref[at, pix:] = a_v
        w_ref[at, :pix] = w_h
        w_ref[at, pix:] = w_v
        k_s = w_h * k_h + w_v * k_v
        dd = conf_h * k_h * k_h + conf_v * k_v * k_v
        for f in range(2):
            pick = picks[s][f]
            at = slice(f * pix, (f + 1) * pix)
            old = h_ref[32:33, at] if s else jnp.full((1, pix), DEPTH_DAMPING, jnp.float32)
            h_ref[32:33, at] = old + pick * dd
            for g in range(4):
                term = jnp.where(sub1 == 6, pick, pick * sels[s][g]) * k_s
                at = (slice(8 * g, 8 * g + 8), slice(f * pix, (f + 1) * pix))
                h_ref[at] = h_ref[at] + term if s else term
    copy = pltpu.make_async_copy(h_ref, h_out, sem)
    copy.start()
    nt = (((1,), (1,)), ((), ()))
    gram = lax.dot_general(w_ref[...], a_ref[...], nt, precision=PRECISE, preferred_element_type=jnp.float32)
    for f in range(2):
        at = slice(f * pix, (f + 1) * pix)
        w_ref[:, at] = h_ref[:32, at] * (1.0 / h_ref[32:33, at])
    schur = lax.dot_general(w_ref[...], h_ref[:32, :], nt, precision=PRECISE, preferred_element_type=jnp.float32)
    pad = jnp.zeros((32, 96), jnp.float32)
    gram = jnp.concatenate([gram, pad], axis=1)
    schur = jnp.concatenate([schur, pad], axis=1)
    lanes = lax.broadcasted_iota(jnp.int32, (8, 128), 1)
    group, inner = lanes >> 3, lanes & 7
    terms = []
    for s in range(slots):
        y = jnp.where(group == s, gram[8 * s : 8 * s + 8, :], 0.0)
        y = pltpu.roll(y, 128 - 8 * s, 1) if s else y
        y = y + pltpu.roll(y, 8, 1)
        y = y + pltpu.roll(y, 16, 1)
        coef = jnp.zeros((8, 128), jnp.float32)
        for g in range(4):
            coef = jnp.where(group == g, sels[s][g], coef)
        terms.append(y * jnp.where(inner == 6, 1.0, coef))
    total = None
    for g in range(4):
        part = -schur[8 * g : 8 * g + 8, :]
        for s in range(slots):
            part = part + sels[s][g] * terms[s]
        part = jnp.where(lanes < 32, part, 0.0)
        total = part if g == 0 else total + pltpu.roll(part, 32 * g, 1)
    out[...] = total
    copy.wait()


REAL = (0, 1, 2, 3, 4, 5, 8, 9, 10, 11, 12, 13)


def down(x, width=16):
    return jnp.broadcast_to(x, (width, 128))


def eliminate(diag, sides):
    diag, sides = list(diag), [list(side) for side in sides]
    count = len(REAL)
    for k in range(count):
        at = slice(REAL[k], REAL[k] + 1)
        scale = down(1.0 / diag[k][at, :])
        diag[k] = diag[k] * scale
        for side in sides:
            side[k] = side[k] * scale
        for i in range(count):
            if i != k:
                f = down(diag[i][at, :])
                diag[i] = diag[i] - f * diag[k]
                for side in sides:
                    side[i] = side[i] - f * side[k]
    return diag, sides


def solve_body(nodes, pix, info, g_ref, h_ref, pose_ref, depth_ref, t_ref, d_ref, l_ref, u_ref, near):
    count = len(REAL)
    lane = lax.broadcasted_iota(jnp.int32, (16, 128), 1)
    sub = lax.broadcasted_iota(jnp.int32, (16, 128), 0)
    me = info[0]
    for n in range(nodes):
        t_ref[n] = g_ref[n ^ me]
    rest = jnp.zeros((128 - nodes, 128), jnp.float32)
    for k in range(6):
        t = jnp.concatenate([t_ref[:, k, :], rest], axis=0).T
        for f in range(2):
            i = 6 * f + k
            far = jnp.where(lane < nodes, pltpu.roll(t[32 * f + 80 : 32 * f + 96], 1, 1), 0.0)
            d_ref[i] = t[32 * f : 32 * f + 16] + far + jnp.where(sub == REAL[i], POSE_DAMPING, 0.0)
            u_ref[i] = jnp.where(lane < nodes - 1, t[32 * f + 16 : 32 * f + 32], 0.0)
            l_ref[i] = jnp.where(lane < nodes, pltpu.roll(t[32 * f + 64 : 32 * f + 80], 1, 1), 0.0)

    def level(step, carry):
        s = jnp.left_shift(1, step)
        diag, (low, up) = eliminate(
            [d_ref[i] for i in range(count)], [[l_ref[i] for i in range(count)], [u_ref[i] for i in range(count)]]
        )
        for k in range(count):
            low_r = jnp.where(sub == 6, diag[k], low[k])
            up_r = jnp.where(sub == 6, diag[k], up[k])
            near[0, k] = pltpu.roll(up_r, s, 1)
            near[1, k] = pltpu.roll(low[k], s, 1)
            near[2, k] = pltpu.roll(low_r, 128 - s, 1)
            near[3, k] = pltpu.roll(up[k], 128 - s, 1)
        for i in range(count):
            d_new = d_ref[i]
            l_old, u_old = l_ref[i], u_ref[i]
            l_new = jnp.zeros((16, 128), jnp.float32)
            u_new = jnp.zeros((16, 128), jnp.float32)
            for k in range(count):
                at = slice(REAL[k], REAL[k] + 1)
                fl, fu = down(l_old[at, :]), down(u_old[at, :])
                d_new = d_new - fl * near[0, k] - fu * near[2, k]
                l_new = l_new - fl * near[1, k]
                u_new = u_new - fu * near[3, k]
            d_ref[i] = d_new
            l_ref[i] = l_new
            u_ref[i] = u_new
        return carry

    levels = max(1, (nodes - 1).bit_length())
    lax.fori_loop(0, levels, level, 0)
    diag, _ = eliminate([d_ref[i] for i in range(count)], [])
    x = jnp.zeros((16, 128), jnp.float32)
    for i in range(count):
        x = jnp.where(sub == REAL[i], down(diag[i][6:7, :]), x)
    own = jnp.sum(jnp.where(lane == me, x, 0.0), axis=1, keepdims=True)
    after = jnp.sum(jnp.where((lane == me + 1) & (lane < nodes), x, 0.0), axis=1, keepdims=True)
    spread = jnp.where((sub & 7) == lane, jnp.broadcast_to(own, (16, 128)), 0.0)
    for f in range(2):
        pose_ref[f : f + 1, :] = jnp.sum(spread[8 * f : 8 * f + 8], axis=0, keepdims=True)[:, :6]
    column = jnp.concatenate([own, after], axis=0)
    column = jnp.where(lax.broadcasted_iota(jnp.int32, (32, 1), 0) == 6, -1.0, column)
    for f in range(2):
        at = slice(f * pix, (f + 1) * pix)
        depth_ref[f : f + 1, :] = -jnp.sum(h_ref[:32, at] * column, axis=0, keepdims=True) / h_ref[32:33, at]


def solve_call(me, gathered, h):
    nodes = gathered.shape[0]
    pix = h.shape[1] // 2
    vmem = pl.BlockSpec(memory_space=pltpu.VMEM)
    return pl.pallas_call(
        functools.partial(solve_body, nodes, pix),
        out_shape=(
            jax.ShapeDtypeStruct((2, 6), jnp.float32),
            jax.ShapeDtypeStruct((2, pix), jnp.float32),
        ),
        in_specs=[pl.BlockSpec(memory_space=pltpu.SMEM), vmem, vmem],
        out_specs=(vmem, vmem),
        scratch_shapes=[
            pltpu.VMEM((nodes, 8, 128), jnp.float32),
            pltpu.VMEM((12, 16, 128), jnp.float32),
            pltpu.VMEM((12, 16, 128), jnp.float32),
            pltpu.VMEM((12, 16, 128), jnp.float32),
            pltpu.VMEM((4, 12, 16, 128), jnp.float32),
        ],
        compiler_params=pltpu.CompilerParams(vmem_limit_bytes=12 << 20),
        name="pose_solve",
    )(me, gathered, h)


NT = (((1,), (1,)), ((), ()))
TILE = 256
CHUNK = 768


def spots(info, slots, pix, halo):
    odd = (info.pix() & 1) == 1
    at1 = pl.multiple_of(jnp.where(odd, 0, halo + pix), halo)
    at3 = pl.multiple_of(jnp.where(odd, halo + pix, 0), halo)
    return at1, at3


def turned(value):
    return value.astype(jnp.float32).T.astype(jnp.bfloat16)


def load_keys(target, owns, nexts, k_ref, vt_ref):
    channels = k_ref.shape[1]

    @pl.when(target < 2)
    def _():
        base = 0
        for part in owns:
            k_ref[base : base + part.shape[1], :] = part[target]
            base += part.shape[1]

    @pl.when(target >= 2)
    def _():
        base = 0
        for part in nexts:
            k_ref[base : base + part.shape[1], :] = part[target - 2]
            base += part.shape[1]

    vt_ref[:channels, :] = turned(k_ref[...])
    vt_ref[channels:, :] = jnp.ones((vt_ref.shape[0] - channels, vt_ref.shape[1]), jnp.bfloat16)


def add_keys(slot, k_ref, vt_ref, qt_ref, old, factor, put):
    chunks = k_ref.shape[0] // CHUNK
    spots_t = [slice(t * TILE, (t + 1) * TILE) for t in range(qt_ref.shape[2] // TILE)]

    def scores(j):
        keys = k_ref[j * CHUNK : (j + 1) * CHUNK, :]
        return [jnp.dot(keys, qt_ref[slot, :, at], preferred_element_type=jnp.float32) for at in spots_t]

    held = scores(0)
    sums = [None if old is None else old[slot, :, at] for at in spots_t]
    for j in range(chunks):
        later = scores(j + 1) if j + 1 < chunks else None
        for t in range(len(spots_t)):
            p = jnp.exp2(held[t] * factor).astype(jnp.bfloat16)
            part = jnp.dot(vt_ref[:, j * CHUNK : (j + 1) * CHUNK], p, preferred_element_type=jnp.float32)
            sums[t] = part if sums[t] is None else sums[t] + part
        held = later
    for at, value in zip(spots_t, sums):
        put(at, value)


def load_queries(info, slots, slot, own_q, side1, side3, qt_ref):
    pix, halo = own_q.shape[1], qt_ref.shape[2] - own_q.shape[1]
    halo = halo // 2
    at1, at3 = spots(info, slots, pix, halo)
    odd = (info.pix() & 1) == 1
    from1 = pl.multiple_of(jnp.where(odd, pix - halo, 0), halo)
    from3 = pl.multiple_of(jnp.where(odd, 0, pix - halo), halo)
    src = info.source(slot) - 2 * info.node()
    qt_ref[slot, :, halo : halo + pix] = turned(own_q[src])
    qt_ref[slot, :, pl.ds(at1, halo)] = turned(side1[src, pl.ds(from1, halo), :])
    qt_ref[slot, :, pl.ds(at3, halo)] = turned(side3[src, pl.ds(from3, halo), :])


def match_factor(channels):
    return 2.0 / math.sqrt(channels) * math.log2(math.e)


def first_body(slots, edges, counts, ranks, own_q, side1, side3, own, after, acc_ref, qt_ref, k_ref, vt_ref):
    info = Facts(edges, counts, ranks)

    def one(slot, carry):
        target = info.target(slot) - 2 * info.node()
        load_queries(info, slots, slot, own_q, side1, side3, qt_ref)
        load_keys(target, (own,), (after,), k_ref, vt_ref)


        def put(at, value):
            acc_ref[slot, :, at] = value

        add_keys(slot, k_ref, vt_ref, qt_ref, None, match_factor(k_ref.shape[1]), put)
        return carry

    lax.fori_loop(0, info.live(), one, 0)


def second_body(slots, parts, edges, counts, ranks, qt_ref, old, *refs):
    info = Facts(edges, counts, ranks)
    owns, nexts = refs[:parts], refs[parts : 2 * parts]
    acc_ref, k_ref, vt_ref = refs[2 * parts :]

    def one(slot, carry):
        target = info.target(slot) - 2 * info.node()
        load_keys(target, owns, nexts, k_ref, vt_ref)


        def put(at, value):
            acc_ref[slot, :, at] = value

        add_keys(slot, k_ref, vt_ref, qt_ref, old, match_factor(k_ref.shape[1]), put)
        return carry

    lax.fori_loop(0, info.live(), one, 0)


def fused_body(dims, edges, counts, ranks, *refs):
    info = Facts(edges, counts, ranks)
    slots, total_rows, rows, cols, last, parts = dims
    (qt_ref, old), refs = refs[:2], refs[2:]
    (state, hide_up, hide_down), refs = refs[:3], refs[3:]
    owns, refs = refs[:parts], refs[parts:]
    nexts, refs = refs[:parts], refs[parts:]
    (wg, wc, wh, poses, rho_ref), refs = refs[:5], refs[5:]
    (fresh_out, block_ref, pull_out), refs = refs[:3], refs[3:]
    fresh_ref, pull_ref, k_ref, vt_ref, acc_ref, kall_ref, vtall_ref, x_ref, h_ref = refs[:9]
    head_ref, a_ref, w_ref, wc01, sems = refs[9:]
    pix_rank = info.pix()
    pix = rows * cols
    halo = 2 * cols
    ext = pix + 2 * halo
    channels = state.shape[-1]
    factor = match_factor(channels)
    px = lax.broadcasted_iota(jnp.int32, (ext, 1), 0)

    def inside(px):
        grow = (px >> (cols.bit_length() - 1)) - 2 + rows * pix_rank
        return jnp.where((grow >= 0) & (grow < total_rows), 1.0, 0.0)

    valid = inside(px)
    wc01[:, :channels] = wc[0]
    wc01[:, channels:] = wc[1]

    def send(slot):
        return pltpu.make_async_copy(fresh_ref.at[slot], fresh_out.at[slot], sems.at[slot])

    def keep(slot, carry):
        fresh_ref[slot] = state[slot]
        head_ref[pl.ds(pl.multiple_of(8 * slot, 8), 8), :] = jnp.zeros((8, pix), jnp.float32)
        send(slot).start()
        return carry

    lax.fori_loop(info.live(), slots, keep, 0)

    def one(slot, carry):
        target = info.target(slot) - 2 * info.node()
        load_keys(target, owns[parts - last :], nexts[parts - last :], k_ref, vt_ref)

        def put(at, value):
            acc_ref[0, :, at] = value

        add_keys(slot, k_ref, vt_ref, qt_ref, old, factor, put)
        sums = acc_ref[0, channels : channels + 1, :]
        fits = (jnp.min(sums) > 1e-20) & (jnp.max(sums) < 1e25)

        @pl.when(jnp.logical_not(fits))
        def _():
            load_keys(target, owns, nexts, kall_ref, vtall_ref)
            chunks = kall_ref.shape[0] // CHUNK

            def exact(t, carry):
                at = pl.ds(pl.multiple_of(t * TILE, TILE), TILE)
                q = qt_ref[slot, :, at]

                def scores(j):
                    span = pl.ds(pl.multiple_of(j * CHUNK, CHUNK), CHUNK)
                    return jnp.dot(kall_ref[span, :], q, preferred_element_type=jnp.float32)

                top = lax.fori_loop(
                    0,
                    chunks,
                    lambda j, top: jnp.maximum(top, jnp.max(scores(j), axis=0, keepdims=True)),
                    jnp.full((1, TILE), -3e38, jnp.float32),
                )

                def add(j, acc):
                    span = pl.ds(pl.multiple_of(j * CHUNK, CHUNK), CHUNK)
                    p = jnp.exp2((scores(j) - top) * factor).astype(jnp.bfloat16)
                    return acc + jnp.dot(vtall_ref[:, span], p, preferred_element_type=jnp.float32)

                acc_ref[0, :, at] = lax.fori_loop(
                    0, chunks, add, jnp.zeros((acc_ref.shape[1], TILE), jnp.float32)
                )
                return carry

            lax.fori_loop(0, ext // TILE, exact, 0)

        h_ref[halo : halo + pix, :] = state[slot]
        h_ref[:halo, :] = hide_up[slot]
        h_ref[halo + pix :, :] = hide_down[slot]
        col = px & (cols - 1)
        first, final = col == 0, col == cols - 1

        def spread(value, at, lane):
            size = value.shape[0]
            span = slice(lane, lane + channels)
            x_ref[at, span] = jnp.where(first[at], 0.0, pltpu.roll(value, 1, 0)).astype(jnp.bfloat16)
            span = slice(lane + 2 * channels, lane + 3 * channels)
            x_ref[at, span] = value.astype(jnp.bfloat16)
            span = slice(lane + 4 * channels, lane + 5 * channels)
            x_ref[at, span] = jnp.where(final[at], 0.0, pltpu.roll(value, size - 1, 0)).astype(jnp.bfloat16)

        wide = h_ref[...].astype(jnp.float32) * valid
        spread(wide, slice(0, ext), 0)
        weight = inside(lax.broadcasted_iota(jnp.int32, (1, ext), 1)) / acc_ref[0, channels : channels + 1, :]
        spread((acc_ref[0, :channels, :] * weight).T, slice(0, ext), channels)
        mid = ext - 2 * cols
        gates = None
        for r in range(3):
            part = jnp.dot(x_ref[r * cols : r * cols + mid, :], wg[r], preferred_element_type=jnp.float32)
            gates = part if r == 0 else gates + part
        inner = slice(cols, cols + mid)
        spread(jax.nn.sigmoid(gates[:, channels:]) * wide[inner], inner, 0)
        pair = jnp.dot(x_ref[cols : 2 * cols + pix, :], wc01[...], preferred_element_type=jnp.float32)
        cand = jnp.dot(x_ref[3 * cols : 3 * cols + pix, :], wc[2], preferred_element_type=jnp.float32)
        cand = cand + pair[:pix, :channels] + pair[cols : cols + pix, channels:]
        update = jax.nn.sigmoid(gates[cols : cols + pix, :channels])
        kept = wide[halo : halo + pix]
        fresh = ((1.0 - update) * kept + update * jnp.tanh(cand)).astype(jnp.bfloat16)
        fresh_ref[slot] = fresh
        head = lax.dot_general(wh[...], fresh, NT, preferred_element_type=jnp.float32)
        head_ref[pl.ds(pl.multiple_of(8 * slot, 8), 4), :] = head
        send(slot).start()
        return carry

    lax.fori_loop(0, info.live(), one, 0)
    bundle_body(
        slots, total_rows, cols, info, poses, rho_ref, head_ref, block_ref, pull_ref, pull_out, a_ref, w_ref, sems.at[slots]
    )
    for slot in range(slots):
        send(slot).wait()


VMEM = pl.BlockSpec(memory_space=pltpu.VMEM)
SMEM = pl.BlockSpec(memory_space=pltpu.SMEM)


def work(slots, ext, keys, channels):
    return pl.CostEstimate(
        flops=4 * slots * ext * keys * 2 * channels,
        bytes_accessed=slots * ext * (channels + 8) * 8,
        transcendentals=slots * ext * keys,
    )


def first_call(facts, slots, cols, queries, own, after):
    pix, channels = own.shape[1:]
    ext = pix + 4 * cols
    return pl.pallas_call(
        functools.partial(first_body, slots),
        in_specs=[SMEM] * 3 + [VMEM] * 5,
        out_specs=(VMEM, VMEM),
        scratch_shapes=[pltpu.VMEM((pix, channels), jnp.bfloat16), pltpu.VMEM((channels + 8, pix), jnp.bfloat16)],
        out_shape=(
            jax.ShapeDtypeStruct((slots, channels + 8, ext), jnp.float32),
            jax.ShapeDtypeStruct((slots, channels, ext), jnp.bfloat16),
        ),
        cost_estimate=work(slots, ext, pix, channels),
        compiler_params=pltpu.CompilerParams(vmem_limit_bytes=14 << 20),
        name="match_first",
    )(*facts, *queries, own, after)


def second_call(facts, qt, old, owns, nexts):
    slots, channels, ext = qt.shape
    keys = sum(part.shape[1] for part in owns)
    return pl.pallas_call(
        functools.partial(second_body, slots, len(owns)),
        in_specs=[SMEM] * 3 + [VMEM] * (2 + 2 * len(owns)),
        out_specs=VMEM,
        scratch_shapes=[pltpu.VMEM((keys, channels), jnp.bfloat16), pltpu.VMEM((channels + 8, keys), jnp.bfloat16)],
        out_shape=jax.ShapeDtypeStruct(old.shape, jnp.float32),
        cost_estimate=work(slots, ext, keys, channels),
        compiler_params=pltpu.CompilerParams(vmem_limit_bytes=14 << 20),
        name="match_second",
    )(*facts, qt, old, *owns, *nexts)


def fused_call(facts, qt, old, state, hide_up, hide_down, owns, nexts, last, weights, poses, inv_depth, total_rows, cols):
    slots, pix, channels = state.shape
    ext = qt.shape[2]
    keys = sum(part.shape[1] for part in owns)
    part_keys = sum(part.shape[1] for part in owns[len(owns) - last :])
    dims = (slots, total_rows, pix // cols, cols, last, len(owns))
    wide = channels + 8
    return pl.pallas_call(
        functools.partial(fused_body, dims),
        in_specs=[SMEM] * 3 + [VMEM] * (5 + 2 * len(owns) + len(weights) + 2),
        out_specs=(pl.BlockSpec(memory_space=pltpu.HBM), VMEM, pl.BlockSpec(memory_space=pltpu.HBM)),
        scratch_shapes=[
            pltpu.VMEM((slots, pix, channels), jnp.bfloat16),
            pltpu.VMEM((40, 2 * pix), jnp.float32),
            pltpu.VMEM((part_keys, channels), jnp.bfloat16),
            pltpu.VMEM((wide, part_keys), jnp.bfloat16),
            pltpu.VMEM((1, wide, ext), jnp.float32),
            pltpu.VMEM((keys, channels), jnp.bfloat16),
            pltpu.VMEM((wide, keys), jnp.bfloat16),
            pltpu.VMEM((ext, 6 * channels), jnp.bfloat16),
            pltpu.VMEM((ext, channels), jnp.bfloat16),
            pltpu.VMEM((8 * slots, pix), jnp.float32),
            pltpu.VMEM((8 * slots, 2 * pix), jnp.float32),
            pltpu.VMEM((8 * slots, 2 * pix), jnp.float32),
            pltpu.VMEM((weights[1].shape[1], 2 * channels), jnp.bfloat16),
            pltpu.SemaphoreType.DMA((slots + 1,)),
        ],
        out_shape=(
            jax.ShapeDtypeStruct((slots, pix, channels), jnp.bfloat16),
            jax.ShapeDtypeStruct((8, 128), jnp.float32),
            jax.ShapeDtypeStruct((40, 2 * pix), jnp.float32),
        ),
        compiler_params=pltpu.CompilerParams(vmem_limit_bytes=26 << 20),
        name="match_update",
    )(*facts, qt, old, state, hide_up, hide_down, *owns, *nexts, *weights, poses, inv_depth)


def shards(features, poses, inv_depth, hidden, edges, counts, w_gates, w_cand, w_head):
    slot_count, row_count, col_count, hid_width = hidden.shape
    channels = features.shape[3]
    node_rank = lax.axis_index(EDGE)
    pix_rank = lax.axis_index("x")
    total_rows = row_count * lax.axis_size("x")
    pix = row_count * col_count
    nodes = lax.axis_size(EDGE)
    halo = 2 * col_count
    facts = (edges.T, counts, jnp.stack([node_rank, pix_rank]).astype(jnp.int32))

    def following(value):
        return lax.ppermute(value, EDGE, [(i + 1, i) for i in range(nodes - 1)])

    own = features.reshape(2, pix, channels)
    state = hidden.reshape(slot_count, pix, hid_width)
    own1, own3 = swapped(own, "x", 1), swapped(own, "x", 3)
    next0 = following(own)
    next1, next3 = following(own1), following(own3)
    half = pix // 2
    own2a, own2b = swapped(own1[:, :half], "x", 3), swapped(own3[:, half:], "x", 1)
    next2a, next2b = following(own2a), following(own2b)
    acc, turned_q = first_call(facts, slot_count, col_count, (own, own1, own3), own, next0)
    rows_x = lax.axis_size("x")
    hide_up = lax.ppermute(state[:, pix - halo :], "x", [(i, i + 1) for i in range(rows_x - 1)])
    hide_down = lax.ppermute(state[:, :halo], "x", [(i + 1, i) for i in range(rows_x - 1)])
    acc = second_call(facts, turned_q, acc, (own1, own3), (next1, next3))
    wg = w_gates.reshape(3, -1, w_gates.shape[2])
    wc = w_cand.reshape(3, -1, w_cand.shape[2])
    fresh, block, pull = fused_call(
        facts,
        turned_q,
        acc,
        state,
        hide_up,
        hide_down,
        (own, own1, own3, own2a, own2b),
        (next0, next1, next3, next2a, next2b),
        2,
        (wg, wc, w_head),
        poses.T,
        inv_depth,
        total_rows,
        col_count,
    )
    gathered = gathered_blocks(block)
    pose_update, depth_update = solve_call(facts[2], gathered, pull)
    return (fresh.reshape(hidden.shape), pose_update, depth_update)


def solution(mesh):
    nodes, pix = mesh.devices.shape
    fine = Mesh(mesh.devices.reshape(nodes // 16, 8, 2, pix), EDGE + ("x",))
    placed = (
        P(EDGE, "x", None, None),
        P(),
        P(EDGE, "x"),
        P(EDGE, "x", None, None),
        P(EDGE, None),
        P(EDGE),
        P(),
        P(),
        P(),
    )
    return jax.shard_map(
        shards,
        mesh=fine,
        in_specs=placed,
        out_specs=(P(EDGE, "x", None, None), P(EDGE, None), P(EDGE, "x")),
        check_vma=False,
    )
```

```python
import functools
import math

import jax
import jax.numpy as jnp
from jax import lax
from jax.experimental import pallas as pl
from jax.experimental.pallas import tpu as pltpu
from jax.sharding import Mesh
from jax.sharding import PartitionSpec as P

PRECISE = lax.Precision.HIGHEST
POSE_DAMPING = 0.1
DEPTH_DAMPING = 0.1

EDGE = ("y", "z", "core")


def swapped(value, axis, step):
    count = lax.axis_size(axis)
    return lax.ppermute(value, axis, [(i, i ^ step) for i in range(count)])


def gathered_blocks(block):
    pair = block + swapped(block, "x", 1)
    block = pair + (swapped(block, "x", 2) + swapped(block, "x", 3))
    parts = jnp.stack([block, swapped(block, "core", 1)])
    parts = jnp.stack([parts] + [swapped(parts, "z", s) for s in (1, 2, 3)])
    parts = jnp.stack([parts, swapped(parts, "z", 4)])
    parts = [parts] + [swapped(parts, "y", s) for s in (1, 2, 3)]
    return [part.reshape((-1,) + block.shape) for part in parts]


class Facts:
    def __init__(self, edges, counts, ranks):
        self.edges, self.counts, self.ranks = edges, counts, ranks

    def source(self, slot):
        return self.edges[0, slot]

    def target(self, slot):
        return self.edges[1, slot]

    def live(self):
        return self.counts[0]

    def node(self):
        return self.ranks[0]

    def pix(self):
        return self.ranks[1]


def bundle_body(slots, rows_all, cols, info, poses, rho_ref, head, out, h_ref, h_out, a_ref, w_ref, sem):
    pix = rho_ref.shape[1]
    rows = pix // cols
    shift = cols.bit_length() - 1
    base = 2 * info.node()
    live = info.live()
    lane = lax.broadcasted_iota(jnp.int32, (1, pix), 1)
    col = (lane & (cols - 1)).astype(jnp.float32)
    row = ((lane >> shift) + info.pix() * rows).astype(jnp.float32)
    half = cols / 2.0
    u = (col - (cols - 1) / 2.0) / half
    v = (row - (rows_all - 1) / 2.0) / half
    sub = lax.broadcasted_iota(jnp.int32, (8, pix), 0)
    zero = jnp.zeros((8, pix), jnp.float32)
    lead_h = jnp.where(sub == 0, 1.0, jnp.where(sub == 2, -u, zero))
    rest_h = jnp.where(sub == 3, -u * v, jnp.where(sub == 4, 1.0 + u * u, jnp.where(sub == 5, -v, zero)))
    lead_v = jnp.where(sub == 1, 1.0, jnp.where(sub == 2, -v, zero))
    rest_v = jnp.where(sub == 3, -(1.0 + v * v), jnp.where(sub == 4, u * v, jnp.where(sub == 5, u, zero)))
    sub1 = lax.broadcasted_iota(jnp.int32, (8, 1), 0)
    frame = lax.broadcasted_iota(jnp.int32, (1, poses.shape[1]), 1)
    picks, sels = [], []
    for s in range(slots):
        src, tgt = info.source(s), info.target(s)
        a_loc, b_loc = src - base, tgt - base
        alive = jnp.where(s < live, 1.0, 0.0)
        picks.append([jnp.where(a_loc == f, 1.0, 0.0) for f in range(2)])
        sels.append([jnp.where(b_loc == g, 1.0, 0.0) - jnp.where(a_loc == g, 1.0, 0.0) for g in range(4)])
        pick_d = jnp.where(frame == tgt, 1.0, 0.0) - jnp.where(frame == src, 1.0, 0.0)
        d = jnp.sum(poses[...] * pick_d, axis=1, keepdims=True)
        d = jnp.concatenate([d, jnp.zeros((2, 1), jnp.float32)], axis=0)
        rho = rho_ref[pl.ds(a_loc, 1), :]
        conf_h = jax.nn.sigmoid(head[8 * s + 2 : 8 * s + 3, :]) * alive
        conf_v = jax.nn.sigmoid(head[8 * s + 3 : 8 * s + 4, :]) * alive
        a_h = rho * lead_h + rest_h
        a_v = rho * lead_v + rest_v
        e_h = head[8 * s : 8 * s + 1, :] - jnp.sum(a_h * d, axis=0, keepdims=True)
        e_v = head[8 * s + 1 : 8 * s + 2, :] - jnp.sum(a_v * d, axis=0, keepdims=True)
        k_h = jnp.sum(lead_h * d, axis=0, keepdims=True)
        k_v = jnp.sum(lead_v * d, axis=0, keepdims=True)
        a_h = jnp.where(sub == 6, e_h, a_h)
        a_v = jnp.where(sub == 6, e_v, a_v)
        w_h = conf_h * a_h
        w_v = conf_v * a_v
        at = slice(8 * s, 8 * s + 8)
        a_ref[at, :pix] = a_h
        a_ref[at, pix:] = a_v
        w_ref[at, :pix] = w_h
        w_ref[at, pix:] = w_v
        k_s = w_h * k_h + w_v * k_v
        dd = conf_h * k_h * k_h + conf_v * k_v * k_v
        for f in range(2):
            pick = picks[s][f]
            at = slice(f * pix, (f + 1) * pix)
            old = h_ref[32:33, at] if s else jnp.full((1, pix), DEPTH_DAMPING, jnp.float32)
            h_ref[32:33, at] = old + pick * dd
            for g in range(4):
                term = jnp.where(sub1 == 6, pick, pick * sels[s][g]) * k_s
                at = (slice(8 * g, 8 * g + 8), slice(f * pix, (f + 1) * pix))
                h_ref[at] = h_ref[at] + term if s else term
    copy = pltpu.make_async_copy(h_ref, h_out, sem)
    copy.start()
    nt = (((1,), (1,)), ((), ()))
    gram = lax.dot_general(w_ref[...], a_ref[...], nt, precision=PRECISE, preferred_element_type=jnp.float32)
    for f in range(2):
        at = slice(f * pix, (f + 1) * pix)
        w_ref[:, at] = h_ref[:32, at] * (1.0 / h_ref[32:33, at])
    schur = lax.dot_general(w_ref[...], h_ref[:32, :], nt, precision=PRECISE, preferred_element_type=jnp.float32)
    pad = jnp.zeros((32, 96), jnp.float32)
    gram = jnp.concatenate([gram, pad], axis=1)
    schur = jnp.concatenate([schur, pad], axis=1)
    lanes = lax.broadcasted_iota(jnp.int32, (8, 128), 1)
    group, inner = lanes >> 3, lanes & 7
    terms = []
    for s in range(slots):
        y = jnp.where(group == s, gram[8 * s : 8 * s + 8, :], 0.0)
        y = pltpu.roll(y, 128 - 8 * s, 1) if s else y
        y = y + pltpu.roll(y, 8, 1)
        y = y + pltpu.roll(y, 16, 1)
        coef = jnp.zeros((8, 128), jnp.float32)
        for g in range(4):
            coef = jnp.where(group == g, sels[s][g], coef)
        terms.append(y * jnp.where(inner == 6, 1.0, coef))
    total = None
    for g in range(4):
        part = -schur[8 * g : 8 * g + 8, :]
        for s in range(slots):
            part = part + sels[s][g] * terms[s]
        part = jnp.where(lanes < 32, part, 0.0)
        total = part if g == 0 else total + pltpu.roll(part, 32 * g, 1)
    out[...] = total
    copy.wait()


REAL = (0, 1, 2, 3, 4, 5, 8, 9, 10, 11, 12, 13)


def down(x, width=16):
    return jnp.broadcast_to(x, (width, 128))


def eliminate(diag, sides):
    diag, sides = list(diag), [list(side) for side in sides]
    count = len(REAL)
    for k in range(count):
        at = slice(REAL[k], REAL[k] + 1)
        scale = down(1.0 / diag[k][at, :])
        diag[k] = diag[k] * scale
        for side in sides:
            side[k] = side[k] * scale
        for i in range(count):
            if i != k:
                f = down(diag[i][at, :])
                diag[i] = diag[i] - f * diag[k]
                for side in sides:
                    side[i] = side[i] - f * side[k]
    return diag, sides


def solve_body(nodes, pix, groups, info, *refs):
    g_refs, refs = refs[:groups], refs[groups:]
    h_ref, pose_ref, depth_ref, t_ref, d_ref, l_ref, u_ref, near = refs
    per = nodes // groups
    count = len(REAL)
    lane = lax.broadcasted_iota(jnp.int32, (16, 128), 1)
    sub = lax.broadcasted_iota(jnp.int32, (16, 128), 0)
    me = info[0]
    for n in range(nodes):
        t_ref[n ^ me] = g_refs[n // per][n % per]
    rest = jnp.zeros((128 - nodes, 128), jnp.float32)
    for k in range(6):
        t = jnp.concatenate([t_ref[:, k, :], rest], axis=0).T
        for f in range(2):
            i = 6 * f + k
            far = jnp.where(lane < nodes, pltpu.roll(t[32 * f + 80 : 32 * f + 96], 1, 1), 0.0)
            d_ref[i] = t[32 * f : 32 * f + 16] + far + jnp.where(sub == REAL[i], POSE_DAMPING, 0.0)
            u_ref[i] = jnp.where(lane < nodes - 1, t[32 * f + 16 : 32 * f + 32], 0.0)
            l_ref[i] = jnp.where(lane < nodes, pltpu.roll(t[32 * f + 64 : 32 * f + 80], 1, 1), 0.0)

    def level(step, carry):
        s = jnp.left_shift(1, step)
        diag, (low, up) = eliminate(
            [d_ref[i] for i in range(count)], [[l_ref[i] for i in range(count)], [u_ref[i] for i in range(count)]]
        )
        for k in range(count):
            low_r = jnp.where(sub == 6, diag[k], low[k])
            up_r = jnp.where(sub == 6, diag[k], up[k])
            near[0, k] = pltpu.roll(up_r, s, 1)
            near[1, k] = pltpu.roll(low[k], s, 1)
            near[2, k] = pltpu.roll(low_r, 128 - s, 1)
            near[3, k] = pltpu.roll(up[k], 128 - s, 1)
        for i in range(count):
            d_new = d_ref[i]
            l_old, u_old = l_ref[i], u_ref[i]
            l_new = jnp.zeros((16, 128), jnp.float32)
            u_new = jnp.zeros((16, 128), jnp.float32)
            for k in range(count):
                at = slice(REAL[k], REAL[k] + 1)
                fl, fu = down(l_old[at, :]), down(u_old[at, :])
                d_new = d_new - fl * near[0, k] - fu * near[2, k]
                l_new = l_new - fl * near[1, k]
                u_new = u_new - fu * near[3, k]
            d_ref[i] = d_new
            l_ref[i] = l_new
            u_ref[i] = u_new
        return carry

    levels = max(1, (nodes - 1).bit_length())
    lax.fori_loop(0, levels, level, 0)
    diag, _ = eliminate([d_ref[i] for i in range(count)], [])
    x = jnp.zeros((16, 128), jnp.float32)
    for i in range(count):
        x = jnp.where(sub == REAL[i], down(diag[i][6:7, :]), x)
    own = jnp.sum(jnp.where(lane == me, x, 0.0), axis=1, keepdims=True)
    after = jnp.sum(jnp.where((lane == me + 1) & (lane < nodes), x, 0.0), axis=1, keepdims=True)
    spread = jnp.where((sub & 7) == lane, jnp.broadcast_to(own, (16, 128)), 0.0)
    for f in range(2):
        pose_ref[f : f + 1, :] = jnp.sum(spread[8 * f : 8 * f + 8], axis=0, keepdims=True)[:, :6]
    column = jnp.concatenate([own, after], axis=0)
    column = jnp.where(lax.broadcasted_iota(jnp.int32, (32, 1), 0) == 6, -1.0, column)
    for f in range(2):
        at = slice(f * pix, (f + 1) * pix)
        depth_ref[f : f + 1, :] = -jnp.sum(h_ref[:32, at] * column, axis=0, keepdims=True) / h_ref[32:33, at]


def solve_call(me, gathered, h):
    nodes = sum(part.shape[0] for part in gathered)
    pix = h.shape[1] // 2
    vmem = pl.BlockSpec(memory_space=pltpu.VMEM)
    return pl.pallas_call(
        functools.partial(solve_body, nodes, pix, len(gathered)),
        out_shape=(
            jax.ShapeDtypeStruct((2, 6), jnp.float32),
            jax.ShapeDtypeStruct((2, pix), jnp.float32),
        ),
        in_specs=[pl.BlockSpec(memory_space=pltpu.SMEM)] + [vmem] * (len(gathered) + 1),
        out_specs=(vmem, vmem),
        scratch_shapes=[
            pltpu.VMEM((nodes, 8, 128), jnp.float32),
            pltpu.VMEM((12, 16, 128), jnp.float32),
            pltpu.VMEM((12, 16, 128), jnp.float32),
            pltpu.VMEM((12, 16, 128), jnp.float32),
            pltpu.VMEM((4, 12, 16, 128), jnp.float32),
        ],
        compiler_params=pltpu.CompilerParams(vmem_limit_bytes=12 << 20),
        name="pose_solve",
    )(me, *gathered, h)


NT = (((1,), (1,)), ((), ()))
TILE = 256
CHUNK = 768


def spots(info, slots, pix, halo):
    odd = (info.pix() & 1) == 1
    at1 = pl.multiple_of(jnp.where(odd, 0, halo + pix), halo)
    at3 = pl.multiple_of(jnp.where(odd, halo + pix, 0), halo)
    return at1, at3


def turned(value):
    return value.astype(jnp.float32).T.astype(jnp.bfloat16)


def load_keys(target, owns, nexts, k_ref, vt_ref):
    channels = k_ref.shape[1]

    @pl.when(target < 2)
    def _():
        base = 0
        for part in owns:
            k_ref[base : base + part.shape[1], :] = part[target]
            base += part.shape[1]

    @pl.when(target >= 2)
    def _():
        base = 0
        for part in nexts:
            k_ref[base : base + part.shape[1], :] = part[target - 2]
            base += part.shape[1]

    vt_ref[:channels, :] = turned(k_ref[...])
    vt_ref[channels:, :] = jnp.ones((vt_ref.shape[0] - channels, vt_ref.shape[1]), jnp.bfloat16)


def add_keys(slot, k_ref, vt_ref, qt_ref, old, factor, put):
    chunks = k_ref.shape[0] // CHUNK
    spots_t = [slice(t * TILE, (t + 1) * TILE) for t in range(qt_ref.shape[2] // TILE)]

    def scores(j):
        keys = k_ref[j * CHUNK : (j + 1) * CHUNK, :]
        return [jnp.dot(keys, qt_ref[slot, :, at], preferred_element_type=jnp.float32) for at in spots_t]

    held = scores(0)
    sums = [None if old is None else old[slot, :, at] for at in spots_t]
    for j in range(chunks):
        later = scores(j + 1) if j + 1 < chunks else None
        for t in range(len(spots_t)):
            p = jnp.exp2(held[t] * factor).astype(jnp.bfloat16)
            part = jnp.dot(vt_ref[:, j * CHUNK : (j + 1) * CHUNK], p, preferred_element_type=jnp.float32)
            sums[t] = part if sums[t] is None else sums[t] + part
        held = later
    for at, value in zip(spots_t, sums):
        put(at, value)


def load_queries(info, slots, slot, own_q, side1, side3, qt_ref):
    pix, halo = own_q.shape[1], qt_ref.shape[2] - own_q.shape[1]
    halo = halo // 2
    at1, at3 = spots(info, slots, pix, halo)
    odd = (info.pix() & 1) == 1
    from1 = pl.multiple_of(jnp.where(odd, pix - halo, 0), halo)
    from3 = pl.multiple_of(jnp.where(odd, 0, pix - halo), halo)
    src = info.source(slot) - 2 * info.node()
    qt_ref[slot, :, halo : halo + pix] = turned(own_q[src])
    qt_ref[slot, :, pl.ds(at1, halo)] = turned(side1[src, pl.ds(from1, halo), :])
    qt_ref[slot, :, pl.ds(at3, halo)] = turned(side3[src, pl.ds(from3, halo), :])


def match_factor(channels):
    return 2.0 / math.sqrt(channels) * math.log2(math.e)


def first_body(slots, edges, counts, ranks, own_q, side1, side3, own, after, acc_ref, qt_ref, k_ref, vt_ref):
    info = Facts(edges, counts, ranks)

    def one(slot, carry):
        target = info.target(slot) - 2 * info.node()
        load_queries(info, slots, slot, own_q, side1, side3, qt_ref)
        load_keys(target, (own,), (after,), k_ref, vt_ref)


        def put(at, value):
            acc_ref[slot, :, at] = value

        add_keys(slot, k_ref, vt_ref, qt_ref, None, match_factor(k_ref.shape[1]), put)
        return carry

    lax.fori_loop(0, info.live(), one, 0)


def second_body(slots, parts, edges, counts, ranks, qt_ref, old, *refs):
    info = Facts(edges, counts, ranks)
    owns, nexts = refs[:parts], refs[parts : 2 * parts]
    acc_ref, k_ref, vt_ref = refs[2 * parts :]

    def one(slot, carry):
        target = info.target(slot) - 2 * info.node()
        load_keys(target, owns, nexts, k_ref, vt_ref)


        def put(at, value):
            acc_ref[slot, :, at] = value

        add_keys(slot, k_ref, vt_ref, qt_ref, old, match_factor(k_ref.shape[1]), put)
        return carry

    lax.fori_loop(0, info.live(), one, 0)


def fused_body(dims, edges, counts, ranks, *refs):
    info = Facts(edges, counts, ranks)
    slots, total_rows, rows, cols, last, parts = dims
    (qt_ref, old), refs = refs[:2], refs[2:]
    (state, hide_up, hide_down), refs = refs[:3], refs[3:]
    owns, refs = refs[:parts], refs[parts:]
    nexts, refs = refs[:parts], refs[parts:]
    (wg, wc, wh, poses, rho_ref), refs = refs[:5], refs[5:]
    (fresh_out, block_ref, pull_out), refs = refs[:3], refs[3:]
    fresh_ref, pull_ref, k_ref, vt_ref, acc_ref, kall_ref, vtall_ref, x_ref, h_ref = refs[:9]
    head_ref, a_ref, w_ref, wc01, sems = refs[9:]
    pix_rank = info.pix()
    pix = rows * cols
    halo = 2 * cols
    ext = pix + 2 * halo
    channels = state.shape[-1]
    factor = match_factor(channels)
    px = lax.broadcasted_iota(jnp.int32, (ext, 1), 0)

    def inside(px):
        grow = (px >> (cols.bit_length() - 1)) - 2 + rows * pix_rank
        return jnp.where((grow >= 0) & (grow < total_rows), 1.0, 0.0)

    valid = inside(px)
    wc01[:, :channels] = wc[0]
    wc01[:, channels:] = wc[1]

    def send(slot):
        return pltpu.make_async_copy(fresh_ref.at[slot], fresh_out.at[slot], sems.at[slot])

    def keep(slot, carry):
        fresh_ref[slot] = state[slot]
        head_ref[pl.ds(pl.multiple_of(8 * slot, 8), 8), :] = jnp.zeros((8, pix), jnp.float32)
        send(slot).start()
        return carry

    lax.fori_loop(info.live(), slots, keep, 0)

    def one(slot, carry):
        target = info.target(slot) - 2 * info.node()
        load_keys(target, owns[parts - last :], nexts[parts - last :], k_ref, vt_ref)

        def put(at, value):
            acc_ref[0, :, at] = value

        add_keys(slot, k_ref, vt_ref, qt_ref, old, factor, put)
        sums = acc_ref[0, channels : channels + 1, :]
        fits = (jnp.min(sums) > 1e-20) & (jnp.max(sums) < 1e25)

        @pl.when(jnp.logical_not(fits))
        def _():
            load_keys(target, owns, nexts, kall_ref, vtall_ref)
            chunks = kall_ref.shape[0] // CHUNK

            def exact(t, carry):
                at = pl.ds(pl.multiple_of(t * TILE, TILE), TILE)
                q = qt_ref[slot, :, at]

                def scores(j):
                    span = pl.ds(pl.multiple_of(j * CHUNK, CHUNK), CHUNK)
                    return jnp.dot(kall_ref[span, :], q, preferred_element_type=jnp.float32)

                top = lax.fori_loop(
                    0,
                    chunks,
                    lambda j, top: jnp.maximum(top, jnp.max(scores(j), axis=0, keepdims=True)),
                    jnp.full((1, TILE), -3e38, jnp.float32),
                )

                def add(j, acc):
                    span = pl.ds(pl.multiple_of(j * CHUNK, CHUNK), CHUNK)
                    p = jnp.exp2((scores(j) - top) * factor).astype(jnp.bfloat16)
                    return acc + jnp.dot(vtall_ref[:, span], p, preferred_element_type=jnp.float32)

                acc_ref[0, :, at] = lax.fori_loop(
                    0, chunks, add, jnp.zeros((acc_ref.shape[1], TILE), jnp.float32)
                )
                return carry

            lax.fori_loop(0, ext // TILE, exact, 0)

        h_ref[halo : halo + pix, :] = state[slot]
        h_ref[:halo, :] = hide_up[slot]
        h_ref[halo + pix :, :] = hide_down[slot]
        col = px & (cols - 1)
        first, final = col == 0, col == cols - 1

        def spread(value, at, lane):
            size = value.shape[0]
            span = slice(lane, lane + channels)
            x_ref[at, span] = jnp.where(first[at], 0.0, pltpu.roll(value, 1, 0)).astype(jnp.bfloat16)
            span = slice(lane + 2 * channels, lane + 3 * channels)
            x_ref[at, span] = value.astype(jnp.bfloat16)
            span = slice(lane + 4 * channels, lane + 5 * channels)
            x_ref[at, span] = jnp.where(final[at], 0.0, pltpu.roll(value, size - 1, 0)).astype(jnp.bfloat16)

        wide = h_ref[...].astype(jnp.float32) * valid
        spread(wide, slice(0, ext), 0)
        weight = inside(lax.broadcasted_iota(jnp.int32, (1, ext), 1)) / acc_ref[0, channels : channels + 1, :]
        spread((acc_ref[0, :channels, :] * weight).T, slice(0, ext), channels)
        mid = ext - 2 * cols
        gates = None
        for r in range(3):
            part = jnp.dot(x_ref[r * cols : r * cols + mid, :], wg[r], preferred_element_type=jnp.float32)
            gates = part if r == 0 else gates + part
        inner = slice(cols, cols + mid)
        spread(jax.nn.sigmoid(gates[:, channels:]) * wide[inner], inner, 0)
        pair = jnp.dot(x_ref[cols : 2 * cols + pix, :], wc01[...], preferred_element_type=jnp.float32)
        cand = jnp.dot(x_ref[3 * cols : 3 * cols + pix, :], wc[2], preferred_element_type=jnp.float32)
        cand = cand + pair[:pix, :channels] + pair[cols : cols + pix, channels:]
        update = jax.nn.sigmoid(gates[cols : cols + pix, :channels])
        kept = wide[halo : halo + pix]
        fresh = ((1.0 - update) * kept + update * jnp.tanh(cand)).astype(jnp.bfloat16)
        fresh_ref[slot] = fresh
        head = lax.dot_general(wh[...], fresh, NT, preferred_element_type=jnp.float32)
        head_ref[pl.ds(pl.multiple_of(8 * slot, 8), 4), :] = head
        send(slot).start()
        return carry

    lax.fori_loop(0, info.live(), one, 0)
    bundle_body(
        slots, total_rows, cols, info, poses, rho_ref, head_ref, block_ref, pull_ref, pull_out, a_ref, w_ref, sems.at[slots]
    )
    for slot in range(slots):
        send(slot).wait()


VMEM = pl.BlockSpec(memory_space=pltpu.VMEM)
SMEM = pl.BlockSpec(memory_space=pltpu.SMEM)


def work(slots, ext, keys, channels):
    return pl.CostEstimate(
        flops=4 * slots * ext * keys * 2 * channels,
        bytes_accessed=slots * ext * (channels + 8) * 8,
        transcendentals=slots * ext * keys,
    )


def first_call(facts, slots, cols, queries, own, after):
    pix, channels = own.shape[1:]
    ext = pix + 4 * cols
    return pl.pallas_call(
        functools.partial(first_body, slots),
        in_specs=[SMEM] * 3 + [VMEM] * 5,
        out_specs=(VMEM, VMEM),
        scratch_shapes=[pltpu.VMEM((pix, channels), jnp.bfloat16), pltpu.VMEM((channels + 8, pix), jnp.bfloat16)],
        out_shape=(
            jax.ShapeDtypeStruct((slots, channels + 8, ext), jnp.float32),
            jax.ShapeDtypeStruct((slots, channels, ext), jnp.bfloat16),
        ),
        cost_estimate=work(slots, ext, pix, channels),
        compiler_params=pltpu.CompilerParams(vmem_limit_bytes=14 << 20),
        name="match_first",
    )(*facts, *queries, own, after)


def second_call(facts, qt, old, owns, nexts):
    slots, channels, ext = qt.shape
    keys = sum(part.shape[1] for part in owns)
    return pl.pallas_call(
        functools.partial(second_body, slots, len(owns)),
        in_specs=[SMEM] * 3 + [VMEM] * (2 + 2 * len(owns)),
        out_specs=VMEM,
        scratch_shapes=[pltpu.VMEM((keys, channels), jnp.bfloat16), pltpu.VMEM((channels + 8, keys), jnp.bfloat16)],
        out_shape=jax.ShapeDtypeStruct(old.shape, jnp.float32),
        cost_estimate=work(slots, ext, keys, channels),
        compiler_params=pltpu.CompilerParams(vmem_limit_bytes=14 << 20),
        name="match_second",
    )(*facts, qt, old, *owns, *nexts)


def fused_call(facts, qt, old, state, hide_up, hide_down, owns, nexts, last, weights, poses, inv_depth, total_rows, cols):
    slots, pix, channels = state.shape
    ext = qt.shape[2]
    keys = sum(part.shape[1] for part in owns)
    part_keys = sum(part.shape[1] for part in owns[len(owns) - last :])
    dims = (slots, total_rows, pix // cols, cols, last, len(owns))
    wide = channels + 8
    return pl.pallas_call(
        functools.partial(fused_body, dims),
        in_specs=[SMEM] * 3 + [VMEM] * (5 + 2 * len(owns) + len(weights) + 2),
        out_specs=(pl.BlockSpec(memory_space=pltpu.HBM), VMEM, pl.BlockSpec(memory_space=pltpu.HBM)),
        scratch_shapes=[
            pltpu.VMEM((slots, pix, channels), jnp.bfloat16),
            pltpu.VMEM((40, 2 * pix), jnp.float32),
            pltpu.VMEM((part_keys, channels), jnp.bfloat16),
            pltpu.VMEM((wide, part_keys), jnp.bfloat16),
            pltpu.VMEM((1, wide, ext), jnp.float32),
            pltpu.VMEM((keys, channels), jnp.bfloat16),
            pltpu.VMEM((wide, keys), jnp.bfloat16),
            pltpu.VMEM((ext, 6 * channels), jnp.bfloat16),
            pltpu.VMEM((ext, channels), jnp.bfloat16),
            pltpu.VMEM((8 * slots, pix), jnp.float32),
            pltpu.VMEM((8 * slots, 2 * pix), jnp.float32),
            pltpu.VMEM((8 * slots, 2 * pix), jnp.float32),
            pltpu.VMEM((weights[1].shape[1], 2 * channels), jnp.bfloat16),
            pltpu.SemaphoreType.DMA((slots + 1,)),
        ],
        out_shape=(
            jax.ShapeDtypeStruct((slots, pix, channels), jnp.bfloat16),
            jax.ShapeDtypeStruct((8, 128), jnp.float32),
            jax.ShapeDtypeStruct((40, 2 * pix), jnp.float32),
        ),
        compiler_params=pltpu.CompilerParams(vmem_limit_bytes=26 << 20),
        name="match_update",
    )(*facts, qt, old, state, hide_up, hide_down, *owns, *nexts, *weights, poses, inv_depth)


def shards(features, poses, inv_depth, hidden, edges, counts, w_gates, w_cand, w_head):
    slot_count, row_count, col_count, hid_width = hidden.shape
    channels = features.shape[3]
    node_rank = lax.axis_index(EDGE)
    pix_rank = lax.axis_index("x")
    total_rows = row_count * lax.axis_size("x")
    pix = row_count * col_count
    nodes = lax.axis_size(EDGE)
    halo = 2 * col_count
    facts = (edges.T, counts, jnp.stack([node_rank, pix_rank]).astype(jnp.int32))

    def following(value):
        return lax.ppermute(value, EDGE, [(i + 1, i) for i in range(nodes - 1)])

    own = features.reshape(2, pix, channels)
    state = hidden.reshape(slot_count, pix, hid_width)
    own1, own3 = swapped(own, "x", 1), swapped(own, "x", 3)
    next0 = following(own)
    next1, next3 = following(own1), following(own3)
    own2 = swapped(own1, "x", 3)
    next2 = following(own2)
    acc, turned_q = first_call(facts, slot_count, col_count, (own, own1, own3), own, next0)
    rows_x = lax.axis_size("x")
    hide_up = lax.ppermute(state[:, pix - halo :], "x", [(i, i + 1) for i in range(rows_x - 1)])
    hide_down = lax.ppermute(state[:, :halo], "x", [(i + 1, i) for i in range(rows_x - 1)])
    acc = second_call(facts, turned_q, acc, (own1, own3), (next1, next3))
    wg = w_gates.reshape(3, -1, w_gates.shape[2])
    wc = w_cand.reshape(3, -1, w_cand.shape[2])
    fresh, block, pull = fused_call(
        facts,
        turned_q,
        acc,
        state,
        hide_up,
        hide_down,
        (own, own1, own3, own2),
        (next0, next1, next3, next2),
        1,
        (wg, wc, w_head),
        poses.T,
        inv_depth,
        total_rows,
        col_count,
    )
    gathered = gathered_blocks(block)
    pose_update, depth_update = solve_call(facts[2], gathered, pull)
    return (fresh.reshape(hidden.shape), pose_update, depth_update)


def solution(mesh):
    nodes, pix = mesh.devices.shape
    fine = Mesh(mesh.devices.reshape(nodes // 16, 8, 2, pix), EDGE + ("x",))
    placed = (
        P(EDGE, "x", None, None),
        P(),
        P(EDGE, "x"),
        P(EDGE, "x", None, None),
        P(EDGE, None),
        P(EDGE),
        P(),
        P(),
        P(),
    )
    return jax.shard_map(
        shards,
        mesh=fine,
        in_specs=placed,
        out_specs=(P(EDGE, "x", None, None), P(EDGE, None), P(EDGE, "x")),
        check_vma=False,
    )
```
